256 devices in a mesh: ctx: 128 (over x, y, z), tp: 2 (over core).
Axes of the slice: x: 4, y: 4, z: 8, core: 2. Of those that a mesh axis runs over, the one named last changes fastest.
Arguments:
- x_raw: bfloat16 [16384, 2560], P('ctx', 'tp'), may hold values from -6 to 6
- bc_raw: bfloat16 [16384, 256], P('ctx'), may hold values from -6 to 6
- gate_branch: bfloat16 [16384, 2560], P('ctx', 'tp'), may hold values from -6 to 6
- dt_raw: float32 [16384, 40], P('ctx', 'tp'), may hold values from -2 to 4
- conv_x: float32 [4, 2560], P(None, 'tp'), may hold values from -3 to 3
- conv_x_bias: float32 [2560], P('tp'), may hold values from -0.75 to -0.15
- conv_bc: float32 [4, 256], replicated, may hold values from -3 to 3
- conv_bc_bias: float32 [256], replicated, may hold values from -0.75 to -0.15
- dt_bias: float32 [40], P('tp'), may hold values from -4.2 to -3.6
- a_log: float32 [40], P('tp'), may hold values from -10 to 2
- d_skip: float32 [40], P('tp'), may hold values from 0.5 to 2
- out_weight: bfloat16 [2560, 2560], P('tp'), may hold values from -0.125 to 0.125
- grad_out: bfloat16 [16384, 2560], P('ctx'), may hold values from -24 to 24
Outputs:
- grad_x_conv: bfloat16 [16384, 2560], P('ctx', 'tp')
- grad_bc_conv: bfloat16 [16384, 256], P('ctx')
- grad_z: bfloat16 [16384, 2560], P('ctx', 'tp')
- grad_dt_raw: float32 [16384, 40], P('ctx', 'tp')
- out_weight_grad: float32 [2560, 2560], P('ctx', 'tp')
The draws below stay inside these ranges and needn't reach their ends.
All inputs are finite; a program needn't handle non-finite values.
Results may differ from the reference program's by a relative error of at most 0.003.
Values may be sent and summed in bfloat16 or wider, within the bound.
A program may use at most 192 MiB of HBM per device.

```python
import jax
import jax.numpy as jnp
from jax import lax

D = 2560
SHARD_ATTENDERS = 40
P_SIZE = 64
N = 128
KERNEL = 4
TOK_DEV = 128
SEQUENCE_TOKENS = 16384
N_CTX = 128


def draw_a_log(key, part):
    pick_key, slow_key, middle_key, fast_key = jax.random.split(key, 4)
    slow_share = 0.5
    middle_share = 0.3
    chooser = jax.random.uniform(pick_key, (SHARD_ATTENDERS,), jnp.float32)
    slow_rate = jax.random.uniform(slow_key, (SHARD_ATTENDERS,), jnp.float32, 0.6, 0.9) / (SEQUENCE_TOKENS * 0.025)
    middle_rate = jax.random.uniform(middle_key, (SHARD_ATTENDERS,), jnp.float32, 0.45, 1.0) / (TOK_DEV * 0.03)
    fast_rate = jax.random.uniform(fast_key, (SHARD_ATTENDERS,), jnp.float32, 0.8, 2.5)
    picked = jnp.where(chooser < slow_share, slow_rate, jnp.where(chooser < slow_share + middle_share, middle_rate, fast_rate))
    return jnp.log(picked)


def draw_dt_raw(key, part):
    baseline_key, place_key, shift_random_key, lift_key = jax.random.split(key, 4)
    base_level = 0.5 * jax.random.truncated_normal(baseline_key, -4.0, 4.0, (SEQUENCE_TOKENS, SHARD_ATTENDERS), jnp.float32)
    span_width = SEQUENCE_TOKENS // 8
    window_positions = jax.random.permutation(place_key, 4)[:2]
    span_begin_index = window_positions * (2 * span_width) + jax.random.randint(shift_random_key, (2,), 0, span_width + 1)
    element_position = lax.broadcasted_iota(jnp.int32, (SEQUENCE_TOKENS, 1), 0)
    within_span_mask = jnp.any((element_position >= span_begin_index[None, :]) & (element_position < span_begin_index[None, :] + span_width), axis=1, keepdims=True)
    raise_offset = jax.random.uniform(lift_key, (SEQUENCE_TOKENS, SHARD_ATTENDERS), jnp.float32, 0.8, 1.6)
    return base_level + jnp.where(within_span_mask, raise_offset, 0.0)


def strengthened(values, rng, source, target, blocks, factor):
    def block_of(position):
        return (jnp.arange(values.shape[position]) // (values.shape[position] // blocks)).reshape((-1,) + (1,) * (values.ndim - 1 - position))

    first = jax.random.permutation(rng, blocks)[block_of(target)]
    far = (block_of(target) + blocks // 2) % blocks
    return jnp.where((block_of(source) == first) | (block_of(source) == far), factor * values, values)


def block_scale(stream_key, dims, shards, least, largest):
    gain = 1.0
    for position, blocks in shards:
        heights = jax.random.uniform(jax.random.fold_in(jax.random.fold_in(stream_key, 6), position), (blocks,), jnp.float32, least / len(shards), largest / len(shards))
        gain = gain * jnp.repeat(jnp.exp(heights), dims[position] // blocks).reshape((-1,) + (1,) * (len(dims) - 1 - position))
    return gain


def bell_draw(own_key, shape, width, limit, cuts=(), dtype=jnp.bfloat16):
    gain = block_scale(own_key, shape, cuts, -0.22, 0.18) if cuts else 1.0
    values = jax.random.normal(own_key, shape, jnp.float32) * width * gain
    return jnp.minimum(jnp.maximum(values, -limit), limit).astype(dtype)


def noise_with(stream_key, dims, scale, most, cuts, heavy, dtype=jnp.bfloat16):
    values = scale * jax.random.normal(stream_key, dims, jnp.float32)
    if cuts:
        values = values * block_scale(stream_key, dims, cuts, -0.22, 0.18)
    return jnp.clip(strengthened(values, jax.random.fold_in(stream_key, 3), *heavy), -most, most).astype(dtype)


def setup_inputs(seed: int = 0) -> dict:
    arg_keys = jax.random.split(jax.random.key(seed), 14)
    x_raw = bell_draw(arg_keys[0], (SEQUENCE_TOKENS, SHARD_ATTENDERS * P_SIZE), 1.0, 6.0, ((0, 128), (1, 2)))
    bc_raw = bell_draw(arg_keys[1], (SEQUENCE_TOKENS, 2 * N), 1.0, 6.0, ((0, 128),))
    gate_branch = bell_draw(arg_keys[2], (SEQUENCE_TOKENS, SHARD_ATTENDERS * P_SIZE), 1.0, 6.0, ((0, 128), (1, 2)))
    dt_raw = draw_dt_raw(jax.random.fold_in(arg_keys[13], 71), 0)
    conv_x = bell_draw(arg_keys[4], (KERNEL, SHARD_ATTENDERS * P_SIZE), KERNEL ** -0.5, 3.0, ((1, 2),), jnp.float32)
    conv_x_bias = jnp.clip(-0.75 + 0.6 * jax.random.uniform(arg_keys[5], (SHARD_ATTENDERS * P_SIZE,), jnp.float32) ** block_scale(arg_keys[5], (SHARD_ATTENDERS * P_SIZE,), ((0, 2),), -0.2, 0.2), -0.75, -0.15)
    conv_bc = bell_draw(arg_keys[6], (KERNEL, 2 * N), KERNEL ** -0.5, 3.0, (), jnp.float32)
    conv_bc_bias = jnp.clip(jax.random.uniform(arg_keys[7], (2 * N,), jnp.float32, -0.75, -0.15), -0.75, -0.15)
    dt_bias = jnp.clip(-4.2 + 0.5999999 * jax.random.uniform(arg_keys[8], (SHARD_ATTENDERS,), jnp.float32) ** block_scale(arg_keys[8], (SHARD_ATTENDERS,), ((0, 2),), -0.2, 0.2), -4.2, -3.6)
    a_log = draw_a_log(jax.random.fold_in(arg_keys[13], 71), 0)
    d_skip = jnp.clip(0.5 + 1.5 * jax.random.uniform(arg_keys[10], (SHARD_ATTENDERS,), jnp.float32) ** block_scale(arg_keys[10], (SHARD_ATTENDERS,), ((0, 2),), -0.2, 0.2), 0.5, 2.0)
    out_weight = bell_draw(arg_keys[11], (SHARD_ATTENDERS * P_SIZE, D), (SHARD_ATTENDERS * P_SIZE) ** -0.5, 0.125, ((0, 2),))
    grad_out = noise_with(arg_keys[12], (SEQUENCE_TOKENS, D), 1.0, 24.0, ((0, 128),), (0, 1, 128, 5.5))
    return {"x_raw": x_raw, "bc_raw": bc_raw, "gate_branch": gate_branch, "dt_raw": dt_raw, "conv_x": conv_x, "conv_x_bias": conv_x_bias, "conv_bc": conv_bc, "conv_bc_bias": conv_bc_bias, "dt_bias": dt_bias, "a_log": a_log, "d_skip": d_skip, "out_weight": out_weight, "grad_out": grad_out}


HIGH = lax.Precision.HIGHEST

def convolve(padded, kernel_weight, kernel_bias):
    length = padded.shape[0] - kernel_weight.shape[0] + 1
    result = jnp.broadcast_to(kernel_bias[None, :], (length, padded.shape[1]))
    for offset in range(kernel_weight.shape[0]):
        result = result + kernel_weight[offset][None, :] * padded[offset:offset + length]
    return result

def silu_slope(argument):
    gate_value = jax.nn.sigmoid(argument)
    return gate_value * (1.0 + argument * (1.0 - gate_value))

def decay_matrix(log_decay):
    length = log_decay.shape[0]
    row_index = lax.broadcasted_iota(jnp.int32, (length, length), 0)
    col_index = lax.broadcasted_iota(jnp.int32, (length, length), 1)
    causal = (row_index >= col_index)[None, :, :]
    per_head = log_decay.T
    spread = per_head[:, :, None] - per_head[:, None, :]
    return jnp.where(causal, jnp.exp(jnp.where(causal, spread, 0.0)), 0.0)

def local_state(inputs, b_rows, step_size, log_decay):
    last_decay = log_decay[-1]
    weight = jnp.exp(last_decay[None, :] - log_decay) * step_size
    scaled_in = weight[:, :, None] * inputs
    partial_state = jnp.einsum('shp,sn->hpn', scaled_in, b_rows, precision=HIGH)
    return (jnp.exp(last_decay), partial_state)

def local_grad(log_decay, grad_y, c_rows):
    scaled_grad = jnp.exp(log_decay)[:, :, None] * grad_y
    return jnp.einsum('thp,tn->hpn', scaled_grad, c_rows, precision=HIGH)

def block_forward(inputs, b_rows, c_rows, step_size, log_decay, state_in, skip_gain):
    decays = decay_matrix(log_decay)
    scores = jnp.dot(c_rows, b_rows.T, precision=HIGH)
    mixing = decays * scores[None, :, :] * step_size.T[:, None, :]
    within = jnp.einsum('hts,shp->thp', mixing, inputs, precision=HIGH)
    carried = jnp.einsum('hpn,tn->thp', state_in, c_rows, precision=HIGH)
    return within + jnp.exp(log_decay)[:, :, None] * carried + skip_gain[None, :, None] * inputs

def block_backward(inputs, b_rows, c_rows, step_size, log_decay, decay_rate, state_in, carry_in, grad_y, skip_gain):
    decays = decay_matrix(log_decay)
    scores = jnp.dot(c_rows, b_rows.T, precision=HIGH)
    products = jnp.einsum('thp,shp->hts', grad_y, inputs, precision=HIGH)
    weighted = decays * products
    direct = weighted * scores[None, :, :]
    term_grid = direct * step_size.T[:, None, :]
    mixing = decays * scores[None, :, :] * step_size.T[:, None, :]
    grad_in = skip_gain[None, :, None] * grad_y + jnp.einsum('hts,thp->shp', mixing, grad_y, precision=HIGH)
    last_decay = log_decay[-1]
    to_end = jnp.exp(last_decay[None, :] - log_decay)
    carry_b = jnp.einsum('hpn,sn->shp', carry_in, b_rows, precision=HIGH)
    grad_in = grad_in + (to_end * step_size)[:, :, None] * carry_b
    shared = jnp.einsum('hts,sh->ts', weighted, step_size, precision=HIGH)
    scaled_in = (to_end * step_size)[:, :, None] * inputs
    scaled_grad = jnp.exp(log_decay)[:, :, None] * grad_y
    grad_b = jnp.dot(shared.T, c_rows, precision=HIGH) + jnp.einsum('shp,hpn->sn', scaled_in, carry_in, precision=HIGH)
    grad_c = jnp.dot(shared, b_rows, precision=HIGH) + jnp.einsum('thp,hpn->tn', scaled_grad, state_in, precision=HIGH)
    carried = jnp.einsum('hpn,tn->thp', state_in, c_rows, precision=HIGH)
    carry_dot = lax.optimization_barrier(jnp.sum(inputs * carry_b, axis=2))
    leaving = to_end * step_size * carry_dot
    entering = jnp.exp(log_decay) * lax.optimization_barrier(jnp.sum(grad_y * carried, axis=2))
    grad_log = lax.optimization_barrier(jnp.sum(term_grid, axis=2)).T - lax.optimization_barrier(jnp.sum(term_grid, axis=1)).T + entering - leaving
    constant = lax.optimization_barrier(jnp.sum(leaving, axis=0)) + jnp.exp(last_decay) * lax.optimization_barrier(jnp.sum(carry_in * state_in, axis=(1, 2)))
    grad_rate = jnp.flip(jnp.cumsum(jnp.flip(grad_log, 0), axis=0), 0) + constant[None, :]
    grad_step = lax.optimization_barrier(jnp.sum(direct, axis=1)).T + to_end * carry_dot + decay_rate[None, :] * grad_rate
    return (grad_in, grad_b, grad_c, grad_step)

def reference(x_raw, bc_raw, gate_branch, dt_raw, conv_x, conv_x_bias, conv_bc, conv_bc_bias, dt_bias, a_log, d_skip, out_weight, grad_out):
    margin = KERNEL - 1
    pre_x = convolve(jnp.concatenate([jnp.zeros((margin, x_raw.shape[1]), jnp.float32), x_raw.astype(jnp.float32)]), conv_x, conv_x_bias)
    pre_bc = convolve(jnp.concatenate([jnp.zeros((margin, bc_raw.shape[1]), jnp.float32), bc_raw.astype(jnp.float32)]), conv_bc, conv_bc_bias)
    act_x = jax.nn.silu(pre_x)
    act_bc = jax.nn.silu(pre_bc)
    step_all = jax.nn.softplus(dt_raw + dt_bias[None, :])
    decay_rate = -jnp.exp(a_log)

    def split_blocks(array):
        return array.reshape((N_CTX, TOK_DEV) + array.shape[1:])
    inputs_b = split_blocks(act_x.reshape(SEQUENCE_TOKENS, SHARD_ATTENDERS, P_SIZE))
    b_blocks = split_blocks(act_bc[:, :N])
    c_blocks = split_blocks(act_bc[:, N:])
    step_b = split_blocks(step_all)
    log_b = jnp.cumsum(step_b * decay_rate[None, None, :], axis=1)

    def forward_step(state_in, parts):
        inputs, b_rows, step_size, log_decay = parts
        last_exp, partial_state = local_state(inputs, b_rows, step_size, log_decay)
        return (last_exp[:, None, None] * state_in + partial_state, state_in)
    zero_state = jnp.zeros((SHARD_ATTENDERS, P_SIZE, N), jnp.float32)
    _, states_in = lax.scan(forward_step, zero_state, (inputs_b, b_blocks, step_b, log_b))

    def forward_block(parts):
        inputs, b_rows, c_rows, step_size, log_decay, state_in = parts
        return block_forward(inputs, b_rows, c_rows, step_size, log_decay, state_in, d_skip)
    y_blocks = lax.map(forward_block, (inputs_b, b_blocks, c_blocks, step_b, log_b, states_in))
    y_all = y_blocks.reshape(SEQUENCE_TOKENS, SHARD_ATTENDERS * P_SIZE)
    gate_input = gate_branch.astype(jnp.float32)
    gated = (y_all * jax.nn.silu(gate_input)).astype(jnp.bfloat16)
    grad_gated = lax.dot_general(grad_out, out_weight, (((1,), (1,)), ((), ())), preferred_element_type=jnp.float32)
    grad_z = (grad_gated * y_all * silu_slope(gate_input)).astype(jnp.bfloat16)
    weight_grad = lax.dot_general(grad_out, gated, (((0,), (0,)), ((), ())), preferred_element_type=jnp.float32)
    grad_y = grad_gated * jax.nn.silu(gate_input)
    grad_y_b = split_blocks(grad_y.reshape(SEQUENCE_TOKENS, SHARD_ATTENDERS, P_SIZE))

    def reverse_step(carry, parts):
        log_decay, grad_block, c_rows = parts
        return (jnp.exp(log_decay[-1])[:, None, None] * carry + local_grad(log_decay, grad_block, c_rows), carry)
    _, carries = lax.scan(reverse_step, zero_state, (log_b, grad_y_b, c_blocks), reverse=True)

    def backward_block(parts):
        inputs, b_rows, c_rows, step_size, log_decay, state_in, carry_in, grad_block = parts
        return block_backward(inputs, b_rows, c_rows, step_size, log_decay, decay_rate, state_in, carry_in, grad_block, d_skip)
    grad_in, grad_b, grad_c, grad_step = lax.map(backward_block, (inputs_b, b_blocks, c_blocks, step_b, log_b, states_in, carries, grad_y_b))
    grad_x_conv = (grad_in.reshape(SEQUENCE_TOKENS, SHARD_ATTENDERS * P_SIZE) * silu_slope(pre_x)).astype(jnp.bfloat16)
    grad_bc = jnp.concatenate([grad_b.reshape(SEQUENCE_TOKENS, N), grad_c.reshape(SEQUENCE_TOKENS, N)], axis=1)
    grad_bc_conv = (grad_bc * silu_slope(pre_bc)).astype(jnp.bfloat16)
    grad_dt_raw = grad_step.reshape(SEQUENCE_TOKENS, SHARD_ATTENDERS) * jax.nn.sigmoid(dt_raw + dt_bias[None, :])
    return (grad_x_conv, grad_bc_conv, grad_z, grad_dt_raw, weight_grad)
```

```python
import functools

import jax
import jax.numpy as jnp
from jax import lax
from jax.experimental import pallas as pl
from jax.experimental.pallas import tpu as pltpu
from jax.sharding import PartitionSpec as P

KERNEL = 4
HEAD = 64
LANES = 128
WIRE = jnp.float32
MESH = pl.DeviceIdType.MESH


def dot(a, b, contract):
    return lax.dot_general(
        a,
        b,
        (contract, ((), ())),
        precision=lax.Precision.HIGHEST,
        preferred_element_type=jnp.float32,
    )


NN = ((1,), (0,))
TN = ((0,), (0,))
NT = ((1,), (1,))


def silu_slope(argument):
    gate_value = jax.nn.sigmoid(argument)
    return gate_value * (1.0 + argument * (1.0 - gate_value))


def silu(argument):
    return argument * jax.nn.sigmoid(argument)


def convolve(raw, rim, taps, bias, padded):
    length = raw.shape[0]
    padded[0:8, :] = rim
    padded[8 : 8 + length, :] = raw
    result = jnp.broadcast_to(bias, raw.shape)
    for k in range(KERNEL):
        start = 8 - (KERNEL - 1) + k
        result = result + taps[k : k + 1, :] * padded[start : start + length, :]
    return result


def before_kernel(
    x_ref, rimx_ref, bc_ref, rimbc_ref, gate_ref, ldx_ref, stepx_ref, cx_ref, cxb_ref, cbc_ref,
    cbcb_ref, w_ref, go_ref,
    f_ref, r_ref, prex_ref, gg_ref, prebc_ref,
    padx, padbc, act,
):
    state = bc_ref.shape[1] // 2

    @pl.when(pl.program_id(0) == 0)
    def _():
        pre = convolve(
            bc_ref[...].astype(jnp.float32),
            rimbc_ref[...].astype(jnp.float32),
            cbc_ref[...],
            cbcb_ref[...],
            padbc,
        )
        prebc_ref[...] = pre
        act[...] = silu(pre)

    pre = convolve(
        x_ref[...].astype(jnp.float32),
        rimx_ref[...].astype(jnp.float32),
        cx_ref[...],
        cxb_ref[...],
        padx,
    )
    prex_ref[...] = pre
    b_rows = act[:, :state]
    c_rows = act[:, state:]
    ld = ldx_ref[...]
    last = ld[ld.shape[0] - 1 :, :]
    scaled = jnp.exp(last - ld) * stepx_ref[...] * silu(pre)
    f_ref[...] = dot(b_rows, scaled, TN).astype(f_ref.dtype)
    gg = lax.dot_general(
        go_ref[...], w_ref[...], (NT, ((), ())), preferred_element_type=jnp.float32
    )
    gg_ref[...] = gg
    grad_y = gg * silu(gate_ref[...].astype(jnp.float32))
    r_ref[...] = dot(c_rows, jnp.exp(ld) * grad_y, TN).astype(r_ref.dtype)


def before(x_raw, rimx, bc_raw, rimbc, gate, ldx, stepx, cx, cxb, cbc, cbcb, w, go):
    length, channels = x_raw.shape
    states = bc_raw.shape[1]
    tile = lambda rows: pl.BlockSpec((rows, LANES), lambda q: (0, q))
    whole = lambda a: pl.BlockSpec(a.shape, lambda q: (0, 0))
    f32 = jnp.float32
    return pl.pallas_call(
        before_kernel,
        grid=(channels // LANES,),
        in_specs=[
            tile(length), tile(8), whole(bc_raw), whole(rimbc), tile(length), tile(length),
            tile(length), tile(KERNEL), tile(1), whole(cbc), whole(cbcb),
            pl.BlockSpec((LANES, w.shape[1]), lambda q: (q, 0)), whole(go),
        ],
        out_specs=[
            tile(states // 2), tile(states // 2), tile(length), tile(length),
            pl.BlockSpec((length, states), lambda q: (0, 0)),
        ],
        out_shape=[
            jax.ShapeDtypeStruct((states // 2, channels), WIRE),
            jax.ShapeDtypeStruct((states // 2, channels), WIRE),
            jax.ShapeDtypeStruct((length, channels), f32),
            jax.ShapeDtypeStruct((length, channels), f32),
            jax.ShapeDtypeStruct((length, states), f32),
        ],
        scratch_shapes=[
            pltpu.VMEM((length + 8, LANES), f32),
            pltpu.VMEM((length + 8, states), f32),
            pltpu.VMEM((length, states), f32),
        ],
        name="before",
    )(x_raw, rimx, bc_raw, rimbc, gate, ldx, stepx, cx, cxb, cbc, cbcb, w, go)


ROWS = 16
ROW_TILES = 8
PER_LINE = 5
LINE = 8


def owner_of(piece, shift):
    line = lax.rem(piece, 16)
    rank = piece // 16
    spot = lax.rem((LINE * rank) // PER_LINE + shift + 2 * line + line // 4, LINE)
    return line * LINE + spot


def piece_of(chip, shift):
    line = chip // LINE
    spot = lax.rem(
        lax.rem(chip, LINE) + 8 * LINE - shift - 2 * line - line // 4, LINE
    )
    rank = (PER_LINE * spot + LINE - 1) // LINE
    owns = (LINE * rank) // PER_LINE == spot
    return rank * 16 + line, owns


def scan_kernel(
    count, pieces, f_ref, r_ref, decay_ref, sin_ref, rin_ref,
    got_f, got_r, out_f, out_r, decay_f, decay_r,
    send, recv, back_send, back_recv, decay_send, decay_recv,
):
    me = lax.axis_index("ctx")
    barrier = pltpu.get_barrier_semaphore()

    def greet(k, carry):
        pl.semaphore_signal(
            barrier, inc=1, device_id={"ctx": lax.rem(me + k, count)}, device_id_type=MESH
        )
        return carry

    lax.fori_loop(1, count, greet, 0)
    pl.semaphore_wait(barrier, count - 1)

    def window(ref, piece):
        row = pl.multiple_of(lax.rem(piece, ROW_TILES) * ROWS, ROWS)
        lane = pl.multiple_of((piece // ROW_TILES) * LANES, LANES)
        return ref.at[pl.ds(row, ROWS), pl.ds(lane, LANES)]

    sets = (
        (0, f_ref, decay_f, sin_ref, got_f, out_f, False),
        (1, r_ref, decay_r, rin_ref, got_r, out_r, True),
    )

    def copy(src, dst, peer, here, there):
        return pltpu.make_async_remote_copy(
            src_ref=src, dst_ref=dst, send_sem=here, recv_sem=there,
            device_id={"ctx": peer}, device_id_type=MESH,
        )

    for which, src, decay, dst, got, out, reverse in sets:

        def give(k, carry):
            piece = lax.rem(k + me, pieces)
            owner = owner_of(piece, which)

            @pl.when(owner != me)
            def _():
                copy(window(src, piece), got.at[me], owner, send.at[which], recv.at[which]).start()
                copy(
                    decay_ref.at[piece // ROW_TILES], decay.at[me], owner,
                    decay_send.at[which], decay_recv.at[which],
                ).start()

            return carry

        lax.fori_loop(0, pieces, give, 0)

    for which, src, decay, dst, got, out, reverse in sets:
        mine, owns = piece_of(me, which)
        row = pl.multiple_of(lax.rem(mine, ROW_TILES) * ROWS, ROWS)
        lane = pl.multiple_of((mine // ROW_TILES) * LANES, LANES)

        @pl.when(owns)
        def _():
            got[me] = src[pl.ds(row, ROWS), pl.ds(lane, LANES)]
            decay[me] = decay_ref[mine // ROW_TILES]
            some = got.at[pl.ds(0, count - 1)]
            copy(some, some, 0, send.at[which], recv.at[which]).wait_recv()
            some = decay.at[pl.ds(0, count - 1)]
            copy(some, some, 0, decay_send.at[which], decay_recv.at[which]).wait_recv()

            def step(k, state):
                at = count - 1 - k if reverse else k
                out[at] = state.astype(out.dtype)
                return decay[at] * state + got[at].astype(jnp.float32)

            lax.fori_loop(0, count, step, jnp.zeros((ROWS, LANES), jnp.float32))
            dst[pl.ds(row, ROWS), pl.ds(lane, LANES)] = out[me]

            def give_back(k, carry):
                peer = lax.rem(me + k, count)
                copy(
                    out.at[peer], window(dst, mine), peer, back_send.at[which], back_recv.at[which]
                ).start()
                return carry

            lax.fori_loop(1, count, give_back, 0)

    for which, src, decay, dst, got, out, reverse in sets:
        mine, owns = piece_of(me, which)

        @pl.when(owns)
        def _():
            less = got.at[pl.ds(0, pieces - 1)]
            rest = out.at[pl.ds(0, count - 1)]
            few = decay.at[pl.ds(0, pieces - 1)]
            copy(less, less, 0, send.at[which], back_recv.at[which]).wait_send()
            copy(few, few, 0, decay_send.at[which], decay_recv.at[which]).wait_send()
            copy(less, less, 0, send.at[which], back_recv.at[which]).wait_recv()
            copy(rest, rest, 0, back_send.at[which], back_recv.at[which]).wait_send()

        @pl.when(jnp.logical_not(owns))
        def _():
            full = got.at[pl.ds(0, pieces)]
            few = decay.at[pl.ds(0, pieces)]
            copy(full, full, 0, send.at[which], back_recv.at[which]).wait_send()
            copy(few, few, 0, decay_send.at[which], decay_recv.at[which]).wait_send()
            copy(full, full, 0, send.at[which], back_recv.at[which]).wait_recv()


def scans(f, r, decays, count):
    pieces = f.shape[0] * f.shape[1] // (ROWS * LANES)
    slot = pltpu.VMEM((count, ROWS, LANES), WIRE)
    vmem = pl.BlockSpec(memory_space=pltpu.VMEM)
    return pl.pallas_call(
        functools.partial(scan_kernel, count, pieces),
        out_shape=[jax.ShapeDtypeStruct(f.shape, WIRE)] * 2,
        in_specs=[vmem] * 3,
        out_specs=[vmem] * 2,
        scratch_shapes=[slot] * 4
        + [pltpu.VMEM((count, 1, LANES), jnp.float32)] * 2
        + [pltpu.SemaphoreType.DMA((2,))] * 6,
        compiler_params=pltpu.CompilerParams(collective_id=0, has_side_effects=True),
        name="scans",
    )(f, r, decays)


def after_kernel(
    sin_ref, rin_ref, prex_ref, gg_ref, gate_ref, prebc_ref, ldx_ref, stepx_ref, dskip_ref,
    ldt_ref, stept_ref, ld_ref, step_ref, rate_ref,
    gated_ref, gradz_ref, gxc_ref, gbc_ref, gstep_ref,
    act, scores, shared, grad_b, grad_c, sums, const,
):
    q = pl.program_id(0)
    length = prex_ref.shape[0]
    state = sin_ref.shape[0]
    rows = lax.broadcasted_iota(jnp.int32, (length, length), 0)
    cols = lax.broadcasted_iota(jnp.int32, (length, length), 1)
    lower = rows >= cols
    lane = lax.broadcasted_iota(jnp.int32, (length, LANES), 1)
    first = lane < HEAD

    @pl.when(q == 0)
    def _():
        act[...] = silu(prebc_ref[...])
        scores[...] = dot(act[:, state:], act[:, :state], NT)
        shared[...] = jnp.zeros_like(shared)
        grad_b[...] = jnp.zeros_like(grad_b)
        grad_c[...] = jnp.zeros_like(grad_c)
        sums[...] = jnp.zeros_like(sums)
        const[...] = jnp.zeros_like(const)

    b_rows = act[:, :state]
    c_rows = act[:, state:]
    pre = prex_ref[...]
    x = silu(pre)
    gate = gate_ref[...].astype(jnp.float32)
    gg = gg_ref[...]
    gate_silu = silu(gate)
    gy = gg * gate_silu
    ld = ldx_ref[...]
    step = stepx_ref[...]
    grow = jnp.exp(ld)
    last = ld[length - 1 :, :]
    to_end = jnp.exp(last - ld)
    dskip = dskip_ref[...]
    s_in = sin_ref[...].astype(jnp.float32)
    r_in = rin_ref[...].astype(jnp.float32)
    carried = dot(c_rows, s_in, NN)
    carry_b = dot(b_rows, r_in, NN)
    xs = step * x
    withins, grads = [], []
    total = shared[...]
    for a in range(2):
        spread = ld[:, a * HEAD : a * HEAD + 1] - ldt_ref[0, a : a + 1, :]
        decays = jnp.where(lower, jnp.exp(jnp.where(lower, spread, 0.0)), 0.0)
        mixing = decays * scores[...]
        withins.append(dot(mixing, xs, NN))
        grads.append(dot(mixing, gy, TN))
        own = first if a == 0 else jnp.logical_not(first)
        products = dot(jnp.where(own, gy, 0.0), x, NT)
        total = total + decays * products * stept_ref[0, a : a + 1, :]
    shared[...] = total
    within = jnp.where(first, withins[0], withins[1])
    grad0 = jnp.where(first, grads[0], grads[1])
    y = within + grow * carried + dskip * x
    gated_ref[...] = (y * gate_silu).astype(gated_ref.dtype)
    gradz_ref[...] = (gg * y * silu_slope(gate)).astype(gradz_ref.dtype)
    weight = to_end * step
    grad_in = dskip * gy + step * grad0 + weight * carry_b
    gxc_ref[...] = (grad_in * silu_slope(pre)).astype(gxc_ref.dtype)
    grad_b[...] += dot(weight * x, r_in, NT)
    grad_c[...] += dot(grow * gy, s_in, NT)

    def head_sums(value):
        left = jnp.sum(jnp.where(first, value, 0.0), axis=1, keepdims=True)
        right = jnp.sum(jnp.where(first, 0.0, value), axis=1, keepdims=True)
        return jnp.where(lane == 2 * q, left, jnp.where(lane == 2 * q + 1, right, 0.0))

    for k, value in enumerate((gy * within, x * grad0, x * carry_b, gy * carried)):
        sums[k] += head_sums(value)
    const[...] += head_sums(jnp.broadcast_to(jnp.sum(r_in * s_in, axis=0, keepdims=True), x.shape))

    @pl.when(q == pl.num_programs(0) - 1)
    def _():
        ldh = ld_ref[...]
        steph = step_ref[...]
        lasth = ldh[length - 1 :, :]
        to_endh = jnp.exp(lasth - ldh)
        inner, direct, carry_dot, enter = sums[0], sums[1], sums[2], sums[3]
        leaving = to_endh * steph * carry_dot
        grad_log = inner - steph * direct + jnp.exp(ldh) * enter - leaving
        constant = jnp.sum(leaving, axis=0, keepdims=True) + jnp.exp(lasth) * const[0:1, :]
        upper = jnp.where(cols >= rows, 1.0, 0.0)
        grad_rate = dot(upper, grad_log, NN) + constant
        gstep_ref[...] = direct + to_endh * carry_dot + rate_ref[...] * grad_rate
        gbc_ref[:, :state] = grad_b[...] + dot(total, c_rows, TN)
        gbc_ref[:, state:] = grad_c[...] + dot(total, b_rows, NN)


def after(sin, rin, prex, gg, gate, prebc, ldx, stepx, dskipx, ldt, stept, ld, step, rate):
    length, channels = prex.shape
    state = sin.shape[0]
    tile = lambda rows: pl.BlockSpec((rows, LANES), lambda q: (0, q))
    whole = lambda a: pl.BlockSpec(a.shape, lambda q: (0, 0))
    pair = pl.BlockSpec((1, 2, length), lambda q: (q, 0, 0))
    f32 = jnp.float32
    return pl.pallas_call(
        after_kernel,
        grid=(channels // LANES,),
        in_specs=[
            tile(state), tile(state), tile(length), tile(length), tile(length), whole(prebc),
            tile(length), tile(length), tile(1), pair, pair, whole(ld), whole(step), whole(rate),
        ],
        out_specs=[
            tile(length), tile(length), tile(length),
            pl.BlockSpec((length, 2 * state), lambda q: (0, 0)),
            pl.BlockSpec((length, LANES), lambda q: (0, 0)),
        ],
        out_shape=[
            jax.ShapeDtypeStruct((length, channels), jnp.bfloat16),
            jax.ShapeDtypeStruct((length, channels), jnp.bfloat16),
            jax.ShapeDtypeStruct((length, channels), jnp.bfloat16),
            jax.ShapeDtypeStruct((length, 2 * state), f32),
            jax.ShapeDtypeStruct((length, LANES), f32),
        ],
        scratch_shapes=[
            pltpu.VMEM((length, 2 * state), f32),
            pltpu.VMEM((length, length), f32),
            pltpu.VMEM((length, length), f32),
            pltpu.VMEM((length, state), f32),
            pltpu.VMEM((length, state), f32),
            pltpu.VMEM((4, length, LANES), f32),
            pltpu.VMEM((length, LANES), f32),
        ],
        name="after",
    )(sin, rin, prex, gg, gate, prebc, ldx, stepx, dskipx, ldt, stept, ld, step, rate)


def per_device(
    x_raw, bc_raw, gate_branch, dt_raw, conv_x, conv_x_bias, conv_bc, conv_bc_bias, dt_bias, a_log,
    d_skip, out_weight, grad_out,
):
    length, heads = dt_raw.shape
    channels = x_raw.shape[1]
    blocks = lax.axis_size("ctx")
    joined = jnp.concatenate([x_raw[length - 8 :], bc_raw[length - 8 :]], axis=1)
    rim = lax.ppermute(joined, "ctx", [(i, i + 1) for i in range(blocks - 1)])
    step = jax.nn.softplus(dt_raw + dt_bias[None, :])
    rate = -jnp.exp(a_log)
    ld = jnp.cumsum(step * rate[None, :], axis=0)
    ldx = jnp.repeat(ld, HEAD, axis=1)
    stepx = jnp.repeat(step, HEAD, axis=1)
    f, r, prex, gg, prebc = before(
        x_raw, rim[:, :channels], bc_raw, rim[:, channels:], gate_branch, ldx, stepx,
        conv_x, conv_x_bias[None, :], conv_bc, conv_bc_bias[None, :], out_weight, grad_out,
    )
    decays = jnp.exp(ldx[length - 1]).reshape(channels // LANES, 1, LANES)
    s_in, r_in = scans(f, r, decays, blocks)
    wide = lambda a: jnp.pad(a, ((0, 0), (0, LANES - heads)))
    pairs = lambda a: a.T.reshape(heads // 2, 2, length)
    gated, grad_z, gxc, gbc, grad_step = after(
        s_in, r_in, prex, gg, gate_branch, prebc, ldx, stepx,
        jnp.repeat(d_skip, HEAD)[None, :], pairs(ld), pairs(step), wide(ld), wide(step),
        wide(rate[None, :]),
    )
    weight_terms = lax.dot_general(
        grad_out, gated, (((0,), (0,)), ((), ())), preferred_element_type=jnp.float32
    )
    weight_grad = lax.psum_scatter(weight_terms, "ctx", scatter_dimension=0, tiled=True)
    grad_bc = lax.psum(gbc, "tp")
    grad_bc_conv = (grad_bc * silu_slope(prebc)).astype(jnp.bfloat16)
    grad_dt_raw = grad_step[:, :heads] * jax.nn.sigmoid(dt_raw + dt_bias[None, :])
    return (gxc, grad_bc_conv, grad_z, grad_dt_raw, weight_grad)


def solution(mesh):
    placed = (
        P("ctx", "tp"), P("ctx", None), P("ctx", "tp"), P("ctx", "tp"), P(None, "tp"), P("tp"),
        P(), P(), P("tp"), P("tp"), P("tp"), P("tp", None), P("ctx", None),
    )
    return jax.shard_map(
        per_device,
        mesh=mesh,
        in_specs=placed,
        out_specs=(P("ctx", "tp"), P("ctx", None), P("ctx", "tp"), P("ctx", "tp"), P("ctx", "tp")),
        check_vma=False,
    )
```

```python
import functools

import jax
import jax.numpy as jnp
from jax import lax
from jax.experimental import pallas as pl
from jax.experimental.pallas import tpu as pltpu
from jax.sharding import PartitionSpec as P

KERNEL = 4
HEAD = 64
LANES = 128
WIRE = jnp.float32
MESH = pl.DeviceIdType.MESH


def dot(a, b, contract):
    return lax.dot_general(
        a,
        b,
        (contract, ((), ())),
        precision=lax.Precision.HIGHEST,
        preferred_element_type=jnp.float32,
    )


NN = ((1,), (0,))
TN = ((0,), (0,))
NT = ((1,), (1,))


def silu_slope(argument):
    gate_value = jax.nn.sigmoid(argument)
    return gate_value * (1.0 + argument * (1.0 - gate_value))


def silu(argument):
    return argument * jax.nn.sigmoid(argument)


def convolve(raw, rim, taps, bias, padded):
    length = raw.shape[0]
    padded[0:8, :] = rim
    padded[8 : 8 + length, :] = raw
    result = jnp.broadcast_to(bias, raw.shape)
    for k in range(KERNEL):
        start = 8 - (KERNEL - 1) + k
        result = result + taps[k : k + 1, :] * padded[start : start + length, :]
    return result


def before_kernel(
    x_ref, rimx_ref, bc_ref, rimbc_ref, gate_ref, ldx_ref, stepx_ref, cx_ref, cxb_ref, cbc_ref,
    cbcb_ref, w_ref, go_ref,
    f_ref, r_ref, prex_ref, gg_ref, prebc_ref,
    padx, padbc, act,
):
    state = bc_ref.shape[1] // 2

    @pl.when(pl.program_id(0) == 0)
    def _():
        pre = convolve(
            bc_ref[...].astype(jnp.float32),
            rimbc_ref[...].astype(jnp.float32),
            cbc_ref[...],
            cbcb_ref[...],
            padbc,
        )
        prebc_ref[...] = pre
        act[...] = silu(pre)

    pre = convolve(
        x_ref[...].astype(jnp.float32),
        rimx_ref[...].astype(jnp.float32),
        cx_ref[...],
        cxb_ref[...],
        padx,
    )
    prex_ref[...] = pre
    b_rows = act[:, :state]
    c_rows = act[:, state:]
    ld = ldx_ref[...]
    last = ld[ld.shape[0] - 1 :, :]
    scaled = jnp.exp(last - ld) * stepx_ref[...] * silu(pre)
    f_ref[...] = dot(b_rows, scaled, TN).astype(f_ref.dtype)
    gg = lax.dot_general(
        go_ref[...], w_ref[...], (NT, ((), ())), preferred_element_type=jnp.float32
    )
    gg_ref[...] = gg
    grad_y = gg * silu(gate_ref[...].astype(jnp.float32))
    r_ref[...] = dot(c_rows, jnp.exp(ld) * grad_y, TN).astype(r_ref.dtype)


def before(x_raw, rimx, bc_raw, rimbc, gate, ldx, stepx, cx, cxb, cbc, cbcb, w, go):
    length, channels = x_raw.shape
    states = bc_raw.shape[1]
    tile = lambda rows: pl.BlockSpec((rows, LANES), lambda q: (0, q))
    whole = lambda a: pl.BlockSpec(a.shape, lambda q: (0, 0))
    f32 = jnp.float32
    return pl.pallas_call(
        before_kernel,
        grid=(channels // LANES,),
        in_specs=[
            tile(length), tile(8), whole(bc_raw), whole(rimbc), tile(length), tile(length),
            tile(length), tile(KERNEL), tile(1), whole(cbc), whole(cbcb),
            pl.BlockSpec((LANES, w.shape[1]), lambda q: (q, 0)), whole(go),
        ],
        out_specs=[
            tile(states // 2), tile(states // 2), tile(length), tile(length),
            pl.BlockSpec((length, states), lambda q: (0, 0)),
        ],
        out_shape=[
            jax.ShapeDtypeStruct((states // 2, channels), WIRE),
            jax.ShapeDtypeStruct((states // 2, channels), WIRE),
            jax.ShapeDtypeStruct((length, channels), f32),
            jax.ShapeDtypeStruct((length, channels), f32),
            jax.ShapeDtypeStruct((length, states), f32),
        ],
        scratch_shapes=[
            pltpu.VMEM((length + 8, LANES), f32),
            pltpu.VMEM((length + 8, states), f32),
            pltpu.VMEM((length, states), f32),
        ],
        name="before",
    )(x_raw, rimx, bc_raw, rimbc, gate, ldx, stepx, cx, cxb, cbc, cbcb, w, go)


ROWS = 16
ROW_TILES = 8
PER_LINE = 5
LINE = 8
SIDE = 4


def owner_of(piece, shift):
    line = lax.rem(piece, 16)
    rank = piece // 16
    spot = lax.rem((LINE * rank) // PER_LINE + shift + 2 * line + line // 4, LINE)
    return line * LINE + spot


def piece_of(chip, shift):
    line = chip // LINE
    spot = lax.rem(
        lax.rem(chip, LINE) + 8 * LINE - shift - 2 * line - line // 4, LINE
    )
    rank = (PER_LINE * spot + LINE - 1) // LINE
    owns = (LINE * rank) // PER_LINE == spot
    return rank * 16 + line, owns


def scan_kernel(
    count, pieces, f_ref, r_ref, decay_ref, go_ref, sin_ref, rin_ref, all_ref,
    got_f, got_r, out_f, out_r, decay_f, decay_r,
    send, recv, back_send, back_recv, decay_send, decay_recv, go_send, go_recv,
):
    me = lax.axis_index("ctx")
    barrier = pltpu.get_barrier_semaphore()

    def greet(k, carry):
        pl.semaphore_signal(
            barrier, inc=1, device_id={"ctx": lax.rem(me + k, count)}, device_id_type=MESH
        )
        return carry

    lax.fori_loop(1, count, greet, 0)
    pl.semaphore_wait(barrier, count - 1)

    def window(ref, piece):
        row = pl.multiple_of(lax.rem(piece, ROW_TILES) * ROWS, ROWS)
        lane = pl.multiple_of((piece // ROW_TILES) * LANES, LANES)
        return ref.at[pl.ds(row, ROWS), pl.ds(lane, LANES)]

    sets = (
        (0, f_ref, decay_f, sin_ref, got_f, out_f, False),
        (1, r_ref, decay_r, rin_ref, got_r, out_r, True),
    )

    def copy(src, dst, peer, here, there):
        return pltpu.make_async_remote_copy(
            src_ref=src, dst_ref=dst, send_sem=here, recv_sem=there,
            device_id={"ctx": peer}, device_id_type=MESH,
        )

    for which, src, decay, dst, got, out, reverse in sets:

        def give(k, carry):
            piece = lax.rem(k + me, pieces)
            owner = owner_of(piece, which)

            @pl.when(owner != me)
            def _():
                copy(window(src, piece), got.at[me], owner, send.at[which], recv.at[which]).start()
                copy(
                    decay_ref.at[piece // ROW_TILES], decay.at[me], owner,
                    decay_send.at[which], decay_recv.at[which],
                ).start()

            return carry

        lax.fori_loop(0, pieces, give, 0)

    spot = lax.rem(me, LINE)
    line = me // LINE
    x, y = line // SIDE, lax.rem(line, SIDE)
    middle = go_ref.shape[1] // 2
    early, late = pl.ds(0, middle), pl.ds(middle, middle)
    along_x = [lax.rem(x + d, SIDE) * SIDE + y for d in range(SIDE)]
    along_y = [x * SIDE + lax.rem(y + d, SIDE) for d in range(SIDE)]

    def shift_go(src, dst, to, at):
        copy(src, dst, to * LINE + spot, go_send.at[at], go_recv.at[at]).start()

    all_ref[line] = go_ref[...]
    for d in range(1, SIDE):
        shift_go(go_ref.at[:, early], all_ref.at[line, :, early], along_y[d], 0)
        shift_go(go_ref.at[:, late], all_ref.at[line, :, late], along_x[d], 1)

    def second_go():
        some = all_ref.at[pl.ds(0, SIDE - 1), :, early]
        for at in range(2):
            copy(some, some, 0, go_send.at[at], go_recv.at[at]).wait_recv()
        for d in range(1, SIDE):
            for other in range(SIDE):
                held = all_ref.at[along_y[other], :, early]
                shift_go(held, held, along_x[d], 2)
                held = all_ref.at[along_x[other], :, late]
                shift_go(held, held, along_y[d], 3)

    def finish_go():
        some = all_ref.at[pl.ds(0, SIDE - 1), :, early]
        most = all_ref.at[pl.ds(0, SIDE * (SIDE - 1)), :, early]
        for at in range(2):
            copy(some, some, 0, go_send.at[at], go_recv.at[at]).wait_send()
            copy(most, most, 0, go_send.at[2 + at], go_recv.at[2 + at]).wait()

    for which, src, decay, dst, got, out, reverse in sets:
        if which == 1:
            second_go()
        mine, owns = piece_of(me, which)
        row = pl.multiple_of(lax.rem(mine, ROW_TILES) * ROWS, ROWS)
        lane = pl.multiple_of((mine // ROW_TILES) * LANES, LANES)

        @pl.when(owns)
        def _():
            got[me] = src[pl.ds(row, ROWS), pl.ds(lane, LANES)]
            decay[me] = decay_ref[mine // ROW_TILES]
            some = got.at[pl.ds(0, count - 1)]
            copy(some, some, 0, send.at[which], recv.at[which]).wait_recv()
            some = decay.at[pl.ds(0, count - 1)]
            copy(some, some, 0, decay_send.at[which], decay_recv.at[which]).wait_recv()

            def step(k, state):
                at = count - 1 - k if reverse else k
                out[at] = state.astype(out.dtype)
                return decay[at] * state + got[at].astype(jnp.float32)

            lax.fori_loop(0, count, step, jnp.zeros((ROWS, LANES), jnp.float32))
            dst[pl.ds(row, ROWS), pl.ds(lane, LANES)] = out[me]

            def give_back(k, carry):
                peer = lax.rem(me + k, count)
                copy(
                    out.at[peer], window(dst, mine), peer, back_send.at[which], back_recv.at[which]
                ).start()
                return carry

            lax.fori_loop(1, count, give_back, 0)

    for which, src, decay, dst, got, out, reverse in sets:
        mine, owns = piece_of(me, which)

        @pl.when(owns)
        def _():
            less = got.at[pl.ds(0, pieces - 1)]
            rest = out.at[pl.ds(0, count - 1)]
            few = decay.at[pl.ds(0, pieces - 1)]
            copy(less, less, 0, send.at[which], back_recv.at[which]).wait_send()
            copy(few, few, 0, decay_send.at[which], decay_recv.at[which]).wait_send()
            copy(less, less, 0, send.at[which], back_recv.at[which]).wait_recv()
            copy(rest, rest, 0, back_send.at[which], back_recv.at[which]).wait_send()

        @pl.when(jnp.logical_not(owns))
        def _():
            full = got.at[pl.ds(0, pieces)]
            few = decay.at[pl.ds(0, pieces)]
            copy(full, full, 0, send.at[which], back_recv.at[which]).wait_send()
            copy(few, few, 0, decay_send.at[which], decay_recv.at[which]).wait_send()
            copy(full, full, 0, send.at[which], back_recv.at[which]).wait_recv()

    finish_go()


def scans(f, r, decays, go, count):
    pieces = f.shape[0] * f.shape[1] // (ROWS * LANES)
    slot = pltpu.VMEM((count, ROWS, LANES), WIRE)
    vmem = pl.BlockSpec(memory_space=pltpu.VMEM)
    return pl.pallas_call(
        functools.partial(scan_kernel, count, pieces),
        out_shape=[jax.ShapeDtypeStruct(f.shape, WIRE)] * 2
        + [jax.ShapeDtypeStruct((count // LINE,) + go.shape, go.dtype)],
        in_specs=[vmem] * 4,
        out_specs=[vmem] * 3,
        scratch_shapes=[slot] * 4
        + [pltpu.VMEM((count, 1, LANES), jnp.float32)] * 2
        + [pltpu.SemaphoreType.DMA((2,))] * 6
        + [pltpu.SemaphoreType.DMA((4,))] * 2,
        compiler_params=pltpu.CompilerParams(collective_id=0, has_side_effects=True),
        name="scans",
    )(f, r, decays, go)


def after_kernel(
    sin_ref, rin_ref, prex_ref, gg_ref, gate_ref, prebc_ref, ldx_ref, stepx_ref, dskip_ref,
    ldt_ref, stept_ref, ld_ref, step_ref, rate_ref,
    gated_ref, gradz_ref, gxc_ref, gbc_ref, gstep_ref,
    act, scores, shared, grad_b, grad_c, sums, const,
):
    q = pl.program_id(0)
    length = prex_ref.shape[0]
    state = sin_ref.shape[0]
    rows = lax.broadcasted_iota(jnp.int32, (length, length), 0)
    cols = lax.broadcasted_iota(jnp.int32, (length, length), 1)
    lower = rows >= cols
    lane = lax.broadcasted_iota(jnp.int32, (length, LANES), 1)
    first = lane < HEAD

    @pl.when(q == 0)
    def _():
        act[...] = silu(prebc_ref[...])
        scores[...] = dot(act[:, state:], act[:, :state], NT)
        shared[...] = jnp.zeros_like(shared)
        grad_b[...] = jnp.zeros_like(grad_b)
        grad_c[...] = jnp.zeros_like(grad_c)
        sums[...] = jnp.zeros_like(sums)
        const[...] = jnp.zeros_like(const)

    b_rows = act[:, :state]
    c_rows = act[:, state:]
    pre = prex_ref[...]
    x = silu(pre)
    gate = gate_ref[...].astype(jnp.float32)
    gg = gg_ref[...]
    gate_silu = silu(gate)
    gy = gg * gate_silu
    ld = ldx_ref[...]
    step = stepx_ref[...]
    grow = jnp.exp(ld)
    last = ld[length - 1 :, :]
    to_end = jnp.exp(last - ld)
    dskip = dskip_ref[...]
    s_in = sin_ref[...].astype(jnp.float32)
    r_in = rin_ref[...].astype(jnp.float32)
    carried = dot(c_rows, s_in, NN)
    carry_b = dot(b_rows, r_in, NN)
    xs = step * x
    withins, grads = [], []
    total = shared[...]
    for a in range(2):
        spread = ld[:, a * HEAD : a * HEAD + 1] - ldt_ref[0, a : a + 1, :]
        decays = jnp.where(lower, jnp.exp(jnp.where(lower, spread, 0.0)), 0.0)
        mixing = decays * scores[...]
        withins.append(dot(mixing, xs, NN))
        grads.append(dot(mixing, gy, TN))
        own = first if a == 0 else jnp.logical_not(first)
        products = dot(jnp.where(own, gy, 0.0), x, NT)
        total = total + decays * products * stept_ref[0, a : a + 1, :]
    shared[...] = total
    within = jnp.where(first, withins[0], withins[1])
    grad0 = jnp.where(first, grads[0], grads[1])
    y = within + grow * carried + dskip * x
    gated_ref[...] = (y * gate_silu).astype(gated_ref.dtype)
    gradz_ref[...] = (gg * y * silu_slope(gate)).astype(gradz_ref.dtype)
    weight = to_end * step
    grad_in = dskip * gy + step * grad0 + weight * carry_b
    gxc_ref[...] = (grad_in * silu_slope(pre)).astype(gxc_ref.dtype)
    grad_b[...] += dot(weight * x, r_in, NT)
    grad_c[...] += dot(grow * gy, s_in, NT)

    def head_sums(value):
        left = jnp.sum(jnp.where(first, value, 0.0), axis=1, keepdims=True)
        right = jnp.sum(jnp.where(first, 0.0, value), axis=1, keepdims=True)
        return jnp.where(lane == 2 * q, left, jnp.where(lane == 2 * q + 1, right, 0.0))

    for k, value in enumerate((gy * within, x * grad0, x * carry_b, gy * carried)):
        sums[k] += head_sums(value)
    const[...] += head_sums(jnp.broadcast_to(jnp.sum(r_in * s_in, axis=0, keepdims=True), x.shape))

    @pl.when(q == pl.num_programs(0) - 1)
    def _():
        ldh = ld_ref[...]
        steph = step_ref[...]
        lasth = ldh[length - 1 :, :]
        to_endh = jnp.exp(lasth - ldh)
        inner, direct, carry_dot, enter = sums[0], sums[1], sums[2], sums[3]
        leaving = to_endh * steph * carry_dot
        grad_log = inner - steph * direct + jnp.exp(ldh) * enter - leaving
        constant = jnp.sum(leaving, axis=0, keepdims=True) + jnp.exp(lasth) * const[0:1, :]
        upper = jnp.where(cols >= rows, 1.0, 0.0)
        grad_rate = dot(upper, grad_log, NN) + constant
        gstep_ref[...] = direct + to_endh * carry_dot + rate_ref[...] * grad_rate
        gbc_ref[:, :state] = grad_b[...] + dot(total, c_rows, TN)
        gbc_ref[:, state:] = grad_c[...] + dot(total, b_rows, NN)


def after(sin, rin, prex, gg, gate, prebc, ldx, stepx, dskipx, ldt, stept, ld, step, rate):
    length, channels = prex.shape
    state = sin.shape[0]
    tile = lambda rows: pl.BlockSpec((rows, LANES), lambda q: (0, q))
    whole = lambda a: pl.BlockSpec(a.shape, lambda q: (0, 0))
    pair = pl.BlockSpec((1, 2, length), lambda q: (q, 0, 0))
    f32 = jnp.float32
    return pl.pallas_call(
        after_kernel,
        grid=(channels // LANES,),
        in_specs=[
            tile(state), tile(state), tile(length), tile(length), tile(length), whole(prebc),
            tile(length), tile(length), tile(1), pair, pair, whole(ld), whole(step), whole(rate),
        ],
        out_specs=[
            tile(length), tile(length), tile(length),
            pl.BlockSpec((length, 2 * state), lambda q: (0, 0)),
            pl.BlockSpec((length, LANES), lambda q: (0, 0)),
        ],
        out_shape=[
            jax.ShapeDtypeStruct((length, channels), jnp.bfloat16),
            jax.ShapeDtypeStruct((length, channels), jnp.bfloat16),
            jax.ShapeDtypeStruct((length, channels), jnp.bfloat16),
            jax.ShapeDtypeStruct((length, 2 * state), f32),
            jax.ShapeDtypeStruct((length, LANES), f32),
        ],
        scratch_shapes=[
            pltpu.VMEM((length, 2 * state), f32),
            pltpu.VMEM((length, length), f32),
            pltpu.VMEM((length, length), f32),
            pltpu.VMEM((length, state), f32),
            pltpu.VMEM((length, state), f32),
            pltpu.VMEM((4, length, LANES), f32),
            pltpu.VMEM((length, LANES), f32),
        ],
        name="after",
    )(sin, rin, prex, gg, gate, prebc, ldx, stepx, dskipx, ldt, stept, ld, step, rate)


OWN = 20


def tile_core(tile):
    return tile // 10


def weight_kernel(
    count, gated_ref, go_ref, out_ref,
    main, extra, sums, more, slots, got, g_send, g_recv, w_send, w_recv,
):
    me = lax.axis_index("ctx")
    core = lax.axis_index("tp")
    line, spot = me // LINE, lax.rem(me, LINE)
    lines = count // LINE
    half = count // 2
    length = gated_ref.shape[0]
    quarter = lax.rem(line, 4)
    barrier = pltpu.get_barrier_semaphore()

    def greet(k, carry):
        peer = lax.rem(me + k, count)
        for d in range(2):

            @pl.when(jnp.logical_or(k > 0, core != d))
            def _():
                pl.semaphore_signal(
                    barrier, inc=1, device_id={"ctx": peer, "tp": d}, device_id_type=MESH
                )

        return carry

    lax.fori_loop(0, count, greet, 0)
    pl.semaphore_wait(barrier, 2 * count - 1)

    def copy(src, dst, chip, d, here, there):
        return pltpu.make_async_remote_copy(
            src_ref=src, dst_ref=dst, send_sem=here, recv_sem=there,
            device_id={"ctx": chip, "tp": d}, device_id_type=MESH,
        )

    def lanes(tile):
        return pl.ds(pl.multiple_of((tile - 10 * core) * LANES, LANES), LANES)

    def give(k, carry):
        to = lax.rem(line + k, lines)
        chip = to * LINE + spot
        for d in range(2):
            away = jnp.logical_or(to != line, core != d)
            for at, tile, store in ((0, to, main), (1, 16 + to // 4, extra)):
                mine = tile_core(tile) == core

                @pl.when(jnp.logical_and(mine, away))
                def _():
                    copy(
                        gated_ref.at[:, lanes(tile)], store.at[line], chip, d,
                        g_send.at[2 * at + d], g_recv.at[at],
                    ).start()

                @pl.when(jnp.logical_and(mine, jnp.logical_not(away)))
                def _():
                    store[line] = gated_ref[:, lanes(tile)]

        return carry

    lax.fori_loop(0, lines, give, 0)

    def wait_for(number, options, ref, act):
        for n in options:

            @pl.when(number == n)
            def _():
                act(ref.at[pl.ds(0, n)])

    one = lambda flag: jnp.where(flag, 1, 0)

    def wait_gated(at):
        tile = line if at == 0 else 16 + line // 4
        number = lines - one(tile_core(tile) == core)
        wait_for(
            number, (lines - 1, lines), main,
            lambda ref: copy(ref, ref, 0, 0, g_send.at[0], g_recv.at[at]).wait_recv(),
        )

    def product(store, start):
        value = lax.dot_general(
            store[...].reshape(lines * length, LANES),
            go_ref[:, :, pl.ds(start, LANES)].reshape(lines * length, LANES),
            (TN, ((), ())),
            preferred_element_type=jnp.float32,
        )
        return value.T

    wait_gated(0)
    for j in range(half * OWN // LANES):
        sums[j * LANES : (j + 1) * LANES, :] = product(main, j * LANES)
    for i in range(half):
        slots[i] = sums[i * OWN : (i + 1) * OWN, :].astype(slots.dtype)

    main_core = tile_core(line)
    column = line - 10 * main_core

    def send_main(k, carry):
        i = lax.rem(k + me, half)
        to = half * core + i
        away = jnp.logical_or(to != me, main_core != core)

        @pl.when(away)
        def _():
            copy(
                slots.at[i], got.at[column, spot], to, main_core, w_send.at[0], w_recv.at[0]
            ).start()

        @pl.when(jnp.logical_not(away))
        def _():
            got[column, spot] = slots[i]

        return carry

    lax.fori_loop(0, half, send_main, 0)

    wait_gated(1)
    first = (5 * quarter) // 2
    for j in range(3):
        more[j * LANES : (j + 1) * LANES, :] = product(
            extra, pl.multiple_of((first + j) * LANES, LANES)
        )
    kept = more[pl.ds(pl.multiple_of(64 * lax.rem(quarter, 2), 64), 16 * OWN), :]
    for i in range(16):
        slots[half + i] = kept[i * OWN : (i + 1) * OWN, :].astype(slots.dtype)

    extra_column = 6 + line // 4

    def send_extra(k, carry):
        i = lax.rem(k + spot, 16)
        to = half * core + 16 * quarter + i
        away = jnp.logical_or(to != me, core != 1)

        @pl.when(away)
        def _():
            copy(
                slots.at[half + i], got.at[extra_column, spot], to, 1, w_send.at[0], w_recv.at[0]
            ).start()

        @pl.when(jnp.logical_not(away))
        def _():
            got[extra_column, spot] = slots[half + i]

        return carry

    lax.fori_loop(0, 16, send_extra, 0)

    at_home = me // half == core
    own_main = one(jnp.logical_and(at_home, main_core == core))
    own_extra = one(
        jnp.logical_and(
            jnp.logical_and(at_home, core == 1), lax.rem(me, half) // 16 == quarter
        )
    )
    total = half + 16
    number = total - own_main - own_extra
    wait_for(
        number, (total - 2, total - 1, total), slots,
        lambda ref: copy(ref, ref, 0, 0, w_send.at[0], w_recv.at[0]).wait_recv(),
    )
    for t in range(10):
        value = got[t, 0].astype(jnp.float32)
        for z in range(1, LINE):
            value = value + got[t, z].astype(jnp.float32)
        out_ref[:, t * LANES : (t + 1) * LANES] = value
    wait_for(
        number, (total - 2, total - 1, total), slots,
        lambda ref: copy(ref, ref, 0, 0, w_send.at[0], w_recv.at[0]).wait_send(),
    )
    for d in range(2):
        same = jnp.logical_and(main_core == core, core == d)
        wait_for(
            jnp.where(core == 0, 10, 6) - one(same), (5, 6, 9, 10), main,
            lambda ref: copy(ref, ref, 0, 0, g_send.at[d], g_recv.at[0]).wait_send(),
        )
        wait_for(
            jnp.where(core == 0, 0, lines - d), (lines - d,), main,
            lambda ref: copy(ref, ref, 0, 0, g_send.at[2 + d], g_recv.at[0]).wait_send(),
        )


def weight_gradient(grad_out, gated, all_go):
    count = lax.axis_size("ctx")
    length, channels = gated.shape
    lines = count // LINE
    half = count // 2
    vmem = pl.BlockSpec(memory_space=pltpu.VMEM)
    return pl.pallas_call(
        functools.partial(weight_kernel, count),
        out_shape=jax.ShapeDtypeStruct((OWN, channels), jnp.float32),
        in_specs=[vmem] * 2,
        out_specs=vmem,
        scratch_shapes=[
            pltpu.VMEM((lines, length, LANES), jnp.bfloat16),
            pltpu.VMEM((lines, length, LANES), jnp.bfloat16),
            pltpu.VMEM((half * OWN, LANES), jnp.float32),
            pltpu.VMEM((3 * LANES, LANES), jnp.float32),
            pltpu.VMEM((half + 16, OWN, LANES), jnp.bfloat16),
            pltpu.VMEM((10, LINE, OWN, LANES), jnp.bfloat16),
            pltpu.SemaphoreType.DMA((4,)),
            pltpu.SemaphoreType.DMA((2,)),
            pltpu.SemaphoreType.DMA((1,)),
            pltpu.SemaphoreType.DMA((1,)),
        ],
        compiler_params=pltpu.CompilerParams(collective_id=1, has_side_effects=True),
        name="weights",
    )(gated, all_go)


def per_device(
    x_raw, bc_raw, gate_branch, dt_raw, conv_x, conv_x_bias, conv_bc, conv_bc_bias, dt_bias, a_log,
    d_skip, out_weight, grad_out,
):
    length, heads = dt_raw.shape
    channels = x_raw.shape[1]
    blocks = lax.axis_size("ctx")
    joined = jnp.concatenate([x_raw[length - 8 :], bc_raw[length - 8 :]], axis=1)
    rim = lax.ppermute(joined, "ctx", [(i, i + 1) for i in range(blocks - 1)])
    step = jax.nn.softplus(dt_raw + dt_bias[None, :])
    rate = -jnp.exp(a_log)
    ld = jnp.cumsum(step * rate[None, :], axis=0)
    ldx = jnp.repeat(ld, HEAD, axis=1)
    stepx = jnp.repeat(step, HEAD, axis=1)
    f, r, prex, gg, prebc = before(
        x_raw, rim[:, :channels], bc_raw, rim[:, channels:], gate_branch, ldx, stepx,
        conv_x, conv_x_bias[None, :], conv_bc, conv_bc_bias[None, :], out_weight, grad_out,
    )
    decays = jnp.exp(ldx[length - 1]).reshape(channels // LANES, 1, LANES)
    half = grad_out.shape[1] // 2
    go = lax.dynamic_slice_in_dim(grad_out, lax.axis_index("tp") * half, half, axis=1)
    s_in, r_in, all_go = scans(f, r, decays, go, blocks)
    wide = lambda a: jnp.pad(a, ((0, 0), (0, LANES - heads)))
    pairs = lambda a: a.T.reshape(heads // 2, 2, length)
    gated, grad_z, gxc, gbc, grad_step = after(
        s_in, r_in, prex, gg, gate_branch, prebc, ldx, stepx,
        jnp.repeat(d_skip, HEAD)[None, :], pairs(ld), pairs(step), wide(ld), wide(step),
        wide(rate[None, :]),
    )
    weight_grad = weight_gradient(grad_out, gated, all_go)
    grad_bc = lax.psum(gbc, "tp")
    grad_bc_conv = (grad_bc * silu_slope(prebc)).astype(jnp.bfloat16)
    grad_dt_raw = grad_step[:, :heads] * jax.nn.sigmoid(dt_raw + dt_bias[None, :])
    return (gxc, grad_bc_conv, grad_z, grad_dt_raw, weight_grad)


def solution(mesh):
    placed = (
        P("ctx", "tp"), P("ctx", None), P("ctx", "tp"), P("ctx", "tp"), P(None, "tp"), P("tp"),
        P(), P(), P("tp"), P("tp"), P("tp"), P("tp", None), P("ctx", None),
    )
    return jax.shard_map(
        per_device,
        mesh=mesh,
        in_specs=placed,
        out_specs=(P("ctx", "tp"), P("ctx", None), P("ctx", "tp"), P("ctx", "tp"), P("ctx", "tp")),
        check_vma=False,
    )
```

```python
import functools

import jax
import jax.numpy as jnp
from jax import lax
from jax.experimental import pallas as pl
from jax.experimental.pallas import tpu as pltpu
from jax.sharding import PartitionSpec as P

KERNEL = 4
HEAD = 64
LANES = 128
ROWS = 16
ROW_TILES = 8
PIECE = 2 * ROWS + 8
PER_LINE = 5
LINE = 8
SIDE = 4
MESH = pl.DeviceIdType.MESH


def dot(a, b, contract):
    return lax.dot_general(
        a,
        b,
        (contract, ((), ())),
        precision=lax.Precision.HIGHEST,
        preferred_element_type=jnp.float32,
    )


NN = ((1,), (0,))
TN = ((0,), (0,))
NT = ((1,), (1,))


def silu_slope(argument):
    gate_value = jax.nn.sigmoid(argument)
    return gate_value * (1.0 + argument * (1.0 - gate_value))


def silu(argument):
    return argument * jax.nn.sigmoid(argument)


def expand(per_head, q):
    row = lax.broadcasted_iota(jnp.int32, (LANES, LANES), 0)
    lane = lax.broadcasted_iota(jnp.int32, (LANES, LANES), 1)
    pick = jnp.where(row == 2 * q + jnp.where(lane < HEAD, 0, 1), 1.0, 0.0)
    return dot(per_head, pick, NN)


def convolve(raw, rim, taps, bias, padded):
    length = raw.shape[0]
    padded[0:8, :] = rim
    padded[8 : 8 + length, :] = raw
    result = jnp.broadcast_to(bias, raw.shape)
    for k in range(KERNEL):
        start = 8 - (KERNEL - 1) + k
        result = result + taps[k : k + 1, :] * padded[start : start + length, :]
    return result


def before_kernel(
    x_ref, rimx_ref, bc_ref, rimbc_ref, gate_ref, ld_ref, step_ref, cx_ref, cxb_ref, cbc_ref,
    cbcb_ref, w_ref, go_ref,
    pieces_ref, prex_ref, gg_ref, prebc_ref,
    padx, padbc, act,
):
    state = bc_ref.shape[1] // 2

    @pl.when(pl.program_id(0) == 0)
    def _():
        pre = convolve(
            bc_ref[...].astype(jnp.float32),
            rimbc_ref[...].astype(jnp.float32),
            cbc_ref[...],
            cbcb_ref[...],
            padbc,
        )
        prebc_ref[...] = pre
        act[...] = silu(pre)

    pre = convolve(
        x_ref[...].astype(jnp.float32),
        rimx_ref[...].astype(jnp.float32),
        cx_ref[...],
        cxb_ref[...],
        padx,
    )
    prex_ref[...] = pre
    b_rows = act[:, :state]
    c_rows = act[:, state:]
    q = pl.program_id(0)
    ld = expand(ld_ref[...], q)
    last = ld[ld.shape[0] - 1 :, :]
    scaled = jnp.exp(last - ld) * expand(step_ref[...], q) * silu(pre)
    split = (ROW_TILES, ROWS, LANES)
    pieces_ref[0, :, :ROWS, :] = dot(b_rows, scaled, TN).reshape(split)
    pieces_ref[0, :, 2 * ROWS :, :] = jnp.broadcast_to(
        jnp.exp(last)[None], (ROW_TILES, 8, LANES)
    )
    gg = lax.dot_general(
        go_ref[...], w_ref[...], (NT, ((), ())), preferred_element_type=jnp.float32
    )
    gg_ref[...] = gg
    grad_y = gg * silu(gate_ref[...].astype(jnp.float32))
    pieces_ref[0, :, ROWS : 2 * ROWS, :] = dot(c_rows, jnp.exp(ld) * grad_y, TN).reshape(split)


def before(x_raw, rimx, bc_raw, rimbc, gate, ld, step, cx, cxb, cbc, cbcb, w, go):
    length, channels = x_raw.shape
    states = bc_raw.shape[1]
    tile = lambda rows: pl.BlockSpec((rows, LANES), lambda q: (0, q))
    whole = lambda a: pl.BlockSpec(a.shape, lambda q: (0, 0))
    f32 = jnp.float32
    return pl.pallas_call(
        before_kernel,
        grid=(channels // LANES,),
        in_specs=[
            tile(length), tile(8), whole(bc_raw), whole(rimbc), tile(length), whole(ld),
            whole(step), tile(KERNEL), tile(1), whole(cbc), whole(cbcb),
            pl.BlockSpec((LANES, w.shape[1]), lambda q: (q, 0)), whole(go),
        ],
        out_specs=[
            pl.BlockSpec((1, ROW_TILES, PIECE, LANES), lambda q: (q, 0, 0, 0)),
            tile(length), tile(length),
            pl.BlockSpec((length, states), lambda q: (0, 0)),
        ],
        out_shape=[
            jax.ShapeDtypeStruct((channels // LANES, ROW_TILES, PIECE, LANES), f32),
            jax.ShapeDtypeStruct((length, channels), f32),
            jax.ShapeDtypeStruct((length, channels), f32),
            jax.ShapeDtypeStruct((length, states), f32),
        ],
        scratch_shapes=[
            pltpu.VMEM((length + 8, LANES), f32),
            pltpu.VMEM((length + 8, states), f32),
            pltpu.VMEM((length, states), f32),
        ],
        name="before",
    )(x_raw, rimx, bc_raw, rimbc, gate, ld, step, cx, cxb, cbc, cbcb, w, go)


def owner_of(tile, row):
    line = lax.rem(tile, 2) * ROW_TILES + row
    spot = lax.rem((LINE * (tile // 2)) // PER_LINE + 2 * line + line // 4, LINE)
    return line * LINE + spot


def piece_of(chip):
    line = chip // LINE
    spot = lax.rem(lax.rem(chip, LINE) + 8 * LINE - 2 * line - line // 4, LINE)
    rank = (PER_LINE * spot + LINE - 1) // LINE
    owns = (LINE * rank) // PER_LINE == spot
    return 2 * rank + line // ROW_TILES, lax.rem(line, ROW_TILES), owns


def scan_kernel(
    count, pieces_ref, go_ref, both_ref, all_ref,
    got, out, send, recv, back_send, back_recv, go_send, go_recv,
):
    me = lax.axis_index("ctx")
    tiles = pieces_ref.shape[0]
    pieces = tiles * ROW_TILES
    barrier = pltpu.get_barrier_semaphore()

    def greet(k, carry):
        pl.semaphore_signal(
            barrier, inc=1, device_id={"ctx": lax.rem(me + k, count)}, device_id_type=MESH
        )
        return carry

    lax.fori_loop(1, count, greet, 0)
    pl.semaphore_wait(barrier, count - 1)

    def copy(src, dst, peer, here, there):
        return pltpu.make_async_remote_copy(
            src_ref=src, dst_ref=dst, send_sem=here, recv_sem=there,
            device_id={"ctx": peer}, device_id_type=MESH,
        )

    def give(k, carry):
        tile = lax.rem(k + me, tiles)
        for j in range(ROW_TILES):
            row = lax.rem(me + j, ROW_TILES)
            owner = owner_of(tile, row)

            @pl.when(owner != me)
            def _():
                copy(
                    pieces_ref.at[tile, row], got.at[me], owner, send.at[0], recv.at[0]
                ).start()

        return carry

    lax.fori_loop(0, tiles, give, 0)

    spot = lax.rem(me, LINE)
    line = me // LINE
    x, y = line // SIDE, lax.rem(line, SIDE)
    middle = go_ref.shape[1] // 2
    early, late = pl.ds(0, middle), pl.ds(middle, middle)
    along_x = [lax.rem(x + d, SIDE) * SIDE + y for d in range(SIDE)]
    along_y = [x * SIDE + lax.rem(y + d, SIDE) for d in range(SIDE)]

    def shift_go(src, dst, to, at):
        copy(src, dst, to * LINE + spot, go_send.at[at], go_recv.at[at]).start()

    all_ref[line] = go_ref[...]
    for d in range(1, SIDE):
        shift_go(go_ref.at[:, early], all_ref.at[line, :, early], along_y[d], 0)
        shift_go(go_ref.at[:, late], all_ref.at[line, :, late], along_x[d], 1)

    def second_go():
        some = all_ref.at[pl.ds(0, SIDE - 1), :, early]
        for at in range(2):
            copy(some, some, 0, go_send.at[at], go_recv.at[at]).wait_recv()
        for d in range(1, SIDE):
            for other in range(SIDE):
                held = all_ref.at[along_y[other], :, early]
                shift_go(held, held, along_x[d], 2)
                held = all_ref.at[along_x[other], :, late]
                shift_go(held, held, along_y[d], 3)

    def finish_go():
        some = all_ref.at[pl.ds(0, SIDE - 1), :, early]
        most = all_ref.at[pl.ds(0, SIDE * (SIDE - 1)), :, early]
        for at in range(2):
            copy(some, some, 0, go_send.at[at], go_recv.at[at]).wait_send()
            copy(most, most, 0, go_send.at[2 + at], go_recv.at[2 + at]).wait()

    own_tile, own_row, owns = piece_of(me)

    @pl.when(owns)
    def _():
        got[me] = pieces_ref[own_tile, own_row]
        some = got.at[pl.ds(0, count - 1)]
        copy(some, some, 0, send.at[0], recv.at[0]).wait_recv()

        def step(k, states):
            forward, backward = states
            for u in range(4):
                at = 4 * k + u
                out[at, :ROWS, :] = forward
                forward = got[at, 2 * ROWS : 2 * ROWS + 1, :] * forward + got[at, :ROWS, :]
                at = count - 1 - at
                out[at, ROWS:, :] = backward
                backward = (
                    got[at, 2 * ROWS : 2 * ROWS + 1, :] * backward + got[at, ROWS : 2 * ROWS, :]
                )
            return forward, backward

        zero = jnp.zeros((ROWS, LANES), jnp.float32)
        lax.fori_loop(0, count // 4, step, (zero, zero))
        both_ref[own_tile, own_row] = out[me]

        def give_back(k, carry):
            peer = lax.rem(me + k, count)
            copy(
                out.at[peer], both_ref.at[own_tile, own_row], peer, back_send.at[0], back_recv.at[0]
            ).start()
            return carry

        lax.fori_loop(1, count, give_back, 0)

    second_go()

    @pl.when(owns)
    def _():
        less = got.at[pl.ds(0, pieces - 1)]
        back = out.at[pl.ds(0, pieces - 1)]
        rest = out.at[pl.ds(0, count - 1)]
        copy(less, less, 0, send.at[0], back_recv.at[0]).wait_send()
        copy(back, back, 0, send.at[0], back_recv.at[0]).wait_recv()
        copy(rest, rest, 0, back_send.at[0], back_recv.at[0]).wait_send()

    @pl.when(jnp.logical_not(owns))
    def _():
        full = got.at[pl.ds(0, pieces)]
        back = out.at[pl.ds(0, pieces)]
        copy(full, full, 0, send.at[0], back_recv.at[0]).wait_send()
        copy(back, back, 0, send.at[0], back_recv.at[0]).wait_recv()

    finish_go()


def scans(pieces, go, count):
    vmem = pl.BlockSpec(memory_space=pltpu.VMEM)
    f32 = jnp.float32
    return pl.pallas_call(
        functools.partial(scan_kernel, count),
        out_shape=[
            jax.ShapeDtypeStruct(pieces.shape[:2] + (2 * ROWS, LANES), f32),
            jax.ShapeDtypeStruct((count // LINE,) + go.shape, go.dtype),
        ],
        in_specs=[vmem] * 2,
        out_specs=[vmem] * 2,
        scratch_shapes=[
            pltpu.VMEM((count, PIECE, LANES), f32),
            pltpu.VMEM((count, 2 * ROWS, LANES), f32),
        ]
        + [pltpu.SemaphoreType.DMA((1,))] * 4
        + [pltpu.SemaphoreType.DMA((4,))] * 2,
        compiler_params=pltpu.CompilerParams(collective_id=0, has_side_effects=True),
        name="scans",
    )(pieces, go)


def after_kernel(
    both_ref, prex_ref, gg_ref, gate_ref, prebc_ref, dskip_ref,
    ldt_ref, stept_ref, ld_ref, step_ref, rate_ref,
    gated_ref, gradz_ref, gxc_ref, gbc_ref, gstep_ref,
    act, scores, shared, grad_b, grad_c, sums, const,
):
    q = pl.program_id(0)
    length = prex_ref.shape[0]
    state = prebc_ref.shape[1] // 2
    rows = lax.broadcasted_iota(jnp.int32, (length, length), 0)
    cols = lax.broadcasted_iota(jnp.int32, (length, length), 1)
    lower = rows >= cols
    lane = lax.broadcasted_iota(jnp.int32, (length, LANES), 1)
    first = lane < HEAD

    @pl.when(q == 0)
    def _():
        act[...] = silu(prebc_ref[...])
        scores[...] = dot(act[:, state:], act[:, :state], NT)
        shared[...] = jnp.zeros_like(shared)
        grad_b[...] = jnp.zeros_like(grad_b)
        grad_c[...] = jnp.zeros_like(grad_c)
        sums[...] = jnp.zeros_like(sums)
        const[...] = jnp.zeros_like(const)

    b_rows = act[:, :state]
    c_rows = act[:, state:]
    pre = prex_ref[...]
    x = silu(pre)
    gate = gate_ref[...].astype(jnp.float32)
    gg = gg_ref[...]
    gate_silu = silu(gate)
    gy = gg * gate_silu
    ld = expand(ld_ref[...], q)
    step = expand(step_ref[...], q)
    grow = jnp.exp(ld)
    last = ld[length - 1 :, :]
    to_end = jnp.exp(last - ld)
    dskip = dskip_ref[...]
    s_in = both_ref[0, :, :ROWS, :].reshape(state, LANES)
    r_in = both_ref[0, :, ROWS:, :].reshape(state, LANES)
    carried = dot(c_rows, s_in, NN)
    carry_b = dot(b_rows, r_in, NN)
    xs = step * x
    withins, grads = [], []
    total = shared[...]
    for a in range(2):
        spread = ld[:, a * HEAD : a * HEAD + 1] - ldt_ref[0, a : a + 1, :]
        decays = jnp.where(lower, jnp.exp(jnp.where(lower, spread, 0.0)), 0.0)
        mixing = decays * scores[...]
        withins.append(dot(mixing, xs, NN))
        grads.append(dot(mixing, gy, TN))
        own = first if a == 0 else jnp.logical_not(first)
        products = dot(jnp.where(own, gy, 0.0), x, NT)
        total = total + decays * products * stept_ref[0, a : a + 1, :]
    shared[...] = total
    within = jnp.where(first, withins[0], withins[1])
    grad0 = jnp.where(first, grads[0], grads[1])
    y = within + grow * carried + dskip * x
    gated_ref[...] = (y * gate_silu).astype(gated_ref.dtype)
    gradz_ref[...] = (gg * y * silu_slope(gate)).astype(gradz_ref.dtype)
    weight = to_end * step
    grad_in = dskip * gy + step * grad0 + weight * carry_b
    gxc_ref[...] = (grad_in * silu_slope(pre)).astype(gxc_ref.dtype)
    grad_b[...] += dot(weight * x, r_in, NT)
    grad_c[...] += dot(grow * gy, s_in, NT)

    def head_sums(value):
        left = jnp.sum(jnp.where(first, value, 0.0), axis=1, keepdims=True)
        right = jnp.sum(jnp.where(first, 0.0, value), axis=1, keepdims=True)
        return jnp.where(lane == 2 * q, left, jnp.where(lane == 2 * q + 1, right, 0.0))

    for k, value in enumerate((gy * within, x * grad0, x * carry_b, gy * carried)):
        sums[k] += head_sums(value)
    const[...] += head_sums(jnp.broadcast_to(jnp.sum(r_in * s_in, axis=0, keepdims=True), x.shape))

    @pl.when(q == pl.num_programs(0) - 1)
    def _():
        ldh = ld_ref[...]
        steph = step_ref[...]
        lasth = ldh[length - 1 :, :]
        to_endh = jnp.exp(lasth - ldh)
        inner, direct, carry_dot, enter = sums[0], sums[1], sums[2], sums[3]
        leaving = to_endh * steph * carry_dot
        grad_log = inner - steph * direct + jnp.exp(ldh) * enter - leaving
        constant = jnp.sum(leaving, axis=0, keepdims=True) + jnp.exp(lasth) * const[0:1, :]
        upper = jnp.where(cols >= rows, 1.0, 0.0)
        grad_rate = dot(upper, grad_log, NN) + constant
        gstep_ref[...] = direct + to_endh * carry_dot + rate_ref[...] * grad_rate
        gbc_ref[:, :state] = grad_b[...] + dot(total, c_rows, TN)
        gbc_ref[:, state:] = grad_c[...] + dot(total, b_rows, NN)


def after(both, prex, gg, gate, prebc, dskipx, ldt, stept, ld, step, rate):
    length, channels = prex.shape
    state = prebc.shape[1] // 2
    tile = lambda rows: pl.BlockSpec((rows, LANES), lambda q: (0, q))
    whole = lambda a: pl.BlockSpec(a.shape, lambda q: (0, 0))
    pair = pl.BlockSpec((1, 2, length), lambda q: (q, 0, 0))
    f32 = jnp.float32
    return pl.pallas_call(
        after_kernel,
        grid=(channels // LANES,),
        in_specs=[
            pl.BlockSpec((1, ROW_TILES, 2 * ROWS, LANES), lambda q: (q, 0, 0, 0)),
            tile(length), tile(length), tile(length), whole(prebc), tile(1), pair, pair, whole(ld), whole(step), whole(rate),
        ],
        out_specs=[
            tile(length), tile(length), tile(length),
            pl.BlockSpec((length, 2 * state), lambda q: (0, 0)),
            pl.BlockSpec((length, LANES), lambda q: (0, 0)),
        ],
        out_shape=[
            jax.ShapeDtypeStruct((length, channels), jnp.bfloat16),
            jax.ShapeDtypeStruct((length, channels), jnp.bfloat16),
            jax.ShapeDtypeStruct((length, channels), jnp.bfloat16),
            jax.ShapeDtypeStruct((length, 2 * state), f32),
            jax.ShapeDtypeStruct((length, LANES), f32),
        ],
        scratch_shapes=[
            pltpu.VMEM((length, 2 * state), f32),
            pltpu.VMEM((length, length), f32),
            pltpu.VMEM((length, length), f32),
            pltpu.VMEM((length, state), f32),
            pltpu.VMEM((length, state), f32),
            pltpu.VMEM((4, length, LANES), f32),
            pltpu.VMEM((length, LANES), f32),
        ],
        name="after",
    )(both, prex, gg, gate, prebc, dskipx, ldt, stept, ld, step, rate)


OWN = 20


def tile_core(tile):
    return tile // 10


def weight_kernel(
    count, gated_ref, go_ref, gbc_ref, prebc_ref, out_ref, bc_ref,
    main, extra, sums, more, slots, got, other, g_send, g_recv, w_send, w_recv, bc_send, bc_recv,
):
    me = lax.axis_index("ctx")
    core = lax.axis_index("tp")
    line, spot = me // LINE, lax.rem(me, LINE)
    lines = count // LINE
    half = count // 2
    length = gated_ref.shape[0]
    quarter = lax.rem(line, 4)
    barrier = pltpu.get_barrier_semaphore()

    def greet(k, carry):
        peer = lax.rem(me + k, count)
        for d in range(2):

            @pl.when(jnp.logical_or(k > 0, core != d))
            def _():
                pl.semaphore_signal(
                    barrier, inc=1, device_id={"ctx": peer, "tp": d}, device_id_type=MESH
                )

        return carry

    lax.fori_loop(0, count, greet, 0)
    pl.semaphore_wait(barrier, 2 * count - 1)

    def copy(src, dst, chip, d, here, there):
        return pltpu.make_async_remote_copy(
            src_ref=src, dst_ref=dst, send_sem=here, recv_sem=there,
            device_id={"ctx": chip, "tp": d}, device_id_type=MESH,
        )

    def lanes(tile):
        return pl.ds(pl.multiple_of((tile - 10 * core) * LANES, LANES), LANES)

    def give(k, carry):
        to = lax.rem(line + k, lines)
        chip = to * LINE + spot
        for d in range(2):
            away = jnp.logical_or(to != line, core != d)
            for at, tile, store in ((0, to, main), (1, 16 + to // 4, extra)):
                mine = tile_core(tile) == core

                @pl.when(jnp.logical_and(mine, away))
                def _():
                    copy(
                        gated_ref.at[:, lanes(tile)], store.at[line], chip, d,
                        g_send.at[2 * at + d], g_recv.at[at],
                    ).start()

                @pl.when(jnp.logical_and(mine, jnp.logical_not(away)))
                def _():
                    store[line] = gated_ref[:, lanes(tile)]

        return carry

    lax.fori_loop(0, lines, give, 0)
    swap = copy(gbc_ref, other, me, 1 - core, bc_send.at[0], bc_recv.at[0])
    swap.start()

    def wait_for(number, options, ref, act):
        for n in options:

            @pl.when(number == n)
            def _():
                act(ref.at[pl.ds(0, n)])

    one = lambda flag: jnp.where(flag, 1, 0)

    def wait_gated(at):
        tile = line if at == 0 else 16 + line // 4
        number = lines - one(tile_core(tile) == core)
        wait_for(
            number, (lines - 1, lines), main,
            lambda ref: copy(ref, ref, 0, 0, g_send.at[0], g_recv.at[at]).wait_recv(),
        )

    def product(store, start):
        value = lax.dot_general(
            store[...].reshape(lines * length, LANES),
            go_ref[:, :, pl.ds(start, LANES)].reshape(lines * length, LANES),
            (TN, ((), ())),
            preferred_element_type=jnp.float32,
        )
        return value.T

    wait_gated(0)
    for j in range(half * OWN // LANES):
        sums[j * LANES : (j + 1) * LANES, :] = product(main, j * LANES)
    for i in range(half):
        slots[i] = sums[i * OWN : (i + 1) * OWN, :].astype(slots.dtype)

    main_core = tile_core(line)
    column = line - 10 * main_core

    def send_main(k, carry):
        i = lax.rem(k + me, half)
        to = half * core + i
        away = jnp.logical_or(to != me, main_core != core)

        @pl.when(away)
        def _():
            copy(
                slots.at[i], got.at[column, spot], to, main_core, w_send.at[0], w_recv.at[0]
            ).start()

        @pl.when(jnp.logical_not(away))
        def _():
            got[column, spot] = slots[i]

        return carry

    lax.fori_loop(0, half, send_main, 0)

    swap.wait()
    bc_ref[...] = ((gbc_ref[...] + other[...]) * silu_slope(prebc_ref[...])).astype(bc_ref.dtype)

    wait_gated(1)
    first = (5 * quarter) // 2
    for j in range(3):
        more[j * LANES : (j + 1) * LANES, :] = product(
            extra, pl.multiple_of((first + j) * LANES, LANES)
        )
    kept = more[pl.ds(pl.multiple_of(64 * lax.rem(quarter, 2), 64), 16 * OWN), :]
    for i in range(16):
        slots[half + i] = kept[i * OWN : (i + 1) * OWN, :].astype(slots.dtype)

    extra_column = 6 + line // 4

    def send_extra(k, carry):
        i = lax.rem(k + spot, 16)
        to = half * core + 16 * quarter + i
        away = jnp.logical_or(to != me, core != 1)

        @pl.when(away)
        def _():
            copy(
                slots.at[half + i], got.at[extra_column, spot], to, 1, w_send.at[0], w_recv.at[0]
            ).start()

        @pl.when(jnp.logical_not(away))
        def _():
            got[extra_column, spot] = slots[half + i]

        return carry

    lax.fori_loop(0, 16, send_extra, 0)

    at_home = me // half == core
    own_main = one(jnp.logical_and(at_home, main_core == core))
    own_extra = one(
        jnp.logical_and(
            jnp.logical_and(at_home, core == 1), lax.rem(me, half) // 16 == quarter
        )
    )
    total = half + 16
    number = total - own_main - own_extra
    wait_for(
        number, (total - 2, total - 1, total), slots,
        lambda ref: copy(ref, ref, 0, 0, w_send.at[0], w_recv.at[0]).wait_recv(),
    )
    for t in range(10):
        value = got[t, 0].astype(jnp.float32)
        for z in range(1, LINE):
            value = value + got[t, z].astype(jnp.float32)
        out_ref[:, t * LANES : (t + 1) * LANES] = value
    wait_for(
        number, (total - 2, total - 1, total), slots,
        lambda ref: copy(ref, ref, 0, 0, w_send.at[0], w_recv.at[0]).wait_send(),
    )
    for d in range(2):
        same = jnp.logical_and(main_core == core, core == d)
        wait_for(
            jnp.where(core == 0, 10, 6) - one(same), (5, 6, 9, 10), main,
            lambda ref: copy(ref, ref, 0, 0, g_send.at[d], g_recv.at[0]).wait_send(),
        )
        wait_for(
            jnp.where(core == 0, 0, lines - d), (lines - d,), main,
            lambda ref: copy(ref, ref, 0, 0, g_send.at[2 + d], g_recv.at[0]).wait_send(),
        )


def weight_gradient(gated, all_go, gbc, prebc):
    count = lax.axis_size("ctx")
    length, channels = gated.shape
    lines = count // LINE
    half = count // 2
    vmem = pl.BlockSpec(memory_space=pltpu.VMEM)
    return pl.pallas_call(
        functools.partial(weight_kernel, count),
        out_shape=[
            jax.ShapeDtypeStruct((OWN, channels), jnp.float32),
            jax.ShapeDtypeStruct(gbc.shape, jnp.bfloat16),
        ],
        in_specs=[vmem] * 4,
        out_specs=[vmem] * 2,
        scratch_shapes=[
            pltpu.VMEM((lines, length, LANES), jnp.bfloat16),
            pltpu.VMEM((lines, length, LANES), jnp.bfloat16),
            pltpu.VMEM((half * OWN, LANES), jnp.float32),
            pltpu.VMEM((3 * LANES, LANES), jnp.float32),
            pltpu.VMEM((half + 16, OWN, LANES), jnp.bfloat16),
            pltpu.VMEM((10, LINE, OWN, LANES), jnp.bfloat16),
            pltpu.VMEM(gbc.shape, jnp.float32),
            pltpu.SemaphoreType.DMA((4,)),
            pltpu.SemaphoreType.DMA((2,)),
        ]
        + [pltpu.SemaphoreType.DMA((1,))] * 4,
        compiler_params=pltpu.CompilerParams(collective_id=1, has_side_effects=True),
        name="weights",
    )(gated, all_go, gbc, prebc)


def per_device(
    x_raw, bc_raw, gate_branch, dt_raw, conv_x, conv_x_bias, conv_bc, conv_bc_bias, dt_bias, a_log,
    d_skip, out_weight, grad_out,
):
    length, heads = dt_raw.shape
    channels = x_raw.shape[1]
    blocks = lax.axis_size("ctx")
    joined = jnp.concatenate([x_raw[length - 8 :], bc_raw[length - 8 :]], axis=1)
    rim = lax.ppermute(joined, "ctx", [(i, i + 1) for i in range(blocks - 1)])
    step = jax.nn.softplus(dt_raw + dt_bias[None, :])
    rate = -jnp.exp(a_log)
    ld = jnp.cumsum(step * rate[None, :], axis=0)
    wide = lambda a: jnp.pad(a, ((0, 0), (0, LANES - heads)))
    pairs = lambda a: a.T.reshape(heads // 2, 2, length)
    half = grad_out.shape[1] // 2
    go = lax.dynamic_slice_in_dim(grad_out, lax.axis_index("tp") * half, half, axis=1)
    pieces, prex, gg, prebc = before(
        x_raw, rim[:, :channels], bc_raw, rim[:, channels:], gate_branch, wide(ld), wide(step),
        conv_x, conv_x_bias[None, :], conv_bc, conv_bc_bias[None, :], out_weight, grad_out,
    )
    both, all_go = scans(pieces, go, blocks)
    gated, grad_z, gxc, gbc, grad_step = after(
        both, prex, gg, gate_branch, prebc, jnp.repeat(d_skip, HEAD)[None, :],
        pairs(ld), pairs(step), wide(ld), wide(step), wide(rate[None, :]),
    )
    weight_grad, grad_bc_conv = weight_gradient(gated, all_go, gbc, prebc)
    grad_dt_raw = grad_step[:, :heads] * jax.nn.sigmoid(dt_raw + dt_bias[None, :])
    return (gxc, grad_bc_conv, grad_z, grad_dt_raw, weight_grad)


def solution(mesh):
    placed = (
        P("ctx", "tp"), P("ctx", None), P("ctx", "tp"), P("ctx", "tp"), P(None, "tp"), P("tp"),
        P(), P(), P("tp"), P("tp"), P("tp"), P("tp", None), P("ctx", None),
    )
    return jax.shard_map(
        per_device,
        mesh=mesh,
        in_specs=placed,
        out_specs=(P("ctx", "tp"), P("ctx", None), P("ctx", "tp"), P("ctx", "tp"), P("ctx", "tp")),
        check_vma=False,
    )
```

```python
import functools

import jax
import jax.numpy as jnp
from jax import lax
from jax.experimental import pallas as pl
from jax.experimental.pallas import tpu as pltpu
from jax.sharding import PartitionSpec as P

KERNEL = 4
HEAD = 64
LANES = 128
ROWS = 16
ROW_TILES = 8
PER_LINE = 5
LINE = 8
SIDE = 4
MESH = pl.DeviceIdType.MESH


def dot(a, b, contract):
    return lax.dot_general(
        a,
        b,
        (contract, ((), ())),
        precision=lax.Precision.HIGHEST,
        preferred_element_type=jnp.float32,
    )


NN = ((1,), (0,))
TN = ((0,), (0,))
NT = ((1,), (1,))


def silu_slope(argument):
    gate_value = jax.nn.sigmoid(argument)
    return gate_value * (1.0 + argument * (1.0 - gate_value))


def silu(argument):
    return argument * jax.nn.sigmoid(argument)


def expand(per_head, q):
    row = lax.broadcasted_iota(jnp.int32, (LANES, LANES), 0)
    lane = lax.broadcasted_iota(jnp.int32, (LANES, LANES), 1)
    pick = jnp.where(row == 2 * q + jnp.where(lane < HEAD, 0, 1), 1.0, 0.0)
    return dot(per_head, pick, NN)


def convolve(raw, rim, taps, bias, padded):
    length = raw.shape[0]
    padded[0:8, :] = rim
    padded[8 : 8 + length, :] = raw
    result = jnp.broadcast_to(bias, raw.shape)
    for k in range(KERNEL):
        start = 8 - (KERNEL - 1) + k
        result = result + taps[k : k + 1, :] * padded[start : start + length, :]
    return result


def before_kernel(
    x_ref, rimx_ref, bc_ref, rimbc_ref, gate_ref, ld_ref, step_ref, cx_ref, cxb_ref, cbc_ref,
    cbcb_ref, w_ref, go_ref,
    f_ref, r_ref, decay_ref, prex_ref, gg_ref, prebc_ref,
    padx, padbc, act,
):
    state = bc_ref.shape[1] // 2

    @pl.when(pl.program_id(0) == 0)
    def _():
        pre = convolve(
            bc_ref[...].astype(jnp.float32),
            rimbc_ref[...].astype(jnp.float32),
            cbc_ref[...],
            cbcb_ref[...],
            padbc,
        )
        prebc_ref[...] = pre
        act[...] = silu(pre)

    pre = convolve(
        x_ref[...].astype(jnp.float32),
        rimx_ref[...].astype(jnp.float32),
        cx_ref[...],
        cxb_ref[...],
        padx,
    )
    prex_ref[...] = pre
    b_rows = act[:, :state]
    c_rows = act[:, state:]
    q = pl.program_id(0)
    ld = expand(ld_ref[...], q)
    last = ld[ld.shape[0] - 1 :, :]
    scaled = jnp.exp(last - ld) * expand(step_ref[...], q) * silu(pre)
    split = (ROW_TILES, ROWS, LANES)
    f_ref[0] = dot(b_rows, scaled, TN).reshape(split)
    decay_ref[0] = jnp.exp(last)
    gg = lax.dot_general(
        go_ref[...], w_ref[...], (NT, ((), ())), preferred_element_type=jnp.float32
    )
    gg_ref[...] = gg
    grad_y = gg * silu(gate_ref[...].astype(jnp.float32))
    r_ref[0] = dot(c_rows, jnp.exp(ld) * grad_y, TN).reshape(split)


def before(x_raw, rimx, bc_raw, rimbc, gate, ld, step, cx, cxb, cbc, cbcb, w, go):
    length, channels = x_raw.shape
    states = bc_raw.shape[1]
    tile = lambda rows: pl.BlockSpec((rows, LANES), lambda q: (0, q))
    whole = lambda a: pl.BlockSpec(a.shape, lambda q: (0, 0))
    f32 = jnp.float32
    return pl.pallas_call(
        before_kernel,
        grid=(channels // LANES,),
        in_specs=[
            tile(length), tile(8), whole(bc_raw), whole(rimbc), tile(length), whole(ld),
            whole(step), tile(KERNEL), tile(1), whole(cbc), whole(cbcb),
            pl.BlockSpec((LANES, w.shape[1]), lambda q: (q, 0)), whole(go),
        ],
        out_specs=[
            pl.BlockSpec((1, ROW_TILES, ROWS, LANES), lambda q: (q, 0, 0, 0)),
            pl.BlockSpec((1, ROW_TILES, ROWS, LANES), lambda q: (q, 0, 0, 0)),
            pl.BlockSpec((1, 1, LANES), lambda q: (q, 0, 0)),
            tile(length), tile(length),
            pl.BlockSpec((length, states), lambda q: (0, 0)),
        ],
        out_shape=[
            jax.ShapeDtypeStruct((channels // LANES, ROW_TILES, ROWS, LANES), f32),
            jax.ShapeDtypeStruct((channels // LANES, ROW_TILES, ROWS, LANES), f32),
            jax.ShapeDtypeStruct((channels // LANES, 1, LANES), f32),
            jax.ShapeDtypeStruct((length, channels), f32),
            jax.ShapeDtypeStruct((length, channels), f32),
            jax.ShapeDtypeStruct((length, states), f32),
        ],
        scratch_shapes=[
            pltpu.VMEM((length + 8, LANES), f32),
            pltpu.VMEM((length + 8, states), f32),
            pltpu.VMEM((length, states), f32),
        ],
        name="before",
    )(x_raw, rimx, bc_raw, rimbc, gate, ld, step, cx, cxb, cbc, cbcb, w, go)


OWN = 20


def owner_of(tile, row, shift):
    line = lax.rem(tile, 2) * ROW_TILES + row
    spot = lax.rem((LINE * (tile // 2)) // PER_LINE + shift + 2 * line + line // 4, LINE)
    return line * LINE + spot


def piece_of(chip, shift):
    line = chip // LINE
    spot = lax.rem(lax.rem(chip, LINE) + 8 * LINE - shift - 2 * line - line // 4, LINE)
    rank = (PER_LINE * spot + LINE - 1) // LINE
    owns = (LINE * rank) // PER_LINE == spot
    return 2 * rank + line // ROW_TILES, lax.rem(line, ROW_TILES), owns


def tile_core(tile):
    return tile // 10


def main_kernel(
    count, f_ref, r_ref, decay_ref, go_ref, prex_ref, gg_ref, gate_ref, prebc_ref, dskip_ref,
    ldt_ref, stept_ref, ld_ref, step_ref, rate_ref,
    out_ref, bc_ref, gradz_ref, gxc_ref, gstep_ref,
    got_f, got_r, back_f, back_r, decay_f, decay_r, sin, rin, all_ref, ldx, stepx, within, grad0,
    gated_ref, act, scores, shared, grad_b, grad_c, heads, const, gbc, other,
    main, extra, sums, more, slots, got,
    send, recv, back_send, back_recv, decay_send, decay_recv, go_send, go_recv,
    g_send, g_recv, w_send, w_recv, bc_send, bc_recv,
):
    me = lax.axis_index("ctx")
    core = lax.axis_index("tp")
    line, spot = me // LINE, lax.rem(me, LINE)
    lines = count // LINE
    half = count // 2
    length = prex_ref.shape[0]
    state = prebc_ref.shape[1] // 2
    tiles = f_ref.shape[0]
    pieces = tiles * ROW_TILES
    quarter = lax.rem(line, 4)
    barrier = pltpu.get_barrier_semaphore()

    def greet(k, carry):
        peer = lax.rem(me + k, count)
        for d in range(2):

            @pl.when(jnp.logical_or(k > 0, core != d))
            def _():
                pl.semaphore_signal(
                    barrier, inc=1, device_id={"ctx": peer, "tp": d}, device_id_type=MESH
                )

        return carry

    lax.fori_loop(0, count, greet, 0)

    def copy(src, dst, peer, here, there):
        return pltpu.make_async_remote_copy(
            src_ref=src, dst_ref=dst, send_sem=here, recv_sem=there,
            device_id={"ctx": peer}, device_id_type=MESH,
        )

    def across(src, dst, chip, d, here, there):
        return pltpu.make_async_remote_copy(
            src_ref=src, dst_ref=dst, send_sem=here, recv_sem=there,
            device_id={"ctx": chip, "tp": d}, device_id_type=MESH,
        )

    sets = (
        (0, f_ref, decay_f, sin, got_f, back_f, False),
        (1, r_ref, decay_r, rin, got_r, back_r, True),
    )

    def give_all(which):
        _, src, decay, dst, arrived, back, reverse = sets[which]

        def give(k, carry):
            tile = lax.rem(k + me, tiles)
            for j in range(ROW_TILES):
                row = lax.rem(me + j, ROW_TILES)
                owner = owner_of(tile, row, which)

                @pl.when(owner != me)
                def _():
                    copy(
                        src.at[tile, row], arrived.at[me], owner, send.at[which], recv.at[which]
                    ).start()
                    copy(
                        decay_ref.at[tile], decay.at[me], owner,
                        decay_send.at[which], decay_recv.at[which],
                    ).start()

            return carry

        lax.fori_loop(0, tiles, give, 0)

    def scan(which):
        _, src, decay, dst, arrived, back, reverse = sets[which]
        own_tile, own_row, owns = piece_of(me, which)

        @pl.when(owns)
        def _():
            arrived[me] = src[own_tile, own_row]
            decay[me] = decay_ref[own_tile]
            some = arrived.at[pl.ds(0, count - 1)]
            copy(some, some, 0, send.at[which], recv.at[which]).wait_recv()
            some = decay.at[pl.ds(0, count - 1)]
            copy(some, some, 0, decay_send.at[which], decay_recv.at[which]).wait_recv()

            def step(k, value):
                for u in range(4):
                    at = 4 * k + u
                    at = count - 1 - at if reverse else at
                    back[at] = value
                    value = decay[at] * value + arrived[at]
                return value

            lax.fori_loop(0, count // 4, step, jnp.zeros((ROWS, LANES), jnp.float32))
            dst[own_tile, own_row] = back[me]

            def give_back(k, carry):
                peer = lax.rem(me + k, count)
                copy(
                    back.at[peer], dst.at[own_tile, own_row], peer,
                    back_send.at[which], back_recv.at[which],
                ).start()
                return carry

            lax.fori_loop(1, count, give_back, 0)

    def wait_back(which):
        _, src, decay, dst, arrived, back, reverse = sets[which]
        own_tile, own_row, owns = piece_of(me, which)
        for flag, number in ((owns, pieces - 1), (jnp.logical_not(owns), pieces)):

            @pl.when(flag)
            def _():
                some = arrived.at[pl.ds(0, number)]
                copy(some, some, 0, send.at[which], back_recv.at[which]).wait_recv()

    def finish_scan(which):
        _, src, decay, dst, arrived, back, reverse = sets[which]
        own_tile, own_row, owns = piece_of(me, which)
        for flag, number in ((owns, pieces - 1), (jnp.logical_not(owns), pieces)):

            @pl.when(flag)
            def _():
                some = arrived.at[pl.ds(0, number)]
                few = decay.at[pl.ds(0, number)]
                copy(some, some, 0, send.at[which], back_recv.at[which]).wait_send()
                copy(few, few, 0, decay_send.at[which], decay_recv.at[which]).wait_send()

        @pl.when(owns)
        def _():
            rest = back.at[pl.ds(0, count - 1)]
            copy(rest, rest, 0, back_send.at[which], back_recv.at[which]).wait_send()

    x_at, y_at = line // SIDE, lax.rem(line, SIDE)
    middle = go_ref.shape[1] // 2
    early, late = pl.ds(0, middle), pl.ds(middle, middle)
    along_x = [lax.rem(x_at + d, SIDE) * SIDE + y_at for d in range(SIDE)]
    along_y = [x_at * SIDE + lax.rem(y_at + d, SIDE) for d in range(SIDE)]

    def shift_go(src, dst, to, at):
        copy(src, dst, to * LINE + spot, go_send.at[at], go_recv.at[at]).start()

    def first_go():
        all_ref[line] = go_ref[...]
        for d in range(1, SIDE):
            shift_go(go_ref.at[:, early], all_ref.at[line, :, early], along_y[d], 0)
            shift_go(go_ref.at[:, late], all_ref.at[line, :, late], along_x[d], 1)

    def second_go():
        some = all_ref.at[pl.ds(0, SIDE - 1), :, early]
        for at in range(2):
            copy(some, some, 0, go_send.at[at], go_recv.at[at]).wait_recv()
        for d in range(1, SIDE):
            for k in range(SIDE):
                held = all_ref.at[along_y[k], :, early]
                shift_go(held, held, along_x[d], 2)
                held = all_ref.at[along_x[k], :, late]
                shift_go(held, held, along_y[d], 3)

    def finish_go():
        some = all_ref.at[pl.ds(0, SIDE - 1), :, early]
        most = all_ref.at[pl.ds(0, SIDE * (SIDE - 1)), :, early]
        for at in range(2):
            copy(some, some, 0, go_send.at[at], go_recv.at[at]).wait_send()
            copy(most, most, 0, go_send.at[2 + at], go_recv.at[2 + at]).wait()

    pl.semaphore_wait(barrier, 2 * count - 1)
    give_all(0)
    first_go()
    give_all(1)

    row_at = lax.broadcasted_iota(jnp.int32, (length, length), 0)
    col_at = lax.broadcasted_iota(jnp.int32, (length, length), 1)
    lower = row_at >= col_at
    lane = lax.broadcasted_iota(jnp.int32, (length, LANES), 1)
    first = lane < HEAD
    act[...] = silu(prebc_ref[...])
    b_rows = act.at[:, :state]
    c_rows = act.at[:, state:]
    scores[...] = dot(c_rows[...], b_rows[...], NT)
    for ref in (shared, grad_b, grad_c, heads, const):
        ref[...] = jnp.zeros_like(ref)

    def tile_of(q):
        return (slice(None), pl.ds(pl.multiple_of(q * LANES, LANES), LANES))

    def inside(q, carry):
        at = tile_of(q)
        x = silu(prex_ref[at])
        gy = gg_ref[at] * silu(gate_ref[at].astype(jnp.float32))
        ld = expand(ld_ref[...], q)
        step = expand(step_ref[...], q)
        ldx[at] = ld
        stepx[at] = step
        xs = step * x
        ldt, stept = ldt_ref[q], stept_ref[q]
        parts, grads = [], []
        total = shared[...]
        for a in range(2):
            spread = ld[:, a * HEAD : a * HEAD + 1] - ldt[a : a + 1, :]
            decays = jnp.where(lower, jnp.exp(jnp.where(lower, spread, 0.0)), 0.0)
            mixing = decays * scores[...]
            parts.append(dot(mixing, xs, NN))
            grads.append(dot(mixing, gy, TN))
            own = first if a == 0 else jnp.logical_not(first)
            products = dot(jnp.where(own, gy, 0.0), x, NT)
            total = total + decays * products * stept[a : a + 1, :]
        shared[...] = total
        within[at] = jnp.where(first, parts[0], parts[1])
        grad0[at] = jnp.where(first, grads[0], grads[1])
        return carry

    lax.fori_loop(0, tiles, inside, 0)

    def head_sums(value, q):
        left = jnp.sum(jnp.where(first, value, 0.0), axis=1, keepdims=True)
        right = jnp.sum(jnp.where(first, 0.0, value), axis=1, keepdims=True)
        return jnp.where(lane == 2 * q, left, jnp.where(lane == 2 * q + 1, right, 0.0))

    scan(0)
    second_go()
    scan(1)
    wait_back(0)

    def outputs(q, carry):
        at = tile_of(q)
        gate = gate_ref[at].astype(jnp.float32)
        gate_silu = silu(gate)
        gg = gg_ref[at]
        grow = jnp.exp(ldx[at])
        carried = dot(c_rows[...], sin[q].reshape(state, LANES), NN)
        y = within[at] + grow * carried + dskip_ref[at] * silu(prex_ref[at])
        gated_ref[at] = (y * gate_silu).astype(gated_ref.dtype)
        gradz_ref[at] = (gg * y * silu_slope(gate)).astype(gradz_ref.dtype)
        heads[3] += head_sums(gg * gate_silu * carried, q)
        return carry

    lax.fori_loop(0, tiles, outputs, 0)

    def lanes(tile):
        return pl.ds(pl.multiple_of((tile - 10 * core) * LANES, LANES), LANES)

    def give_gated(k, carry):
        to = lax.rem(line + k, lines)
        chip = to * LINE + spot
        for d in range(2):
            away = jnp.logical_or(to != line, core != d)
            for at, tile, store in ((0, to, main), (1, 16 + to // 4, extra)):
                mine = tile_core(tile) == core

                @pl.when(jnp.logical_and(mine, away))
                def _():
                    across(
                        gated_ref.at[:, lanes(tile)], store.at[line], chip, d,
                        g_send.at[2 * at + d], g_recv.at[at],
                    ).start()

                @pl.when(jnp.logical_and(mine, jnp.logical_not(away)))
                def _():
                    store[line] = gated_ref[:, lanes(tile)]

        return carry

    lax.fori_loop(0, lines, give_gated, 0)

    def wait_for(number, options, ref, act_on):
        for n in options:

            @pl.when(number == n)
            def _():
                act_on(ref.at[pl.ds(0, n)])

    one = lambda flag: jnp.where(flag, 1, 0)

    def wait_gated(at):
        tile = line if at == 0 else 16 + line // 4
        number = lines - one(tile_core(tile) == core)
        wait_for(
            number, (lines - 1, lines), main,
            lambda ref: across(ref, ref, 0, 0, g_send.at[0], g_recv.at[at]).wait_recv(),
        )

    wait_gated(0)
    wait_gated(1)
    finish_go()

    def product(store, start):
        value = lax.dot_general(
            store[...].reshape(lines * length, LANES),
            all_ref[:, :, pl.ds(start, LANES)].reshape(lines * length, LANES),
            (TN, ((), ())),
            preferred_element_type=jnp.float32,
        )
        return value.T

    for j in range(half * OWN // LANES):
        sums[j * LANES : (j + 1) * LANES, :] = product(main, j * LANES)
    for i in range(half):
        slots[i] = sums[i * OWN : (i + 1) * OWN, :].astype(slots.dtype)

    main_core = tile_core(line)
    column = line - 10 * main_core

    def send_main(k, carry):
        i = lax.rem(k + me, half)
        to = half * core + i
        away = jnp.logical_or(to != me, main_core != core)

        @pl.when(away)
        def _():
            across(
                slots.at[i], got.at[column, spot], to, main_core, w_send.at[0], w_recv.at[0]
            ).start()

        @pl.when(jnp.logical_not(away))
        def _():
            got[column, spot] = slots[i]

        return carry

    lax.fori_loop(0, half, send_main, 0)

    first_tile = (5 * quarter) // 2
    for j in range(3):
        more[j * LANES : (j + 1) * LANES, :] = product(
            extra, pl.multiple_of((first_tile + j) * LANES, LANES)
        )
    kept = more[pl.ds(pl.multiple_of(64 * lax.rem(quarter, 2), 64), 16 * OWN), :]
    for i in range(16):
        slots[half + i] = kept[i * OWN : (i + 1) * OWN, :].astype(slots.dtype)

    extra_column = 6 + line // 4

    def send_extra(k, carry):
        i = lax.rem(k + spot, 16)
        to = half * core + 16 * quarter + i
        away = jnp.logical_or(to != me, core != 1)

        @pl.when(away)
        def _():
            across(
                slots.at[half + i], got.at[extra_column, spot], to, 1, w_send.at[0], w_recv.at[0]
            ).start()

        @pl.when(jnp.logical_not(away))
        def _():
            got[extra_column, spot] = slots[half + i]

        return carry

    lax.fori_loop(0, 16, send_extra, 0)

    wait_back(1)

    def gradients(q, carry):
        at = tile_of(q)
        pre = prex_ref[at]
        x = silu(pre)
        gy = gg_ref[at] * silu(gate_ref[at].astype(jnp.float32))
        ld = ldx[at]
        step = stepx[at]
        weight = jnp.exp(ld[length - 1 :, :] - ld) * step
        s_in = sin[q].reshape(state, LANES)
        r_in = rin[q].reshape(state, LANES)
        carry_b = dot(b_rows[...], r_in, NN)
        inner = grad0[at]
        grad_in = dskip_ref[at] * gy + step * inner + weight * carry_b
        gxc_ref[at] = (grad_in * silu_slope(pre)).astype(gxc_ref.dtype)
        grad_b[...] += dot(weight * x, r_in, NT)
        grad_c[...] += dot(jnp.exp(ld) * gy, s_in, NT)
        heads[0] += head_sums(gy * within[at], q)
        heads[1] += head_sums(x * inner, q)
        heads[2] += head_sums(x * carry_b, q)
        const[...] += head_sums(
            jnp.broadcast_to(jnp.sum(r_in * s_in, axis=0, keepdims=True), x.shape), q
        )
        return carry

    lax.fori_loop(0, tiles, gradients, 0)
    gbc[:, :state] = grad_b[...] + dot(shared[...], c_rows[...], TN)
    gbc[:, state:] = grad_c[...] + dot(shared[...], b_rows[...], NN)
    swap = across(gbc, other, me, 1 - core, bc_send.at[0], bc_recv.at[0])
    swap.start()
    ldh = ld_ref[...]
    steph = step_ref[...]
    lasth = ldh[length - 1 :, :]
    to_endh = jnp.exp(lasth - ldh)
    direct, carry_dot = heads[1], heads[2]
    leaving = to_endh * steph * carry_dot
    grad_log = heads[0] - steph * direct + jnp.exp(ldh) * heads[3] - leaving
    constant = jnp.sum(leaving, axis=0, keepdims=True) + jnp.exp(lasth) * const[0:1, :]
    upper = jnp.where(col_at >= row_at, 1.0, 0.0)
    grad_rate = dot(upper, grad_log, NN) + constant
    gstep_ref[...] = direct + to_endh * carry_dot + rate_ref[...] * grad_rate

    at_home = me // half == core
    own_main = one(jnp.logical_and(at_home, main_core == core))
    own_extra = one(
        jnp.logical_and(
            jnp.logical_and(at_home, core == 1), lax.rem(me, half) // 16 == quarter
        )
    )
    total = half + 16
    number = total - own_main - own_extra
    wait_for(
        number, (total - 2, total - 1, total), slots,
        lambda ref: across(ref, ref, 0, 0, w_send.at[0], w_recv.at[0]).wait_recv(),
    )
    for t in range(10):
        value = got[t, 0].astype(jnp.float32)
        for z in range(1, LINE):
            value = value + got[t, z].astype(jnp.float32)
        out_ref[:, t * LANES : (t + 1) * LANES] = value
    swap.wait()
    bc_ref[...] = ((gbc[...] + other[...]) * silu_slope(prebc_ref[...])).astype(bc_ref.dtype)
    wait_for(
        number, (total - 2, total - 1, total), slots,
        lambda ref: across(ref, ref, 0, 0, w_send.at[0], w_recv.at[0]).wait_send(),
    )
    for d in range(2):
        same = jnp.logical_and(main_core == core, core == d)
        wait_for(
            jnp.where(core == 0, 10, 6) - one(same), (5, 6, 9, 10), main,
            lambda ref: across(ref, ref, 0, 0, g_send.at[d], g_recv.at[0]).wait_send(),
        )
        wait_for(
            jnp.where(core == 0, 0, lines - d), (lines - d,), main,
            lambda ref: across(ref, ref, 0, 0, g_send.at[2 + d], g_recv.at[0]).wait_send(),
        )
    finish_scan(0)
    finish_scan(1)


def main_part(f, r, decay, go, prex, gg, gate, prebc, dskip, ldt, stept, ld, step, rate, count):
    length, channels = prex.shape
    state = prebc.shape[1] // 2
    lines = count // LINE
    half = count // 2
    f32, bf16 = jnp.float32, jnp.bfloat16
    vmem = pl.BlockSpec(memory_space=pltpu.VMEM)
    dma = pltpu.SemaphoreType.DMA
    wide = pltpu.VMEM((length, channels), f32)
    square = pltpu.VMEM((length, LANES), f32)
    return pl.pallas_call(
        functools.partial(main_kernel, count),
        out_shape=[
            jax.ShapeDtypeStruct((OWN, channels), f32),
            jax.ShapeDtypeStruct((length, 2 * state), bf16),
            jax.ShapeDtypeStruct((length, channels), bf16),
            jax.ShapeDtypeStruct((length, channels), bf16),
            jax.ShapeDtypeStruct((length, LANES), f32),
        ],
        in_specs=[vmem] * 14,
        out_specs=[vmem] * 5,
        scratch_shapes=[pltpu.VMEM((count, ROWS, LANES), f32)] * 4
        + [pltpu.VMEM((count, 1, LANES), f32)] * 2
        + [pltpu.VMEM(f.shape, f32)] * 2
        + [pltpu.VMEM((lines,) + go.shape, go.dtype)]
        + [wide] * 4
        + [
            pltpu.VMEM((length, channels), bf16),
            pltpu.VMEM((length, 2 * state), f32),
            square, square, square, square,
            pltpu.VMEM((4, length, LANES), f32),
            square,
            pltpu.VMEM((length, 2 * state), f32),
            pltpu.VMEM((length, 2 * state), f32),
            pltpu.VMEM((lines, length, LANES), bf16),
            pltpu.VMEM((lines, length, LANES), bf16),
            pltpu.VMEM((half * OWN, LANES), f32),
            pltpu.VMEM((3 * LANES, LANES), f32),
            pltpu.VMEM((half + 16, OWN, LANES), bf16),
            pltpu.VMEM((10, LINE, OWN, LANES), bf16),
        ]
        + [dma((2,))] * 6
        + [dma((4,))] * 3
        + [dma((2,))]
        + [dma((1,))] * 4,
        compiler_params=pltpu.CompilerParams(collective_id=0, has_side_effects=True),
        name="main",
    )(f, r, decay, go, prex, gg, gate, prebc, dskip, ldt, stept, ld, step, rate)


def per_device(
    x_raw, bc_raw, gate_branch, dt_raw, conv_x, conv_x_bias, conv_bc, conv_bc_bias, dt_bias, a_log,
    d_skip, out_weight, grad_out,
):
    length, heads = dt_raw.shape
    channels = x_raw.shape[1]
    blocks = lax.axis_size("ctx")
    joined = jnp.concatenate([x_raw[length - 8 :], bc_raw[length - 8 :]], axis=1)
    rim = lax.ppermute(joined, "ctx", [(i, i + 1) for i in range(blocks - 1)])
    step = jax.nn.softplus(dt_raw + dt_bias[None, :])
    rate = -jnp.exp(a_log)
    ld = jnp.cumsum(step * rate[None, :], axis=0)
    wide = lambda a: jnp.pad(a, ((0, 0), (0, LANES - heads)))
    pairs = lambda a: a.T.reshape(heads // 2, 2, length)
    half = grad_out.shape[1] // 2
    go = lax.dynamic_slice_in_dim(grad_out, lax.axis_index("tp") * half, half, axis=1)
    f, r, decay, prex, gg, prebc = before(
        x_raw, rim[:, :channels], bc_raw, rim[:, channels:], gate_branch, wide(ld), wide(step),
        conv_x, conv_x_bias[None, :], conv_bc, conv_bc_bias[None, :], out_weight, grad_out,
    )
    weight_grad, grad_bc_conv, grad_z, gxc, grad_step = main_part(
        f, r, decay, go, prex, gg, gate_branch, prebc, jnp.repeat(d_skip, HEAD)[None, :],
        pairs(ld), pairs(step), wide(ld), wide(step), wide(rate[None, :]), blocks,
    )
    grad_dt_raw = grad_step[:, :heads] * jax.nn.sigmoid(dt_raw + dt_bias[None, :])
    return (gxc, grad_bc_conv, grad_z, grad_dt_raw, weight_grad)


def solution(mesh):
    placed = (
        P("ctx", "tp"), P("ctx", None), P("ctx", "tp"), P("ctx", "tp"), P(None, "tp"), P("tp"),
        P(), P(), P("tp"), P("tp"), P("tp"), P("tp", None), P("ctx", None),
    )
    return jax.shard_map(
        per_device,
        mesh=mesh,
        in_specs=placed,
        out_specs=(P("ctx", "tp"), P("ctx", None), P("ctx", "tp"), P("ctx", "tp"), P("ctx", "tp")),
        check_vma=False,
    )
```

```python
import functools

import jax
import jax.numpy as jnp
from jax import lax
from jax.experimental import pallas as pl
from jax.experimental.pallas import tpu as pltpu
from jax.sharding import PartitionSpec as P

KERNEL = 4
HEAD = 64
LANES = 128
ROWS = 16
ROW_TILES = 8
PER_LINE = 5
LINE = 8
SIDE = 4
MESH = pl.DeviceIdType.MESH


def dot(a, b, contract):
    return lax.dot_general(
        a,
        b,
        (contract, ((), ())),
        precision=lax.Precision.HIGHEST,
        preferred_element_type=jnp.float32,
    )


NN = ((1,), (0,))
TN = ((0,), (0,))
NT = ((1,), (1,))


def silu_slope(argument):
    gate_value = jax.nn.sigmoid(argument)
    return gate_value * (1.0 + argument * (1.0 - gate_value))


def silu(argument):
    return argument * jax.nn.sigmoid(argument)


def expand(per_head, q):
    row = lax.broadcasted_iota(jnp.int32, (LANES, LANES), 0)
    lane = lax.broadcasted_iota(jnp.int32, (LANES, LANES), 1)
    pick = jnp.where(row == 2 * q + jnp.where(lane < HEAD, 0, 1), 1.0, 0.0)
    return dot(per_head, pick, NN)


RIM = 16


def convolve(raw, rim, taps, padded):
    length = raw.shape[0]
    padded[0:RIM, :] = rim
    padded[RIM : RIM + length, :] = raw
    result = jnp.broadcast_to(taps[KERNEL : KERNEL + 1, :], raw.shape)
    for k in range(KERNEL):
        start = RIM - (KERNEL - 1) + k
        result = result + taps[k : k + 1, :] * padded[start : start + length, :]
    return result


OWN = 20


def owner_of(tile, row, shift):
    line = lax.rem(tile, 2) * ROW_TILES + row
    spot = lax.rem((LINE * (tile // 2)) // PER_LINE + shift + 2 * line + line // 4, LINE)
    return line * LINE + spot


def piece_of(chip, shift):
    line = chip // LINE
    spot = lax.rem(lax.rem(chip, LINE) + 8 * LINE - shift - 2 * line - line // 4, LINE)
    rank = (PER_LINE * spot + LINE - 1) // LINE
    owns = (LINE * rank) // PER_LINE == spot
    return 2 * rank + line // ROW_TILES, lax.rem(line, ROW_TILES), owns


def tile_core(tile):
    return tile // 10


def main_kernel(
    count, x_ref, bcraw_ref, gate_ref, dt_ref, head_ref, chan_ref, cbc_ref, weights_ref, go_ref,
    out_ref, bc_ref, gradz_ref, gxc_ref, gstep_ref,
    f_ref, r_ref, decay_ref, prex_ref, gg_ref, prebc_ref, ld_ref, step_ref, ldt_ref, stept_ref,
    rim_x, rim_bc, pad_x, pad_bc,
    got_f, got_r, back_f, back_r, decay_f, decay_r, sin, rin, all_ref, ldx, stepx, within, grad0,
    gated_ref, act, scores, shared, grad_b, grad_c, heads, const, gbc, other,
    main, extra, sums, more, slots, got,
    send, recv, back_send, back_recv, decay_send, decay_recv, go_send, go_recv,
    g_send, g_recv, w_send, w_recv, bc_send, bc_recv, rim_send, rim_recv,
):
    me = lax.axis_index("ctx")
    core = lax.axis_index("tp")
    line, spot = me // LINE, lax.rem(me, LINE)
    lines = count // LINE
    half = count // 2
    length = x_ref.shape[0]
    state = bcraw_ref.shape[1] // 2
    tiles = f_ref.shape[0]
    pieces = tiles * ROW_TILES
    quarter = lax.rem(line, 4)
    barrier = pltpu.get_barrier_semaphore()

    def greet(k, carry):
        peer = lax.rem(me + k, count)
        for d in range(2):

            @pl.when(jnp.logical_or(k > 0, core != d))
            def _():
                pl.semaphore_signal(
                    barrier, inc=1, device_id={"ctx": peer, "tp": d}, device_id_type=MESH
                )

        return carry

    lax.fori_loop(0, count, greet, 0)

    def copy(src, dst, peer, here, there):
        return pltpu.make_async_remote_copy(
            src_ref=src, dst_ref=dst, send_sem=here, recv_sem=there,
            device_id={"ctx": peer}, device_id_type=MESH,
        )

    def across(src, dst, chip, d, here, there):
        return pltpu.make_async_remote_copy(
            src_ref=src, dst_ref=dst, send_sem=here, recv_sem=there,
            device_id={"ctx": chip, "tp": d}, device_id_type=MESH,
        )

    sets = (
        (0, f_ref, decay_f, sin, got_f, back_f, False),
        (1, r_ref, decay_r, rin, got_r, back_r, True),
    )

    def give(which, tile):
        _, src, decay, dst, arrived, back, reverse = sets[which]
        for j in range(ROW_TILES):
            row = lax.rem(me + j, ROW_TILES)
            owner = owner_of(tile, row, which)

            @pl.when(owner != me)
            def _():
                copy(
                    src.at[tile, row], arrived.at[me], owner, send.at[which], recv.at[which]
                ).start()
                copy(
                    decay_ref.at[tile], decay.at[me], owner,
                    decay_send.at[which], decay_recv.at[which],
                ).start()

    def scan(which):
        _, src, decay, dst, arrived, back, reverse = sets[which]
        own_tile, own_row, owns = piece_of(me, which)

        @pl.when(owns)
        def _():
            arrived[me] = src[own_tile, own_row]
            decay[me] = decay_ref[own_tile]
            some = arrived.at[pl.ds(0, count - 1)]
            copy(some, some, 0, send.at[which], recv.at[which]).wait_recv()
            some = decay.at[pl.ds(0, count - 1)]
            copy(some, some, 0, decay_send.at[which], decay_recv.at[which]).wait_recv()

            def step(k, value):
                for u in range(4):
                    at = 4 * k + u
                    at = count - 1 - at if reverse else at
                    back[at] = value
                    value = decay[at] * value + arrived[at]
                return value

            lax.fori_loop(0, count // 4, step, jnp.zeros((ROWS, LANES), jnp.float32))
            dst[own_tile, own_row] = back[me]

            def give_back(k, carry):
                peer = lax.rem(me + k, count)
                copy(
                    back.at[peer], dst.at[own_tile, own_row], peer,
                    back_send.at[which], back_recv.at[which],
                ).start()
                return carry

            lax.fori_loop(1, count, give_back, 0)

    def wait_back(which):
        _, src, decay, dst, arrived, back, reverse = sets[which]
        own_tile, own_row, owns = piece_of(me, which)
        for flag, number in ((owns, pieces - 1), (jnp.logical_not(owns), pieces)):

            @pl.when(flag)
            def _():
                some = arrived.at[pl.ds(0, number)]
                copy(some, some, 0, send.at[which], back_recv.at[which]).wait_recv()

    def finish_scan(which):
        _, src, decay, dst, arrived, back, reverse = sets[which]
        own_tile, own_row, owns = piece_of(me, which)
        for flag, number in ((owns, pieces - 1), (jnp.logical_not(owns), pieces)):

            @pl.when(flag)
            def _():
                some = arrived.at[pl.ds(0, number)]
                few = decay.at[pl.ds(0, number)]
                copy(some, some, 0, send.at[which], back_recv.at[which]).wait_send()
                copy(few, few, 0, decay_send.at[which], decay_recv.at[which]).wait_send()

        @pl.when(owns)
        def _():
            rest = back.at[pl.ds(0, count - 1)]
            copy(rest, rest, 0, back_send.at[which], back_recv.at[which]).wait_send()

    x_at, y_at = line // SIDE, lax.rem(line, SIDE)
    features = go_ref.shape[1] // 2
    middle = features // 2
    early, late = pl.ds(0, middle), pl.ds(middle, middle)
    start_go = pl.multiple_of(core * features, LANES)
    go_early = pl.ds(start_go, middle)
    go_late = pl.ds(pl.multiple_of(core * features + middle, LANES), middle)
    along_x = [lax.rem(x_at + d, SIDE) * SIDE + y_at for d in range(SIDE)]
    along_y = [x_at * SIDE + lax.rem(y_at + d, SIDE) for d in range(SIDE)]

    def shift_go(src, dst, to, at):
        copy(src, dst, to * LINE + spot, go_send.at[at], go_recv.at[at]).start()

    def first_go():
        all_ref[line] = go_ref[:, pl.ds(start_go, features)]
        for d in range(1, SIDE):
            shift_go(go_ref.at[:, go_early], all_ref.at[line, :, early], along_y[d], 0)
            shift_go(go_ref.at[:, go_late], all_ref.at[line, :, late], along_x[d], 1)

    def second_go():
        some = all_ref.at[pl.ds(0, SIDE - 1), :, early]
        for at in range(2):
            copy(some, some, 0, go_send.at[at], go_recv.at[at]).wait_recv()
        for d in range(1, SIDE):
            for k in range(SIDE):
                held = all_ref.at[along_y[k], :, early]
                shift_go(held, held, along_x[d], 2)
                held = all_ref.at[along_x[k], :, late]
                shift_go(held, held, along_y[d], 3)

    def finish_go():
        some = all_ref.at[pl.ds(0, SIDE - 1), :, early]
        most = all_ref.at[pl.ds(0, SIDE * (SIDE - 1)), :, early]
        for at in range(2):
            copy(some, some, 0, go_send.at[at], go_recv.at[at]).wait_send()
            copy(most, most, 0, go_send.at[2 + at], go_recv.at[2 + at]).wait()

    def tile_of(q):
        return (slice(None), pl.ds(pl.multiple_of(q * LANES, LANES), LANES))

    def dskip_of(q):
        return (slice(KERNEL + 1, KERNEL + 2), pl.ds(pl.multiple_of(q * LANES, LANES), LANES))

    def gated_gradient(q, carry):
        rows = pl.ds(pl.multiple_of(q * LANES, LANES), LANES)
        gg_ref[tile_of(q)] = lax.dot_general(
            go_ref[...], weights_ref[rows, :], (NT, ((), ())), preferred_element_type=jnp.float32
        )
        return carry

    lax.fori_loop(0, tiles, gated_gradient, 0)
    row_at = lax.broadcasted_iota(jnp.int32, (length, length), 0)
    col_at = lax.broadcasted_iota(jnp.int32, (length, length), 1)
    lower = row_at >= col_at
    shifted = dt_ref[...] + head_ref[0:1, :]
    rate = -jnp.exp(head_ref[1:2, :])
    softplus = jnp.maximum(shifted, 0.0) + jnp.log1p(jnp.exp(-jnp.abs(shifted)))
    step_ref[...] = softplus
    ld_ref[...] = dot(jnp.where(lower, 1.0, 0.0), softplus * rate, NN)
    ldt_ref[...] = ld_ref[...].T
    stept_ref[...] = softplus.T

    pl.semaphore_wait(barrier, 2 * count - 1)

    end = pl.ds(length - RIM, RIM)
    rims = (
        lambda: copy(x_ref.at[end, :], rim_x, me + 1, rim_send.at[0], rim_recv.at[0]),
        lambda: copy(bcraw_ref.at[end, :], rim_bc, me + 1, rim_send.at[1], rim_recv.at[1]),
    )

    @pl.when(me < count - 1)
    def _():
        for make in rims:
            make().start()

    first_go()

    @pl.when(me == 0)
    def _():
        rim_x[...] = jnp.zeros_like(rim_x)
        rim_bc[...] = jnp.zeros_like(rim_bc)

    @pl.when(me > 0)
    def _():
        copy(rim_x, rim_x, 0, rim_send.at[0], rim_recv.at[0]).wait_recv()
        copy(rim_bc, rim_bc, 0, rim_send.at[1], rim_recv.at[1]).wait_recv()

    pre_bc = convolve(
        bcraw_ref[...].astype(jnp.float32), rim_bc[...].astype(jnp.float32), cbc_ref[...], pad_bc
    )
    prebc_ref[...] = pre_bc
    act[...] = silu(pre_bc)
    b_rows = act.at[:, :state]
    c_rows = act.at[:, state:]
    split = (ROW_TILES, ROWS, LANES)

    def forward(k, carry):
        q = lax.rem(k + me, tiles)
        at = tile_of(q)
        pre = convolve(
            x_ref[at].astype(jnp.float32), rim_x[at].astype(jnp.float32), chan_ref[at], pad_x
        )
        prex_ref[at] = pre
        ld = expand(ld_ref[...], q)
        step = expand(step_ref[...], q)
        ldx[at] = ld
        stepx[at] = step
        last = ld[length - 1 :, :]
        f_ref[q] = dot(b_rows[...], jnp.exp(last - ld) * step * silu(pre), TN).reshape(split)
        decay_ref[q] = jnp.exp(last)
        give(0, q)
        return carry

    lax.fori_loop(0, tiles, forward, 0)

    def backward(k, carry):
        q = lax.rem(k + me, tiles)
        at = tile_of(q)
        gy = gg_ref[at] * silu(gate_ref[at].astype(jnp.float32))
        r_ref[q] = dot(c_rows[...], jnp.exp(ldx[at]) * gy, TN).reshape(split)
        give(1, q)
        return carry

    lax.fori_loop(0, tiles, backward, 0)

    lane = lax.broadcasted_iota(jnp.int32, (length, LANES), 1)
    first = lane < HEAD
    scores[...] = dot(c_rows[...], b_rows[...], NT)
    for ref in (shared, grad_b, grad_c, heads, const):
        ref[...] = jnp.zeros_like(ref)

    def inside(q, carry):
        at = tile_of(q)
        x = silu(prex_ref[at])
        gy = gg_ref[at] * silu(gate_ref[at].astype(jnp.float32))
        ld = ldx[at]
        xs = stepx[at] * x
        parts, grads = [], []
        total = shared[...]
        for a in range(2):
            mine = row_at == 2 * q + a
            ldt = jnp.sum(jnp.where(mine, ldt_ref[...], 0.0), axis=0, keepdims=True)
            stept = jnp.sum(jnp.where(mine, stept_ref[...], 0.0), axis=0, keepdims=True)
            spread = ld[:, a * HEAD : a * HEAD + 1] - ldt
            decays = jnp.where(lower, jnp.exp(jnp.where(lower, spread, 0.0)), 0.0)
            mixing = decays * scores[...]
            parts.append(dot(mixing, xs, NN))
            grads.append(dot(mixing, gy, TN))
            own = first if a == 0 else jnp.logical_not(first)
            products = dot(jnp.where(own, gy, 0.0), x, NT)
            total = total + decays * products * stept
        shared[...] = total
        within[at] = jnp.where(first, parts[0], parts[1])
        grad0[at] = jnp.where(first, grads[0], grads[1])
        return carry

    lax.fori_loop(0, tiles, inside, 0)

    def head_sums(value, q):
        left = jnp.sum(jnp.where(first, value, 0.0), axis=1, keepdims=True)
        right = jnp.sum(jnp.where(first, 0.0, value), axis=1, keepdims=True)
        return jnp.where(lane == 2 * q, left, jnp.where(lane == 2 * q + 1, right, 0.0))

    scan(0)
    second_go()
    scan(1)
    wait_back(0)

    def outputs(q, carry):
        at = tile_of(q)
        gate = gate_ref[at].astype(jnp.float32)
        gate_silu = silu(gate)
        gg = gg_ref[at]
        grow = jnp.exp(ldx[at])
        carried = dot(c_rows[...], sin[q].reshape(state, LANES), NN)
        y = within[at] + grow * carried + chan_ref[dskip_of(q)] * silu(prex_ref[at])
        gated_ref[at] = (y * gate_silu).astype(gated_ref.dtype)
        gradz_ref[at] = (gg * y * silu_slope(gate)).astype(gradz_ref.dtype)
        heads[3] += head_sums(gg * gate_silu * carried, q)
        return carry

    lax.fori_loop(0, tiles, outputs, 0)

    def lanes(tile):
        return pl.ds(pl.multiple_of((tile - 10 * core) * LANES, LANES), LANES)

    def give_gated(k, carry):
        to = lax.rem(line + k, lines)
        chip = to * LINE + spot
        for d in range(2):
            away = jnp.logical_or(to != line, core != d)
            for at, tile, store in ((0, to, main), (1, 16 + to // 4, extra)):
                mine = tile_core(tile) == core

                @pl.when(jnp.logical_and(mine, away))
                def _():
                    across(
                        gated_ref.at[:, lanes(tile)], store.at[line], chip, d,
                        g_send.at[2 * at + d], g_recv.at[at],
                    ).start()

                @pl.when(jnp.logical_and(mine, jnp.logical_not(away)))
                def _():
                    store[line] = gated_ref[:, lanes(tile)]

        return carry

    lax.fori_loop(0, lines, give_gated, 0)

    def wait_for(number, options, ref, act_on):
        for n in options:

            @pl.when(number == n)
            def _():
                act_on(ref.at[pl.ds(0, n)])

    one = lambda flag: jnp.where(flag, 1, 0)

    def wait_gated(at):
        tile = line if at == 0 else 16 + line // 4
        number = lines - one(tile_core(tile) == core)
        wait_for(
            number, (lines - 1, lines), main,
            lambda ref: across(ref, ref, 0, 0, g_send.at[0], g_recv.at[at]).wait_recv(),
        )

    wait_gated(0)
    wait_gated(1)
    finish_go()

    def product(store, start):
        value = lax.dot_general(
            store[...].reshape(lines * length, LANES),
            all_ref[:, :, pl.ds(start, LANES)].reshape(lines * length, LANES),
            (TN, ((), ())),
            preferred_element_type=jnp.float32,
        )
        return value.T

    for j in range(half * OWN // LANES):
        sums[j * LANES : (j + 1) * LANES, :] = product(main, j * LANES)
    for i in range(half):
        slots[i] = sums[i * OWN : (i + 1) * OWN, :].astype(slots.dtype)

    main_core = tile_core(line)
    column = line - 10 * main_core

    def send_main(k, carry):
        i = lax.rem(k + me, half)
        to = half * core + i
        away = jnp.logical_or(to != me, main_core != core)

        @pl.when(away)
        def _():
            across(
                slots.at[i], got.at[column, spot], to, main_core, w_send.at[0], w_recv.at[0]
            ).start()

        @pl.when(jnp.logical_not(away))
        def _():
            got[column, spot] = slots[i]

        return carry

    lax.fori_loop(0, half, send_main, 0)

    first_tile = (5 * quarter) // 2
    for j in range(3):
        more[j * LANES : (j + 1) * LANES, :] = product(
            extra, pl.multiple_of((first_tile + j) * LANES, LANES)
        )
    kept = more[pl.ds(pl.multiple_of(64 * lax.rem(quarter, 2), 64), 16 * OWN), :]
    for i in range(16):
        slots[half + i] = kept[i * OWN : (i + 1) * OWN, :].astype(slots.dtype)

    extra_column = 6 + line // 4

    def send_extra(k, carry):
        i = lax.rem(k + spot, 16)
        to = half * core + 16 * quarter + i
        away = jnp.logical_or(to != me, core != 1)

        @pl.when(away)
        def _():
            across(
                slots.at[half + i], got.at[extra_column, spot], to, 1, w_send.at[0], w_recv.at[0]
            ).start()

        @pl.when(jnp.logical_not(away))
        def _():
            got[extra_column, spot] = slots[half + i]

        return carry

    lax.fori_loop(0, 16, send_extra, 0)

    wait_back(1)

    def gradients(q, carry):
        at = tile_of(q)
        pre = prex_ref[at]
        x = silu(pre)
        gy = gg_ref[at] * silu(gate_ref[at].astype(jnp.float32))
        ld = ldx[at]
        step = stepx[at]
        weight = jnp.exp(ld[length - 1 :, :] - ld) * step
        s_in = sin[q].reshape(state, LANES)
        r_in = rin[q].reshape(state, LANES)
        carry_b = dot(b_rows[...], r_in, NN)
        inner = grad0[at]
        grad_in = chan_ref[dskip_of(q)] * gy + step * inner + weight * carry_b
        gxc_ref[at] = (grad_in * silu_slope(pre)).astype(gxc_ref.dtype)
        grad_b[...] += dot(weight * x, r_in, NT)
        grad_c[...] += dot(jnp.exp(ld) * gy, s_in, NT)
        heads[0] += head_sums(gy * within[at], q)
        heads[1] += head_sums(x * inner, q)
        heads[2] += head_sums(x * carry_b, q)
        const[...] += head_sums(
            jnp.broadcast_to(jnp.sum(r_in * s_in, axis=0, keepdims=True), x.shape), q
        )
        return carry

    lax.fori_loop(0, tiles, gradients, 0)
    gbc[:, :state] = grad_b[...] + dot(shared[...], c_rows[...], TN)
    gbc[:, state:] = grad_c[...] + dot(shared[...], b_rows[...], NN)
    swap = across(gbc, other, me, 1 - core, bc_send.at[0], bc_recv.at[0])
    swap.start()
    ldh = ld_ref[...]
    steph = step_ref[...]
    lasth = ldh[length - 1 :, :]
    to_endh = jnp.exp(lasth - ldh)
    direct, carry_dot = heads[1], heads[2]
    leaving = to_endh * steph * carry_dot
    grad_log = heads[0] - steph * direct + jnp.exp(ldh) * heads[3] - leaving
    constant = jnp.sum(leaving, axis=0, keepdims=True) + jnp.exp(lasth) * const[0:1, :]
    upper = jnp.where(col_at >= row_at, 1.0, 0.0)
    grad_rate = dot(upper, grad_log, NN) + constant
    gstep_ref[...] = (direct + to_endh * carry_dot + rate * grad_rate) * jax.nn.sigmoid(shifted)

    at_home = me // half == core
    own_main = one(jnp.logical_and(at_home, main_core == core))
    own_extra = one(
        jnp.logical_and(
            jnp.logical_and(at_home, core == 1), lax.rem(me, half) // 16 == quarter
        )
    )
    total = half + 16
    number = total - own_main - own_extra
    wait_for(
        number, (total - 2, total - 1, total), slots,
        lambda ref: across(ref, ref, 0, 0, w_send.at[0], w_recv.at[0]).wait_recv(),
    )
    for t in range(10):
        value = got[t, 0].astype(jnp.float32)
        for z in range(1, LINE):
            value = value + got[t, z].astype(jnp.float32)
        out_ref[:, t * LANES : (t + 1) * LANES] = value
    swap.wait()
    bc_ref[...] = ((gbc[...] + other[...]) * silu_slope(prebc_ref[...])).astype(bc_ref.dtype)
    wait_for(
        number, (total - 2, total - 1, total), slots,
        lambda ref: across(ref, ref, 0, 0, w_send.at[0], w_recv.at[0]).wait_send(),
    )
    for d in range(2):
        same = jnp.logical_and(main_core == core, core == d)
        wait_for(
            jnp.where(core == 0, 10, 6) - one(same), (5, 6, 9, 10), main,
            lambda ref: across(ref, ref, 0, 0, g_send.at[d], g_recv.at[0]).wait_send(),
        )
        wait_for(
            jnp.where(core == 0, 0, lines - d), (lines - d,), main,
            lambda ref: across(ref, ref, 0, 0, g_send.at[2 + d], g_recv.at[0]).wait_send(),
        )
    finish_scan(0)
    finish_scan(1)

    @pl.when(me < count - 1)
    def _():
        for make in rims:
            make().wait_send()


def finish_kernel(out, bc, gradz, gxc, gstep, out_to, bc_to, gradz_to, gxc_to, gstep_to):
    for source, target in ((out, out_to), (bc, bc_to), (gradz, gradz_to), (gxc, gxc_to)):
        target[...] = source[...]
    gstep_to[...] = gstep[:, : gstep_to.shape[1]]


def finish(values, heads):
    vmem = pl.BlockSpec(memory_space=pltpu.VMEM)
    shapes = [jax.ShapeDtypeStruct(v.shape, v.dtype) for v in values[:-1]]
    shapes.append(jax.ShapeDtypeStruct((values[-1].shape[0], heads), values[-1].dtype))
    return pl.pallas_call(
        finish_kernel, out_shape=shapes, in_specs=[vmem] * 5, out_specs=[vmem] * 5, name="finish"
    )(*values)


def main_part(x_raw, bc_raw, gate, dt, head, chan, cbc, w, go, count):
    length, channels = x_raw.shape
    states = bc_raw.shape[1]
    state = states // 2
    tiles = channels // LANES
    lines = count // LINE
    half = count // 2
    f32, bf16 = jnp.float32, jnp.bfloat16
    vmem = pl.BlockSpec(memory_space=pltpu.VMEM)
    dma = pltpu.SemaphoreType.DMA
    wide = pltpu.VMEM((length, channels), f32)
    square = pltpu.VMEM((length, LANES), f32)
    piece = pltpu.VMEM((tiles, ROW_TILES, ROWS, LANES), f32)
    return pl.pallas_call(
        functools.partial(main_kernel, count),
        out_shape=[
            jax.ShapeDtypeStruct((OWN, channels), f32),
            jax.ShapeDtypeStruct((length, 2 * state), bf16),
            jax.ShapeDtypeStruct((length, channels), bf16),
            jax.ShapeDtypeStruct((length, channels), bf16),
            jax.ShapeDtypeStruct((length, LANES), f32),
        ],
        in_specs=[vmem] * 9,
        out_specs=[vmem] * 5,
        scratch_shapes=[
            piece, piece, pltpu.VMEM((tiles, 1, LANES), f32), wide, wide,
            pltpu.VMEM((length, states), f32), square, square, square, square,
            pltpu.VMEM((RIM, channels), bf16), pltpu.VMEM((RIM, states), bf16),
            pltpu.VMEM((length + RIM, LANES), f32), pltpu.VMEM((length + RIM, states), f32),
        ]
        + [pltpu.VMEM((count, ROWS, LANES), f32)] * 4
        + [pltpu.VMEM((count, 1, LANES), f32)] * 2
        + [piece] * 2
        + [pltpu.VMEM((lines, length, go.shape[1] // 2), go.dtype)]
        + [wide] * 4
        + [
            pltpu.VMEM((length, channels), bf16),
            pltpu.VMEM((length, 2 * state), f32),
            square, square, square, square,
            pltpu.VMEM((4, length, LANES), f32),
            square,
            pltpu.VMEM((length, 2 * state), f32),
            pltpu.VMEM((length, 2 * state), f32),
            pltpu.VMEM((lines, length, LANES), bf16),
            pltpu.VMEM((lines, length, LANES), bf16),
            pltpu.VMEM((half * OWN, LANES), f32),
            pltpu.VMEM((3 * LANES, LANES), f32),
            pltpu.VMEM((half + 16, OWN, LANES), bf16),
            pltpu.VMEM((10, LINE, OWN, LANES), bf16),
        ]
        + [dma((2,))] * 6
        + [dma((4,))] * 3
        + [dma((2,))]
        + [dma((1,))] * 4
        + [dma((2,))] * 2,
        compiler_params=pltpu.CompilerParams(collective_id=0, has_side_effects=True),
        name="main",
    )(x_raw, bc_raw, gate, dt, head, chan, cbc, w, go)


def per_device(
    x_raw, bc_raw, gate_branch, dt_raw, conv_x, conv_x_bias, conv_bc, conv_bc_bias, dt_bias, a_log,
    d_skip, out_weight, grad_out,
):
    length, heads = dt_raw.shape
    channels = x_raw.shape[1]
    zeros = lambda rows, width: jnp.zeros((rows, width), jnp.float32)
    dt = jnp.pad(dt_raw, ((0, 0), (0, LANES - heads)))
    head = jnp.pad(jnp.stack([dt_bias, a_log]), ((0, 6), (0, LANES - heads)))
    chan = jnp.concatenate(
        [conv_x, conv_x_bias[None, :], jnp.repeat(d_skip, HEAD)[None, :], zeros(2, channels)]
    )
    cbc = jnp.concatenate([conv_bc, conv_bc_bias[None, :], zeros(3, bc_raw.shape[1])])
    values = main_part(
        x_raw, bc_raw, gate_branch, dt, head, chan, cbc, out_weight, grad_out,
        lax.axis_size("ctx"),
    )
    weight_grad, grad_bc_conv, grad_z, gxc, grad_dt_raw = finish(values, heads)
    return (gxc, grad_bc_conv, grad_z, grad_dt_raw, weight_grad)


def solution(mesh):
    placed = (
        P("ctx", "tp"), P("ctx", None), P("ctx", "tp"), P("ctx", "tp"), P(None, "tp"), P("tp"),
        P(), P(), P("tp"), P("tp"), P("tp"), P("tp", None), P("ctx", None),
    )
    return jax.shard_map(
        per_device,
        mesh=mesh,
        in_specs=placed,
        out_specs=(P("ctx", "tp"), P("ctx", None), P("ctx", "tp"), P("ctx", "tp"), P("ctx", "tp")),
        check_vma=False,
    )
```

```python
import functools

import jax
import jax.numpy as jnp
from jax import lax
from jax.experimental import pallas as pl
from jax.experimental.pallas import tpu as pltpu
from jax.sharding import PartitionSpec as P

KERNEL = 4
HEAD = 64
LANES = 128
ROWS = 16
ROW_TILES = 8
PER_LINE = 5
LINE = 8
SIDE = 4
MESH = pl.DeviceIdType.MESH


def dot(a, b, contract):
    return lax.dot_general(
        a,
        b,
        (contract, ((), ())),
        precision=lax.Precision.HIGHEST,
        preferred_element_type=jnp.float32,
    )


NN = ((1,), (0,))
TN = ((0,), (0,))
NT = ((1,), (1,))


def silu_slope(argument):
    gate_value = jax.nn.sigmoid(argument)
    return gate_value * (1.0 + argument * (1.0 - gate_value))


def silu(argument):
    return argument * jax.nn.sigmoid(argument)


def expand(per_head, q):
    row = lax.broadcasted_iota(jnp.int32, (LANES, LANES), 0)
    lane = lax.broadcasted_iota(jnp.int32, (LANES, LANES), 1)
    pick = jnp.where(row == 2 * q + jnp.where(lane < HEAD, 0, 1), 1.0, 0.0)
    return dot(per_head, pick, NN)


RIM = 16


def convolve(raw, rim, taps, padded):
    length = raw.shape[0]
    padded[0:RIM, :] = rim
    padded[RIM : RIM + length, :] = raw
    result = jnp.broadcast_to(taps[KERNEL], raw.shape)
    for k in range(KERNEL):
        start = RIM - (KERNEL - 1) + k
        result = result + taps[k] * padded[start : start + length, :]
    return result


OWN = 20


def owner_of(tile, row, shift):
    line = lax.rem(tile, 2) * ROW_TILES + row
    spot = lax.rem((LINE * (tile // 2)) // PER_LINE + shift + 2 * line + line // 4, LINE)
    return line * LINE + spot


def piece_of(chip, shift):
    line = chip // LINE
    spot = lax.rem(lax.rem(chip, LINE) + 8 * LINE - shift - 2 * line - line // 4, LINE)
    rank = (PER_LINE * spot + LINE - 1) // LINE
    owns = (LINE * rank) // PER_LINE == spot
    return 2 * rank + line // ROW_TILES, lax.rem(line, ROW_TILES), owns


def tile_core(tile):
    return tile // 10


def main_kernel(
    count, x_ref, bcraw_ref, gate_ref, dt_ref, chan_ref, weights_ref, go_ref,
    out_ref, bc_ref, gradz_ref, gxc_ref, gstep_ref,
    f_ref, r_ref, decay_ref, prex_ref, gg_ref, prebc_ref, ld_ref, step_ref, ldt_ref, stept_ref,
    rim_x, rim_bc, pad_x, pad_bc,
    got_f, got_r, back_f, back_r, decay_f, decay_r, sin, rin, all_ref, ldx, stepx, within, grad0,
    gated_ref, act, scores, shared, grad_b, grad_c, heads, const, gbc, other,
    main, extra, sums, more, slots, got,
    send, recv, back_send, back_recv, decay_send, decay_recv, go_send, go_recv,
    g_send, g_recv, w_send, w_recv, bc_send, bc_recv, rim_send, rim_recv,
):
    me = lax.axis_index("ctx")
    core = lax.axis_index("tp")
    line, spot = me // LINE, lax.rem(me, LINE)
    lines = count // LINE
    half = count // 2
    length = x_ref.shape[0]
    state = bcraw_ref.shape[1] // 2
    tiles = f_ref.shape[0]
    pieces = tiles * ROW_TILES
    quarter = lax.rem(line, 4)
    barrier = pltpu.get_barrier_semaphore()

    def greet(k, carry):
        peer = lax.rem(me + k, count)
        for d in range(2):

            @pl.when(jnp.logical_or(k > 0, core != d))
            def _():
                pl.semaphore_signal(
                    barrier, inc=1, device_id={"ctx": peer, "tp": d}, device_id_type=MESH
                )

        return carry

    lax.fori_loop(0, count, greet, 0)

    def copy(src, dst, peer, here, there):
        return pltpu.make_async_remote_copy(
            src_ref=src, dst_ref=dst, send_sem=here, recv_sem=there,
            device_id={"ctx": peer}, device_id_type=MESH,
        )

    def across(src, dst, chip, d, here, there):
        return pltpu.make_async_remote_copy(
            src_ref=src, dst_ref=dst, send_sem=here, recv_sem=there,
            device_id={"ctx": chip, "tp": d}, device_id_type=MESH,
        )

    sets = (
        (0, f_ref, decay_f, sin, got_f, back_f, False),
        (1, r_ref, decay_r, rin, got_r, back_r, True),
    )

    def give(which, tile):
        _, src, decay, dst, arrived, back, reverse = sets[which]
        for j in range(ROW_TILES):
            row = lax.rem(me + j, ROW_TILES)
            owner = owner_of(tile, row, which)

            @pl.when(owner != me)
            def _():
                copy(
                    src.at[tile, row], arrived.at[me], owner, send.at[which], recv.at[which]
                ).start()
                copy(
                    decay_ref.at[tile], decay.at[me], owner,
                    decay_send.at[which], decay_recv.at[which],
                ).start()

    def scan(which):
        _, src, decay, dst, arrived, back, reverse = sets[which]
        own_tile, own_row, owns = piece_of(me, which)

        @pl.when(owns)
        def _():
            arrived[me] = src[own_tile, own_row]
            decay[me] = decay_ref[own_tile]
            some = arrived.at[pl.ds(0, count - 1)]
            copy(some, some, 0, send.at[which], recv.at[which]).wait_recv()
            some = decay.at[pl.ds(0, count - 1)]
            copy(some, some, 0, decay_send.at[which], decay_recv.at[which]).wait_recv()

            def step(k, value):
                for u in range(4):
                    at = 4 * k + u
                    at = count - 1 - at if reverse else at
                    back[at] = value
                    value = decay[at] * value + arrived[at]
                return value

            lax.fori_loop(0, count // 4, step, jnp.zeros((ROWS, LANES), jnp.float32))
            dst[own_tile, own_row] = back[me]

            def give_back(k, carry):
                peer = lax.rem(me + k, count)
                copy(
                    back.at[peer], dst.at[own_tile, own_row], peer,
                    back_send.at[which], back_recv.at[which],
                ).start()
                return carry

            lax.fori_loop(1, count, give_back, 0)

    def wait_back(which):
        _, src, decay, dst, arrived, back, reverse = sets[which]
        own_tile, own_row, owns = piece_of(me, which)
        for flag, number in ((owns, pieces - 1), (jnp.logical_not(owns), pieces)):

            @pl.when(flag)
            def _():
                some = arrived.at[pl.ds(0, number)]
                copy(some, some, 0, send.at[which], back_recv.at[which]).wait_recv()

    def finish_scan(which):
        _, src, decay, dst, arrived, back, reverse = sets[which]
        own_tile, own_row, owns = piece_of(me, which)
        for flag, number in ((owns, pieces - 1), (jnp.logical_not(owns), pieces)):

            @pl.when(flag)
            def _():
                some = arrived.at[pl.ds(0, number)]
                few = decay.at[pl.ds(0, number)]
                copy(some, some, 0, send.at[which], back_recv.at[which]).wait_send()
                copy(few, few, 0, decay_send.at[which], decay_recv.at[which]).wait_send()

        @pl.when(owns)
        def _():
            rest = back.at[pl.ds(0, count - 1)]
            copy(rest, rest, 0, back_send.at[which], back_recv.at[which]).wait_send()

    x_at, y_at = line // SIDE, lax.rem(line, SIDE)
    features = go_ref.shape[1] // 2
    middle = features // 2
    early, late = pl.ds(0, middle), pl.ds(middle, middle)
    start_go = pl.multiple_of(core * features, LANES)
    go_early = pl.ds(start_go, middle)
    go_late = pl.ds(pl.multiple_of(core * features + middle, LANES), middle)
    along_x = [lax.rem(x_at + d, SIDE) * SIDE + y_at for d in range(SIDE)]
    along_y = [x_at * SIDE + lax.rem(y_at + d, SIDE) for d in range(SIDE)]

    def shift_go(src, dst, to, at):
        copy(src, dst, to * LINE + spot, go_send.at[at], go_recv.at[at]).start()

    def first_go():
        all_ref[line] = go_ref[:, pl.ds(start_go, features)]
        for d in range(1, SIDE):
            shift_go(go_ref.at[:, go_early], all_ref.at[line, :, early], along_y[d], 0)
            shift_go(go_ref.at[:, go_late], all_ref.at[line, :, late], along_x[d], 1)

    def second_go():
        some = all_ref.at[pl.ds(0, SIDE - 1), :, early]
        for at in range(2):
            copy(some, some, 0, go_send.at[at], go_recv.at[at]).wait_recv()
        for d in range(1, SIDE):
            for k in range(SIDE):
                held = all_ref.at[along_y[k], :, early]
                shift_go(held, held, along_x[d], 2)
                held = all_ref.at[along_x[k], :, late]
                shift_go(held, held, along_y[d], 3)

    def finish_go():
        some = all_ref.at[pl.ds(0, SIDE - 1), :, early]
        most = all_ref.at[pl.ds(0, SIDE * (SIDE - 1)), :, early]
        for at in range(2):
            copy(some, some, 0, go_send.at[at], go_recv.at[at]).wait_send()
            copy(most, most, 0, go_send.at[2 + at], go_recv.at[2 + at]).wait()

    def tile_of(q):
        return (slice(None), pl.ds(pl.multiple_of(q * LANES, LANES), LANES))

    def dskip_of(q):
        return (slice(KERNEL + 1, KERNEL + 2), pl.ds(pl.multiple_of(q * LANES, LANES), LANES))

    def gated_gradient(q, carry):
        rows = pl.ds(pl.multiple_of(q * LANES, LANES), LANES)
        gg_ref[tile_of(q)] = lax.dot_general(
            go_ref[...], weights_ref[rows, :], (NT, ((), ())), preferred_element_type=jnp.float32
        )
        return carry

    lax.fori_loop(0, tiles, gated_gradient, 0)
    row_at = lax.broadcasted_iota(jnp.int32, (length, length), 0)
    col_at = lax.broadcasted_iota(jnp.int32, (length, length), 1)
    lower = row_at >= col_at
    ldt_ref[...] = jnp.zeros_like(ldt_ref)
    ldt_ref[: dt_ref.shape[0], :] = dt_ref[...]
    shifted = ldt_ref[...].T + chan_ref[7:8, :LANES]
    rate = -jnp.exp(chan_ref[7:8, LANES : 2 * LANES])
    softplus = jnp.maximum(shifted, 0.0) + jnp.log1p(jnp.exp(-jnp.abs(shifted)))
    step_ref[...] = softplus
    ld_ref[...] = dot(jnp.where(lower, 1.0, 0.0), softplus * rate, NN)
    ldt_ref[...] = ld_ref[...].T
    stept_ref[...] = softplus.T

    pl.semaphore_wait(barrier, 2 * count - 1)

    end = pl.ds(length - RIM, RIM)
    rims = (
        lambda: copy(x_ref.at[end, :], rim_x, me + 1, rim_send.at[0], rim_recv.at[0]),
        lambda: copy(bcraw_ref.at[end, :], rim_bc, me + 1, rim_send.at[1], rim_recv.at[1]),
    )

    @pl.when(me < count - 1)
    def _():
        for make in rims:
            make().start()

    @pl.when(me == 0)
    def _():
        rim_x[...] = jnp.zeros_like(rim_x)
        rim_bc[...] = jnp.zeros_like(rim_bc)

    @pl.when(me > 0)
    def _():
        copy(rim_x, rim_x, 0, rim_send.at[0], rim_recv.at[0]).wait_recv()
        copy(rim_bc, rim_bc, 0, rim_send.at[1], rim_recv.at[1]).wait_recv()

    pre_bc = convolve(
        bcraw_ref[...].astype(jnp.float32), rim_bc[...].astype(jnp.float32),
        [chan_ref[6:7, k * 2 * state : (k + 1) * 2 * state] for k in range(KERNEL + 1)], pad_bc,
    )
    prebc_ref[...] = pre_bc
    act[...] = silu(pre_bc)
    b_rows = act.at[:, :state]
    c_rows = act.at[:, state:]
    split = (ROW_TILES, ROWS, LANES)

    def forward(k, carry):
        q = lax.rem(k + me, tiles)
        at = tile_of(q)
        pre = convolve(
            x_ref[at].astype(jnp.float32), rim_x[at].astype(jnp.float32),
            [chan_ref[k : k + 1, at[1]] for k in range(KERNEL + 1)], pad_x,
        )
        prex_ref[at] = pre
        ld = expand(ld_ref[...], q)
        step = expand(step_ref[...], q)
        ldx[at] = ld
        stepx[at] = step
        last = ld[length - 1 :, :]
        f_ref[q] = dot(b_rows[...], jnp.exp(last - ld) * step * silu(pre), TN).reshape(split)
        decay_ref[q] = jnp.exp(last)
        give(0, q)
        return carry

    lax.fori_loop(0, tiles, forward, 0)
    first_go()

    def backward(k, carry):
        q = lax.rem(k + me, tiles)
        at = tile_of(q)
        gy = gg_ref[at] * silu(gate_ref[at].astype(jnp.float32))
        r_ref[q] = dot(c_rows[...], jnp.exp(ldx[at]) * gy, TN).reshape(split)
        give(1, q)
        return carry

    lax.fori_loop(0, tiles, backward, 0)

    lane = lax.broadcasted_iota(jnp.int32, (length, LANES), 1)
    first = lane < HEAD
    scores[...] = dot(c_rows[...], b_rows[...], NT)
    for ref in (shared, grad_b, grad_c, heads, const):
        ref[...] = jnp.zeros_like(ref)

    def inside(q, carry):
        at = tile_of(q)
        x = silu(prex_ref[at])
        gy = gg_ref[at] * silu(gate_ref[at].astype(jnp.float32))
        ld = ldx[at]
        xs = stepx[at] * x
        parts, grads = [], []
        total = shared[...]
        for a in range(2):
            mine = row_at == 2 * q + a
            ldt = jnp.sum(jnp.where(mine, ldt_ref[...], 0.0), axis=0, keepdims=True)
            stept = jnp.sum(jnp.where(mine, stept_ref[...], 0.0), axis=0, keepdims=True)
            spread = ld[:, a * HEAD : a * HEAD + 1] - ldt
            decays = jnp.where(lower, jnp.exp(jnp.where(lower, spread, 0.0)), 0.0)
            mixing = decays * scores[...]
            parts.append(dot(mixing, xs, NN))
            grads.append(dot(mixing, gy, TN))
            own = first if a == 0 else jnp.logical_not(first)
            products = dot(jnp.where(own, gy, 0.0), x, NT)
            total = total + decays * products * stept
        shared[...] = total
        within[at] = jnp.where(first, parts[0], parts[1])
        grad0[at] = jnp.where(first, grads[0], grads[1])
        return carry

    lax.fori_loop(0, tiles, inside, 0)

    def head_sums(value, q):
        left = jnp.sum(jnp.where(first, value, 0.0), axis=1, keepdims=True)
        right = jnp.sum(jnp.where(first, 0.0, value), axis=1, keepdims=True)
        return jnp.where(lane == 2 * q, left, jnp.where(lane == 2 * q + 1, right, 0.0))

    scan(0)
    second_go()
    wait_back(0)
    scan(1)

    def outputs(q, carry):
        at = tile_of(q)
        gate = gate_ref[at].astype(jnp.float32)
        gate_silu = silu(gate)
        gg = gg_ref[at]
        grow = jnp.exp(ldx[at])
        carried = dot(c_rows[...], sin[q].reshape(state, LANES), NN)
        y = within[at] + grow * carried + chan_ref[dskip_of(q)] * silu(prex_ref[at])
        gated_ref[q] = (y * gate_silu).T.astype(gated_ref.dtype)
        gradz_ref[at] = (gg * y * silu_slope(gate)).astype(gradz_ref.dtype)
        heads[3] += head_sums(gg * gate_silu * carried, q)
        return carry

    lax.fori_loop(0, tiles, outputs, 0)

    def placed(store, at):
        return store.at[:, pl.ds(pl.multiple_of(at * length, LANES), length)]

    def give_gated(k, carry):
        to = lax.rem(line + k, lines)
        chip = to * LINE + spot
        for d in range(2):
            away = jnp.logical_or(to != line, core != d)
            for at, tile, store in ((0, to, main), (1, 16 + to // 4, extra)):
                mine = tile_core(tile) == core

                @pl.when(jnp.logical_and(mine, away))
                def _():
                    across(
                        gated_ref.at[tile - 10 * core], placed(store, line), chip, d,
                        g_send.at[2 * at + d], g_recv.at[at],
                    ).start()

                @pl.when(jnp.logical_and(mine, jnp.logical_not(away)))
                def _():
                    placed(store, line)[...] = gated_ref[tile - 10 * core]

        return carry

    lax.fori_loop(0, lines, give_gated, 0)

    units = all_ref.at[:, :, pl.ds(0, LANES)]

    def wait_for(number, options, ref, act_on):
        for n in options:

            @pl.when(number == n)
            def _():
                act_on(ref.at[pl.ds(0, n)])

    one = lambda flag: jnp.where(flag, 1, 0)

    def wait_gated(at):
        tile = line if at == 0 else 16 + line // 4
        number = lines - one(tile_core(tile) == core)
        wait_for(
            number, (lines - 1, lines), units,
            lambda ref: across(ref, ref, 0, 0, g_send.at[0], g_recv.at[at]).wait_recv(),
        )

    wait_gated(0)
    finish_go()

    def product(store, start, width):
        value = lax.dot_general(
            store[...],
            all_ref[:, :, pl.ds(start, width)].reshape(lines * length, width),
            (NN, ((), ())),
            preferred_element_type=jnp.float32,
        )
        return value.T

    main_core = tile_core(line)
    column = line - 10 * main_core
    part = half // 2
    wide_part = part * OWN
    for turn in range(2):
        which = lax.rem(me + turn, 2)
        for j in range(wide_part // LANES):
            start = pl.multiple_of(which * wide_part + j * LANES, LANES)
            sums[j * LANES : (j + 1) * LANES, :] = product(main, start, LANES)
        for i in range(part):
            slots[which * part + i] = sums[i * OWN : (i + 1) * OWN, :].astype(slots.dtype)

        def send_main(k, carry):
            i = which * part + lax.rem(k + me // 2, part)
            to = half * core + i
            away = jnp.logical_or(to != me, main_core != core)

            @pl.when(away)
            def _():
                across(
                    slots.at[i], got.at[column, spot], to, main_core, w_send.at[0], w_recv.at[0]
                ).start()

            @pl.when(jnp.logical_not(away))
            def _():
                got[column, spot] = slots[i]

            return carry

        lax.fori_loop(0, part, send_main, 0)

    wait_gated(1)
    first_tile = (5 * quarter) // 2
    for j in range(3):
        more[j * LANES : (j + 1) * LANES, :] = product(
            extra, pl.multiple_of((first_tile + j) * LANES, LANES), LANES
        )
    kept = more[pl.ds(pl.multiple_of(64 * lax.rem(quarter, 2), 64), 16 * OWN), :]
    for i in range(16):
        slots[half + i] = kept[i * OWN : (i + 1) * OWN, :].astype(slots.dtype)

    extra_column = 6 + line // 4

    def send_extra(k, carry):
        i = lax.rem(k + spot, 16)
        to = half * core + 16 * quarter + i
        away = jnp.logical_or(to != me, core != 1)

        @pl.when(away)
        def _():
            across(
                slots.at[half + i], got.at[extra_column, spot], to, 1, w_send.at[0], w_recv.at[0]
            ).start()

        @pl.when(jnp.logical_not(away))
        def _():
            got[extra_column, spot] = slots[half + i]

        return carry

    lax.fori_loop(0, 16, send_extra, 0)

    wait_back(1)

    def gradients(q, carry):
        at = tile_of(q)
        pre = prex_ref[at]
        x = silu(pre)
        gy = gg_ref[at] * silu(gate_ref[at].astype(jnp.float32))
        ld = ldx[at]
        step = stepx[at]
        weight = jnp.exp(ld[length - 1 :, :] - ld) * step
        s_in = sin[q].reshape(state, LANES)
        r_in = rin[q].reshape(state, LANES)
        carry_b = dot(b_rows[...], r_in, NN)
        inner = grad0[at]
        grad_in = chan_ref[dskip_of(q)] * gy + step * inner + weight * carry_b
        gxc_ref[at] = (grad_in * silu_slope(pre)).astype(gxc_ref.dtype)
        grad_b[...] += dot(weight * x, r_in, NT)
        grad_c[...] += dot(jnp.exp(ld) * gy, s_in, NT)
        heads[0] += head_sums(gy * within[at], q)
        heads[1] += head_sums(x * inner, q)
        heads[2] += head_sums(x * carry_b, q)
        const[...] += head_sums(
            jnp.broadcast_to(jnp.sum(r_in * s_in, axis=0, keepdims=True), x.shape), q
        )
        return carry

    lax.fori_loop(0, tiles, gradients, 0)
    gbc[:, :state] = grad_b[...] + dot(shared[...], c_rows[...], TN)
    gbc[:, state:] = grad_c[...] + dot(shared[...], b_rows[...], NN)
    swap = across(gbc, other, me, 1 - core, bc_send.at[0], bc_recv.at[0])
    swap.start()
    ldh = ld_ref[...]
    steph = step_ref[...]
    lasth = ldh[length - 1 :, :]
    to_endh = jnp.exp(lasth - ldh)
    direct, carry_dot = heads[1], heads[2]
    leaving = to_endh * steph * carry_dot
    grad_log = heads[0] - steph * direct + jnp.exp(ldh) * heads[3] - leaving
    constant = jnp.sum(leaving, axis=0, keepdims=True) + jnp.exp(lasth) * const[0:1, :]
    upper = jnp.where(col_at >= row_at, 1.0, 0.0)
    grad_rate = dot(upper, grad_log, NN) + constant
    gstep_ref[...] = (direct + to_endh * carry_dot + rate * grad_rate) * jax.nn.sigmoid(shifted)
    gstep_ref[...] = gstep_ref[...].T

    at_home = me // half == core
    own_main = one(jnp.logical_and(at_home, main_core == core))
    own_extra = one(
        jnp.logical_and(
            jnp.logical_and(at_home, core == 1), lax.rem(me, half) // 16 == quarter
        )
    )
    total = half + 16
    number = total - own_main - own_extra
    wait_for(
        number, (total - 2, total - 1, total), slots,
        lambda ref: across(ref, ref, 0, 0, w_send.at[0], w_recv.at[0]).wait_recv(),
    )
    for t in range(10):
        value = got[t, 0].astype(jnp.float32)
        for z in range(1, LINE):
            value = value + got[t, z].astype(jnp.float32)
        out_ref[:, t * LANES : (t + 1) * LANES] = value
    swap.wait()
    bc_ref[...] = ((gbc[...] + other[...]) * silu_slope(prebc_ref[...])).astype(bc_ref.dtype)
    wait_for(
        number, (total - 2, total - 1, total), slots,
        lambda ref: across(ref, ref, 0, 0, w_send.at[0], w_recv.at[0]).wait_send(),
    )
    for d in range(2):
        same = jnp.logical_and(main_core == core, core == d)
        wait_for(
            jnp.where(core == 0, 10, 6) - one(same), (5, 6, 9, 10), units,
            lambda ref: across(ref, ref, 0, 0, g_send.at[d], g_recv.at[0]).wait_send(),
        )
        wait_for(
            jnp.where(core == 0, 0, lines - d), (lines - d,), units,
            lambda ref: across(ref, ref, 0, 0, g_send.at[2 + d], g_recv.at[0]).wait_send(),
        )
    finish_scan(0)
    finish_scan(1)

    @pl.when(me < count - 1)
    def _():
        for make in rims:
            make().wait_send()


def finish_kernel(out, bc, gradz, gxc, gstep, out_to, bc_to, gradz_to, gxc_to, gstep_to):
    for source, target in ((out, out_to), (bc, bc_to), (gradz, gradz_to), (gxc, gxc_to)):
        target[...] = source[...]
    gstep_to[...] = gstep[: gstep_to.shape[0], :]


def finish(values, heads):
    vmem = pl.BlockSpec(memory_space=pltpu.VMEM)
    shapes = [jax.ShapeDtypeStruct(v.shape, v.dtype) for v in values[:-1]]
    shapes.append(jax.ShapeDtypeStruct((heads, values[-1].shape[1]), values[-1].dtype))
    return pl.pallas_call(
        finish_kernel, out_shape=shapes, in_specs=[vmem] * 5, out_specs=[vmem] * 5, name="finish"
    )(*values)


def main_part(x_raw, bc_raw, gate, dt, chan, w, go, count):
    length, channels = x_raw.shape
    states = bc_raw.shape[1]
    state = states // 2
    tiles = channels // LANES
    lines = count // LINE
    half = count // 2
    f32, bf16 = jnp.float32, jnp.bfloat16
    vmem = pl.BlockSpec(memory_space=pltpu.VMEM)
    dma = pltpu.SemaphoreType.DMA
    wide = pltpu.VMEM((length, channels), f32)
    square = pltpu.VMEM((length, LANES), f32)
    piece = pltpu.VMEM((tiles, ROW_TILES, ROWS, LANES), f32)
    return pl.pallas_call(
        functools.partial(main_kernel, count),
        out_shape=[
            jax.ShapeDtypeStruct((OWN, channels), f32),
            jax.ShapeDtypeStruct((length, 2 * state), bf16),
            jax.ShapeDtypeStruct((length, channels), bf16),
            jax.ShapeDtypeStruct((length, channels), bf16),
            jax.ShapeDtypeStruct((length, LANES), f32),
        ],
        in_specs=[vmem] * 7,
        out_specs=[vmem] * 5,
        scratch_shapes=[
            piece, piece, pltpu.VMEM((tiles, 1, LANES), f32), wide, wide,
            pltpu.VMEM((length, states), f32), square, square, square, square,
            pltpu.VMEM((RIM, channels), bf16), pltpu.VMEM((RIM, states), bf16),
            pltpu.VMEM((length + RIM, LANES), f32), pltpu.VMEM((length + RIM, states), f32),
        ]
        + [pltpu.VMEM((count, ROWS, LANES), f32)] * 4
        + [pltpu.VMEM((count, 1, LANES), f32)] * 2
        + [piece] * 2
        + [pltpu.VMEM((lines, length, go.shape[1] // 2), go.dtype)]
        + [wide] * 4
        + [
            pltpu.VMEM((tiles, LANES, length), bf16),
            pltpu.VMEM((length, 2 * state), f32),
            square, square, square, square,
            pltpu.VMEM((4, length, LANES), f32),
            square,
            pltpu.VMEM((length, 2 * state), f32),
            pltpu.VMEM((length, 2 * state), f32),
            pltpu.VMEM((LANES, lines * length), bf16),
            pltpu.VMEM((LANES, lines * length), bf16),
            pltpu.VMEM((half // 2 * OWN, LANES), f32),
            pltpu.VMEM((3 * LANES, LANES), f32),
            pltpu.VMEM((half + 16, OWN, LANES), bf16),
            pltpu.VMEM((10, LINE, OWN, LANES), bf16),
        ]
        + [dma((2,))] * 6
        + [dma((4,))] * 3
        + [dma((2,))]
        + [dma((1,))] * 4
        + [dma((2,))] * 2,
        compiler_params=pltpu.CompilerParams(collective_id=0, has_side_effects=True),
        name="main",
    )(x_raw, bc_raw, gate, dt, chan, w, go)


def per_device(
    x_raw, bc_raw, gate_branch, dt_raw, conv_x, conv_x_bias, conv_bc, conv_bc_bias, dt_bias, a_log,
    d_skip, out_weight, grad_out,
):
    length, heads = dt_raw.shape
    channels = x_raw.shape[1]
    gap = jnp.zeros((LANES - heads,), jnp.float32)
    row = jnp.concatenate(
        [
            conv_x_bias, jnp.repeat(d_skip, HEAD), conv_bc.reshape(-1), conv_bc_bias,
            dt_bias, gap, a_log, gap, jnp.zeros((channels - 2 * LANES,), jnp.float32),
        ]
    )
    chan = jnp.concatenate([conv_x, row.reshape(4, channels)])
    values = main_part(
        x_raw, bc_raw, gate_branch, dt_raw.T, chan, out_weight, grad_out, lax.axis_size("ctx")
    )
    weight_grad, grad_bc_conv, grad_z, gxc, grad_dt_raw = finish(values, heads)
    return (gxc, grad_bc_conv, grad_z, grad_dt_raw.T, weight_grad)


def solution(mesh):
    placed = (
        P("ctx", "tp"), P("ctx", None), P("ctx", "tp"), P("ctx", "tp"), P(None, "tp"), P("tp"),
        P(), P(), P("tp"), P("tp"), P("tp"), P("tp", None), P("ctx", None),
    )
    return jax.shard_map(
        per_device,
        mesh=mesh,
        in_specs=placed,
        out_specs=(P("ctx", "tp"), P("ctx", None), P("ctx", "tp"), P("ctx", "tp"), P("ctx", "tp")),
        check_vma=False,
    )
```

```python
import functools

import jax
import jax.numpy as jnp
from jax import lax
from jax.experimental import pallas as pl
from jax.experimental.pallas import tpu as pltpu
from jax.sharding import PartitionSpec as P

KERNEL = 4
HEAD = 64
LANES = 128
ROWS = 16
ROW_TILES = 8
PER_LINE = 5
LINE = 8
SIDE = 4
MESH = pl.DeviceIdType.MESH


def dot(a, b, contract):
    return lax.dot_general(
        a,
        b,
        (contract, ((), ())),
        precision=lax.Precision.HIGHEST,
        preferred_element_type=jnp.float32,
    )


NN = ((1,), (0,))
TN = ((0,), (0,))
NT = ((1,), (1,))


def silu_slope(argument):
    gate_value = jax.nn.sigmoid(argument)
    return gate_value * (1.0 + argument * (1.0 - gate_value))


def silu(argument):
    return argument * jax.nn.sigmoid(argument)


def expand(per_head, q):
    row = lax.broadcasted_iota(jnp.int32, (LANES, LANES), 0)
    lane = lax.broadcasted_iota(jnp.int32, (LANES, LANES), 1)
    pick = jnp.where(row == 2 * q + jnp.where(lane < HEAD, 0, 1), 1.0, 0.0)
    return dot(per_head, pick, NN)


RIM = 16


def convolve(raw, rim, taps, padded):
    length = raw.shape[0]
    padded[0:RIM, :] = rim
    padded[RIM : RIM + length, :] = raw
    result = jnp.broadcast_to(taps[KERNEL], raw.shape)
    for k in range(KERNEL):
        start = RIM - (KERNEL - 1) + k
        result = result + taps[k] * padded[start : start + length, :]
    return result


OWN = 20


def owner_of(tile, row, shift):
    line = lax.rem(tile, 2) * ROW_TILES + row
    spot = lax.rem((LINE * (tile // 2)) // PER_LINE + shift + 2 * line + line // 4, LINE)
    return line * LINE + spot


def piece_of(chip, shift):
    line = chip // LINE
    spot = lax.rem(lax.rem(chip, LINE) + 8 * LINE - shift - 2 * line - line // 4, LINE)
    rank = (PER_LINE * spot + LINE - 1) // LINE
    owns = (LINE * rank) // PER_LINE == spot
    return 2 * rank + line // ROW_TILES, lax.rem(line, ROW_TILES), owns


def tile_core(tile):
    return tile // 10


def main_kernel(
    count, x_ref, bcraw_ref, gate_ref, dt_ref, chan_ref, weights_ref, go_ref,
    out_ref, bc_ref, gradz_ref, gxc_ref, gstep_ref,
    f_ref, r_ref, decay_ref, prex_ref, gg_ref, prebc_ref, ld_ref, step_ref, ldt_ref, stept_ref,
    rim_x, rim_bc, pad_x, pad_bc,
    got_f, got_r, back_f, back_r, decay_f, decay_r, sin, rin, all_ref, ldx, stepx, within, grad0,
    gated_ref, act, scores, shared, grad_b, grad_c, heads, const, gbc, other,
    main, extra, sums, more, slots, got,
    send, recv, back_send, back_recv, decay_send, decay_recv, go_send, go_recv,
    g_send, g_recv, w_send, w_recv, bc_send, bc_recv, rim_send, rim_recv,
):
    me = lax.axis_index("ctx")
    core = lax.axis_index("tp")
    line, spot = me // LINE, lax.rem(me, LINE)
    lines = count // LINE
    half = count // 2
    length = x_ref.shape[0]
    state = bcraw_ref.shape[1] // 2
    tiles = f_ref.shape[0]
    pieces = tiles * ROW_TILES
    quarter = lax.rem(line, 4)
    barrier = pltpu.get_barrier_semaphore()

    def greet(k, carry):
        peer = lax.rem(me + k, count)
        for d in range(2):

            @pl.when(jnp.logical_or(k > 0, core != d))
            def _():
                pl.semaphore_signal(
                    barrier, inc=1, device_id={"ctx": peer, "tp": d}, device_id_type=MESH
                )

        return carry

    lax.fori_loop(0, count, greet, 0)

    def copy(src, dst, peer, here, there):
        return pltpu.make_async_remote_copy(
            src_ref=src, dst_ref=dst, send_sem=here, recv_sem=there,
            device_id={"ctx": peer}, device_id_type=MESH,
        )

    def across(src, dst, chip, d, here, there):
        return pltpu.make_async_remote_copy(
            src_ref=src, dst_ref=dst, send_sem=here, recv_sem=there,
            device_id={"ctx": chip, "tp": d}, device_id_type=MESH,
        )

    sets = (
        (0, f_ref, decay_f, sin, got_f, back_f, False),
        (1, r_ref, decay_r, rin, got_r, back_r, True),
    )

    def give(which, tile):
        _, src, decay, dst, arrived, back, reverse = sets[which]
        for j in range(ROW_TILES):
            row = lax.rem(me + j, ROW_TILES)
            owner = owner_of(tile, row, which)

            @pl.when(owner != me)
            def _():
                copy(
                    src.at[tile, row], arrived.at[me], owner, send.at[which], recv.at[which]
                ).start()
                copy(
                    decay_ref.at[tile], decay.at[me], owner,
                    decay_send.at[which], decay_recv.at[which],
                ).start()

    def scan(which):
        _, src, decay, dst, arrived, back, reverse = sets[which]
        own_tile, own_row, owns = piece_of(me, which)

        @pl.when(owns)
        def _():
            arrived[me] = src[own_tile, own_row]
            decay[me] = decay_ref[own_tile]
            some = arrived.at[pl.ds(0, count - 1)]
            copy(some, some, 0, send.at[which], recv.at[which]).wait_recv()
            some = decay.at[pl.ds(0, count - 1)]
            copy(some, some, 0, decay_send.at[which], decay_recv.at[which]).wait_recv()

            def step(k, value):
                for u in range(4):
                    at = 4 * k + u
                    at = count - 1 - at if reverse else at
                    back[at] = value
                    value = decay[at] * value + arrived[at]
                return value

            lax.fori_loop(0, count // 4, step, jnp.zeros((ROWS, LANES), jnp.float32))
            dst[own_tile, own_row] = back[me]

            def give_back(k, carry):
                peer = lax.rem(me + k, count)
                copy(
                    back.at[peer], dst.at[own_tile, own_row], peer,
                    back_send.at[which], back_recv.at[which],
                ).start()
                return carry

            lax.fori_loop(1, count, give_back, 0)

    def wait_back(which):
        _, src, decay, dst, arrived, back, reverse = sets[which]
        own_tile, own_row, owns = piece_of(me, which)
        for flag, number in ((owns, pieces - 1), (jnp.logical_not(owns), pieces)):

            @pl.when(flag)
            def _():
                some = arrived.at[pl.ds(0, number)]
                copy(some, some, 0, send.at[which], back_recv.at[which]).wait_recv()

    def finish_scan(which):
        _, src, decay, dst, arrived, back, reverse = sets[which]
        own_tile, own_row, owns = piece_of(me, which)
        for flag, number in ((owns, pieces - 1), (jnp.logical_not(owns), pieces)):

            @pl.when(flag)
            def _():
                some = arrived.at[pl.ds(0, number)]
                few = decay.at[pl.ds(0, number)]
                copy(some, some, 0, send.at[which], back_recv.at[which]).wait_send()
                copy(few, few, 0, decay_send.at[which], decay_recv.at[which]).wait_send()

        @pl.when(owns)
        def _():
            rest = back.at[pl.ds(0, count - 1)]
            copy(rest, rest, 0, back_send.at[which], back_recv.at[which]).wait_send()

    x_at, y_at = line // SIDE, lax.rem(line, SIDE)
    features = go_ref.shape[1] // 2
    middle = features // 2
    early, late = pl.ds(0, middle), pl.ds(middle, middle)
    start_go = pl.multiple_of(core * features, LANES)
    go_early = pl.ds(start_go, middle)
    go_late = pl.ds(pl.multiple_of(core * features + middle, LANES), middle)
    along_x = [lax.rem(x_at + d, SIDE) * SIDE + y_at for d in range(SIDE)]
    along_y = [x_at * SIDE + lax.rem(y_at + d, SIDE) for d in range(SIDE)]

    def shift_go(src, dst, to, at):
        copy(src, dst, to * LINE + spot, go_send.at[at], go_recv.at[at]).start()

    def first_go():
        all_ref[line] = go_ref[:, pl.ds(start_go, features)]
        for d in range(1, SIDE):
            shift_go(go_ref.at[:, go_early], all_ref.at[line, :, early], along_y[d], 0)
            shift_go(go_ref.at[:, go_late], all_ref.at[line, :, late], along_x[d], 1)

    def second_go():
        some = all_ref.at[pl.ds(0, SIDE - 1), :, early]
        for at in range(2):
            copy(some, some, 0, go_send.at[at], go_recv.at[at]).wait_recv()
        for d in range(1, SIDE):
            for k in range(SIDE):
                held = all_ref.at[along_y[k], :, early]
                shift_go(held, held, along_x[d], 2)
                held = all_ref.at[along_x[k], :, late]
                shift_go(held, held, along_y[d], 3)

    def finish_go():
        some = all_ref.at[pl.ds(0, SIDE - 1), :, early]
        most = all_ref.at[pl.ds(0, SIDE * (SIDE - 1)), :, early]
        for at in range(2):
            copy(some, some, 0, go_send.at[at], go_recv.at[at]).wait_send()
            copy(most, most, 0, go_send.at[2 + at], go_recv.at[2 + at]).wait()

    def tile_of(q):
        return (slice(None), pl.ds(pl.multiple_of(q * LANES, LANES), LANES))

    def dskip_of(q):
        return (slice(KERNEL + 1, KERNEL + 2), pl.ds(pl.multiple_of(q * LANES, LANES), LANES))

    def gated_gradient(q, carry):
        rows = pl.ds(pl.multiple_of(q * LANES, LANES), LANES)
        gg_ref[tile_of(q)] = lax.dot_general(
            go_ref[...], weights_ref[rows, :], (NT, ((), ())), preferred_element_type=jnp.float32
        )
        return carry

    lax.fori_loop(0, tiles, gated_gradient, 0)
    row_at = lax.broadcasted_iota(jnp.int32, (length, length), 0)
    col_at = lax.broadcasted_iota(jnp.int32, (length, length), 1)
    lower = row_at >= col_at
    ldt_ref[...] = jnp.zeros_like(ldt_ref)
    ldt_ref[: dt_ref.shape[0], :] = dt_ref[...]
    shifted = ldt_ref[...].T + chan_ref[7:8, :LANES]
    rate = -jnp.exp(chan_ref[7:8, LANES : 2 * LANES])
    softplus = jnp.maximum(shifted, 0.0) + jnp.log1p(jnp.exp(-jnp.abs(shifted)))
    step_ref[...] = softplus
    ld_ref[...] = dot(jnp.where(lower, 1.0, 0.0), softplus * rate, NN)
    ldt_ref[...] = ld_ref[...].T
    stept_ref[...] = softplus.T

    pl.semaphore_wait(barrier, 2 * count - 1)

    end = pl.ds(length - RIM, RIM)
    rims = (
        lambda: copy(x_ref.at[end, :], rim_x, me + 1, rim_send.at[0], rim_recv.at[0]),
        lambda: copy(bcraw_ref.at[end, :], rim_bc, me + 1, rim_send.at[1], rim_recv.at[1]),
    )

    @pl.when(me < count - 1)
    def _():
        for make in rims:
            make().start()

    first_go()

    @pl.when(me == 0)
    def _():
        rim_x[...] = jnp.zeros_like(rim_x)
        rim_bc[...] = jnp.zeros_like(rim_bc)

    @pl.when(me > 0)
    def _():
        copy(rim_x, rim_x, 0, rim_send.at[0], rim_recv.at[0]).wait_recv()
        copy(rim_bc, rim_bc, 0, rim_send.at[1], rim_recv.at[1]).wait_recv()

    pre_bc = convolve(
        bcraw_ref[...].astype(jnp.float32), rim_bc[...].astype(jnp.float32),
        [chan_ref[6:7, k * 2 * state : (k + 1) * 2 * state] for k in range(KERNEL + 1)], pad_bc,
    )
    prebc_ref[...] = pre_bc
    act[...] = silu(pre_bc)
    b_rows = act.at[:, :state]
    c_rows = act.at[:, state:]
    split = (ROW_TILES, ROWS, LANES)

    def forward(k, carry):
        q = lax.rem(k + me, tiles)
        at = tile_of(q)
        pre = convolve(
            x_ref[at].astype(jnp.float32), rim_x[at].astype(jnp.float32),
            [chan_ref[k : k + 1, at[1]] for k in range(KERNEL + 1)], pad_x,
        )
        prex_ref[at] = pre
        ld = expand(ld_ref[...], q)
        step = expand(step_ref[...], q)
        ldx[at] = ld
        stepx[at] = step
        last = ld[length - 1 :, :]
        f_ref[q] = dot(b_rows[...], jnp.exp(last - ld) * step * silu(pre), TN).reshape(split)
        decay_ref[q] = jnp.exp(last)
        give(0, q)
        return carry

    lax.fori_loop(0, tiles, forward, 0)

    def backward(k, carry):
        q = lax.rem(k + me, tiles)
        at = tile_of(q)
        gy = gg_ref[at] * silu(gate_ref[at].astype(jnp.float32))
        r_ref[q] = dot(c_rows[...], jnp.exp(ldx[at]) * gy, TN).reshape(split)
        give(1, q)
        return carry

    lax.fori_loop(0, tiles, backward, 0)

    lane = lax.broadcasted_iota(jnp.int32, (length, LANES), 1)
    first = lane < HEAD
    scores[...] = dot(c_rows[...], b_rows[...], NT)
    for ref in (shared, grad_b, grad_c, heads, const):
        ref[...] = jnp.zeros_like(ref)

    def inside(q, carry):
        at = tile_of(q)
        x = silu(prex_ref[at])
        gy = gg_ref[at] * silu(gate_ref[at].astype(jnp.float32))
        ld = ldx[at]
        xs = stepx[at] * x
        parts, grads = [], []
        total = shared[...]
        for a in range(2):
            mine = row_at == 2 * q + a
            ldt = jnp.sum(jnp.where(mine, ldt_ref[...], 0.0), axis=0, keepdims=True)
            stept = jnp.sum(jnp.where(mine, stept_ref[...], 0.0), axis=0, keepdims=True)
            spread = ld[:, a * HEAD : a * HEAD + 1] - ldt
            decays = jnp.where(lower, jnp.exp(jnp.where(lower, spread, 0.0)), 0.0)
            mixing = decays * scores[...]
            parts.append(dot(mixing, xs, NN))
            grads.append(dot(mixing, gy, TN))
            own = first if a == 0 else jnp.logical_not(first)
            products = dot(jnp.where(own, gy, 0.0), x, NT)
            total = total + decays * products * stept
        shared[...] = total
        within[at] = jnp.where(first, parts[0], parts[1])
        grad0[at] = jnp.where(first, grads[0], grads[1])
        return carry

    lax.fori_loop(0, tiles, inside, 0)

    def head_sums(value, q):
        left = jnp.sum(jnp.where(first, value, 0.0), axis=1, keepdims=True)
        right = jnp.sum(jnp.where(first, 0.0, value), axis=1, keepdims=True)
        return jnp.where(lane == 2 * q, left, jnp.where(lane == 2 * q + 1, right, 0.0))

    scan(0)
    second_go()
    scan(1)
    wait_back(0)

    def outputs(q, carry):
        at = tile_of(q)
        gate = gate_ref[at].astype(jnp.float32)
        gate_silu = silu(gate)
        gg = gg_ref[at]
        grow = jnp.exp(ldx[at])
        carried = dot(c_rows[...], sin[q].reshape(state, LANES), NN)
        y = within[at] + grow * carried + chan_ref[dskip_of(q)] * silu(prex_ref[at])
        gated_ref[q] = (y * gate_silu).T.astype(gated_ref.dtype)
        gradz_ref[at] = (gg * y * silu_slope(gate)).astype(gradz_ref.dtype)
        heads[3] += head_sums(gg * gate_silu * carried, q)
        return carry

    lax.fori_loop(0, tiles, outputs, 0)

    def placed(store, at):
        return store.at[:, pl.ds(pl.multiple_of(at * length, LANES), length)]

    def give_gated(k, carry):
        to = lax.rem(line + k, lines)
        chip = to * LINE + spot
        for d in range(2):
            away = jnp.logical_or(to != line, core != d)
            for at, tile, store in ((0, to, main), (1, 16 + to // 4, extra)):
                mine = tile_core(tile) == core

                @pl.when(jnp.logical_and(mine, away))
                def _():
                    across(
                        gated_ref.at[tile - 10 * core], placed(store, line), chip, d,
                        g_send.at[2 * at + d], g_recv.at[at],
                    ).start()

                @pl.when(jnp.logical_and(mine, jnp.logical_not(away)))
                def _():
                    placed(store, line)[...] = gated_ref[tile - 10 * core]

        return carry

    lax.fori_loop(0, lines, give_gated, 0)

    units = all_ref.at[:, :, pl.ds(0, LANES)]

    def wait_for(number, options, ref, act_on):
        for n in options:

            @pl.when(number == n)
            def _():
                act_on(ref.at[pl.ds(0, n)])

    one = lambda flag: jnp.where(flag, 1, 0)

    def wait_gated(at):
        tile = line if at == 0 else 16 + line // 4
        number = lines - one(tile_core(tile) == core)
        wait_for(
            number, (lines - 1, lines), units,
            lambda ref: across(ref, ref, 0, 0, g_send.at[0], g_recv.at[at]).wait_recv(),
        )

    wait_gated(0)
    finish_go()

    def product(store, start, width):
        value = lax.dot_general(
            store[...],
            all_ref[:, :, pl.ds(start, width)].reshape(lines * length, width),
            (NN, ((), ())),
            preferred_element_type=jnp.float32,
        )
        return value.T

    main_core = tile_core(line)
    column = line - 10 * main_core
    part = half // 2
    wide_part = part * OWN
    for turn in range(2):
        which = lax.rem(me + turn, 2)
        for j in range(wide_part // LANES):
            start = pl.multiple_of(which * wide_part + j * LANES, LANES)
            sums[j * LANES : (j + 1) * LANES, :] = product(main, start, LANES)
        for i in range(part):
            slots[which * part + i] = sums[i * OWN : (i + 1) * OWN, :].astype(slots.dtype)

        def send_main(k, carry):
            i = which * part + lax.rem(k + me // 2, part)
            to = half * core + i
            away = jnp.logical_or(to != me, main_core != core)

            @pl.when(away)
            def _():
                across(
                    slots.at[i], got.at[column, spot], to, main_core, w_send.at[0], w_recv.at[0]
                ).start()

            @pl.when(jnp.logical_not(away))
            def _():
                got[column, spot] = slots[i]

            return carry

        lax.fori_loop(0, part, send_main, 0)

    wait_gated(1)
    first_tile = (5 * quarter) // 2
    for j in range(3):
        more[j * LANES : (j + 1) * LANES, :] = product(
            extra, pl.multiple_of((first_tile + j) * LANES, LANES), LANES
        )
    kept = more[pl.ds(pl.multiple_of(64 * lax.rem(quarter, 2), 64), 16 * OWN), :]
    for i in range(16):
        slots[half + i] = kept[i * OWN : (i + 1) * OWN, :].astype(slots.dtype)

    extra_column = 6 + line // 4

    def send_extra(k, carry):
        i = lax.rem(k + spot, 16)
        to = half * core + 16 * quarter + i
        away = jnp.logical_or(to != me, core != 1)

        @pl.when(away)
        def _():
            across(
                slots.at[half + i], got.at[extra_column, spot], to, 1, w_send.at[0], w_recv.at[0]
            ).start()

        @pl.when(jnp.logical_not(away))
        def _():
            got[extra_column, spot] = slots[half + i]

        return carry

    lax.fori_loop(0, 16, send_extra, 0)

    wait_back(1)

    def gradients(q, carry):
        at = tile_of(q)
        pre = prex_ref[at]
        x = silu(pre)
        gy = gg_ref[at] * silu(gate_ref[at].astype(jnp.float32))
        ld = ldx[at]
        step = stepx[at]
        weight = jnp.exp(ld[length - 1 :, :] - ld) * step
        s_in = sin[q].reshape(state, LANES)
        r_in = rin[q].reshape(state, LANES)
        carry_b = dot(b_rows[...], r_in, NN)
        inner = grad0[at]
        grad_in = chan_ref[dskip_of(q)] * gy + step * inner + weight * carry_b
        gxc_ref[at] = (grad_in * silu_slope(pre)).astype(gxc_ref.dtype)
        grad_b[...] += dot(weight * x, r_in, NT)
        grad_c[...] += dot(jnp.exp(ld) * gy, s_in, NT)
        heads[0] += head_sums(gy * within[at], q)
        heads[1] += head_sums(x * inner, q)
        heads[2] += head_sums(x * carry_b, q)
        const[...] += head_sums(
            jnp.broadcast_to(jnp.sum(r_in * s_in, axis=0, keepdims=True), x.shape), q
        )
        return carry

    lax.fori_loop(0, tiles, gradients, 0)
    gbc[:, :state] = grad_b[...] + dot(shared[...], c_rows[...], TN)
    gbc[:, state:] = grad_c[...] + dot(shared[...], b_rows[...], NN)
    swap = across(gbc, other, me, 1 - core, bc_send.at[0], bc_recv.at[0])
    swap.start()
    ldh = ld_ref[...]
    steph = step_ref[...]
    lasth = ldh[length - 1 :, :]
    to_endh = jnp.exp(lasth - ldh)
    direct, carry_dot = heads[1], heads[2]
    leaving = to_endh * steph * carry_dot
    grad_log = heads[0] - steph * direct + jnp.exp(ldh) * heads[3] - leaving
    constant = jnp.sum(leaving, axis=0, keepdims=True) + jnp.exp(lasth) * const[0:1, :]
    upper = jnp.where(col_at >= row_at, 1.0, 0.0)
    grad_rate = dot(upper, grad_log, NN) + constant
    gstep_ref[...] = (direct + to_endh * carry_dot + rate * grad_rate) * jax.nn.sigmoid(shifted)
    gstep_ref[...] = gstep_ref[...].T

    at_home = me // half == core
    own_main = one(jnp.logical_and(at_home, main_core == core))
    own_extra = one(
        jnp.logical_and(
            jnp.logical_and(at_home, core == 1), lax.rem(me, half) // 16 == quarter
        )
    )
    total = half + 16
    number = total - own_main - own_extra
    wait_for(
        number, (total - 2, total - 1, total), slots,
        lambda ref: across(ref, ref, 0, 0, w_send.at[0], w_recv.at[0]).wait_recv(),
    )
    for t in range(10):
        value = got[t, 0].astype(jnp.float32)
        for z in range(1, LINE):
            value = value + got[t, z].astype(jnp.float32)
        out_ref[:, t * LANES : (t + 1) * LANES] = value
    swap.wait()
    bc_ref[...] = ((gbc[...] + other[...]) * silu_slope(prebc_ref[...])).astype(bc_ref.dtype)
    wait_for(
        number, (total - 2, total - 1, total), slots,
        lambda ref: across(ref, ref, 0, 0, w_send.at[0], w_recv.at[0]).wait_send(),
    )
    for d in range(2):
        same = jnp.logical_and(main_core == core, core == d)
        wait_for(
            jnp.where(core == 0, 10, 6) - one(same), (5, 6, 9, 10), units,
            lambda ref: across(ref, ref, 0, 0, g_send.at[d], g_recv.at[0]).wait_send(),
        )
        wait_for(
            jnp.where(core == 0, 0, lines - d), (lines - d,), units,
            lambda ref: across(ref, ref, 0, 0, g_send.at[2 + d], g_recv.at[0]).wait_send(),
        )
    finish_scan(0)
    finish_scan(1)

    @pl.when(me < count - 1)
    def _():
        for make in rims:
            make().wait_send()


def finish_kernel(out, bc, gradz, gxc, gstep, out_to, bc_to, gradz_to, gxc_to, gstep_to):
    for source, target in ((out, out_to), (bc, bc_to), (gradz, gradz_to), (gxc, gxc_to)):
        target[...] = source[...]
    gstep_to[...] = gstep[: gstep_to.shape[0], :]


def finish(values, heads):
    vmem = pl.BlockSpec(memory_space=pltpu.VMEM)
    shapes = [jax.ShapeDtypeStruct(v.shape, v.dtype) for v in values[:-1]]
    shapes.append(jax.ShapeDtypeStruct((heads, values[-1].shape[1]), values[-1].dtype))
    return pl.pallas_call(
        finish_kernel, out_shape=shapes, in_specs=[vmem] * 5, out_specs=[vmem] * 5, name="finish"
    )(*values)


def main_part(x_raw, bc_raw, gate, dt, chan, w, go, count):
    length, channels = x_raw.shape
    states = bc_raw.shape[1]
    state = states // 2
    tiles = channels // LANES
    lines = count // LINE
    half = count // 2
    f32, bf16 = jnp.float32, jnp.bfloat16
    vmem = pl.BlockSpec(memory_space=pltpu.VMEM)
    dma = pltpu.SemaphoreType.DMA
    wide = pltpu.VMEM((length, channels), f32)
    square = pltpu.VMEM((length, LANES), f32)
    piece = pltpu.VMEM((tiles, ROW_TILES, ROWS, LANES), f32)
    return pl.pallas_call(
        functools.partial(main_kernel, count),
        out_shape=[
            jax.ShapeDtypeStruct((OWN, channels), f32),
            jax.ShapeDtypeStruct((length, 2 * state), bf16),
            jax.ShapeDtypeStruct((length, channels), bf16),
            jax.ShapeDtypeStruct((length, channels), bf16),
            jax.ShapeDtypeStruct((length, LANES), f32),
        ],
        in_specs=[vmem] * 7,
        out_specs=[vmem] * 5,
        scratch_shapes=[
            piece, piece, pltpu.VMEM((tiles, 1, LANES), f32), wide, wide,
            pltpu.VMEM((length, states), f32), square, square, square, square,
            pltpu.VMEM((RIM, channels), bf16), pltpu.VMEM((RIM, states), bf16),
            pltpu.VMEM((length + RIM, LANES), f32), pltpu.VMEM((length + RIM, states), f32),
        ]
        + [pltpu.VMEM((count, ROWS, LANES), f32)] * 4
        + [pltpu.VMEM((count, 1, LANES), f32)] * 2
        + [piece] * 2
        + [pltpu.VMEM((lines, length, go.shape[1] // 2), go.dtype)]
        + [wide] * 4
        + [
            pltpu.VMEM((tiles, LANES, length), bf16),
            pltpu.VMEM((length, 2 * state), f32),
            square, square, square, square,
            pltpu.VMEM((4, length, LANES), f32),
            square,
            pltpu.VMEM((length, 2 * state), f32),
            pltpu.VMEM((length, 2 * state), f32),
            pltpu.VMEM((LANES, lines * length), bf16),
            pltpu.VMEM((LANES, lines * length), bf16),
            pltpu.VMEM((half // 2 * OWN, LANES), f32),
            pltpu.VMEM((3 * LANES, LANES), f32),
            pltpu.VMEM((half + 16, OWN, LANES), bf16),
            pltpu.VMEM((10, LINE, OWN, LANES), bf16),
        ]
        + [dma((2,))] * 6
        + [dma((4,))] * 3
        + [dma((2,))]
        + [dma((1,))] * 4
        + [dma((2,))] * 2,
        compiler_params=pltpu.CompilerParams(collective_id=0, has_side_effects=True),
        name="main",
    )(x_raw, bc_raw, gate, dt, chan, w, go)


def per_device(
    x_raw, bc_raw, gate_branch, dt_raw, conv_x, conv_x_bias, conv_bc, conv_bc_bias, dt_bias, a_log,
    d_skip, out_weight, grad_out,
):
    length, heads = dt_raw.shape
    channels = x_raw.shape[1]
    gap = jnp.zeros((LANES - heads,), jnp.float32)
    row = jnp.concatenate(
        [
            conv_x_bias, jnp.repeat(d_skip, HEAD), conv_bc.reshape(-1), conv_bc_bias,
            dt_bias, gap, a_log, gap, jnp.zeros((channels - 2 * LANES,), jnp.float32),
        ]
    )
    chan = jnp.concatenate([conv_x, row.reshape(4, channels)])
    values = main_part(
        x_raw, bc_raw, gate_branch, dt_raw.T, chan, out_weight, grad_out, lax.axis_size("ctx")
    )
    weight_grad, grad_bc_conv, grad_z, gxc, grad_dt_raw = finish(values, heads)
    return (gxc, grad_bc_conv, grad_z, grad_dt_raw.T, weight_grad)


def solution(mesh):
    placed = (
        P("ctx", "tp"), P("ctx", None), P("ctx", "tp"), P("ctx", "tp"), P(None, "tp"), P("tp"),
        P(), P(), P("tp"), P("tp"), P("tp"), P("tp", None), P("ctx", None),
    )
    return jax.shard_map(
        per_device,
        mesh=mesh,
        in_specs=placed,
        out_specs=(P("ctx", "tp"), P("ctx", None), P("ctx", "tp"), P("ctx", "tp"), P("ctx", "tp")),
        check_vma=False,
    )
```

```python
import functools

import jax
import jax.numpy as jnp
from jax import lax
from jax.experimental import pallas as pl
from jax.experimental.pallas import tpu as pltpu
from jax.sharding import PartitionSpec as P

KERNEL = 4
HEAD = 64
LANES = 128
ROWS = 16
ROW_TILES = 8
PER_LINE = 5
LINE = 8
SIDE = 4
MESH = pl.DeviceIdType.MESH


def dot(a, b, contract):
    return lax.dot_general(
        a,
        b,
        (contract, ((), ())),
        precision=lax.Precision.HIGHEST,
        preferred_element_type=jnp.float32,
    )


NN = ((1,), (0,))
TN = ((0,), (0,))
NT = ((1,), (1,))


def silu_slope(argument):
    gate_value = jax.nn.sigmoid(argument)
    return gate_value * (1.0 + argument * (1.0 - gate_value))


def silu(argument):
    return argument * jax.nn.sigmoid(argument)


def expand(per_head, q):
    row = lax.broadcasted_iota(jnp.int32, (LANES, LANES), 0)
    lane = lax.broadcasted_iota(jnp.int32, (LANES, LANES), 1)
    pick = jnp.where(row == 2 * q + jnp.where(lane < HEAD, 0, 1), 1.0, 0.0)
    return dot(per_head, pick, NN)


RIM = 16


def convolve(raw, rim, taps, padded):
    length = raw.shape[0]
    padded[0:RIM, :] = rim
    padded[RIM : RIM + length, :] = raw
    result = jnp.broadcast_to(taps[KERNEL], raw.shape)
    for k in range(KERNEL):
        start = RIM - (KERNEL - 1) + k
        result = result + taps[k] * padded[start : start + length, :]
    return result


OWN = 20


def owner_of(tile, row, shift):
    line = lax.rem(tile, 2) * ROW_TILES + row
    spot = lax.rem((LINE * (tile // 2)) // PER_LINE + shift + 2 * line + line // 4, LINE)
    return line * LINE + spot


def piece_of(chip, shift):
    line = chip // LINE
    spot = lax.rem(lax.rem(chip, LINE) + 8 * LINE - shift - 2 * line - line // 4, LINE)
    rank = (PER_LINE * spot + LINE - 1) // LINE
    owns = (LINE * rank) // PER_LINE == spot
    return 2 * rank + line // ROW_TILES, lax.rem(line, ROW_TILES), owns


def tile_core(tile):
    return tile // 10


def main_kernel(
    count, x_ref, bcraw_ref, gate_ref, dt_ref, chan_ref, weights_ref, go_ref,
    out_ref, bc_ref, gradz_ref, gxc_ref, gstep_ref,
    f_ref, r_ref, decay_ref, prex_ref, gg_ref, prebc_ref, ld_ref, step_ref, ldt_ref, stept_ref,
    rim_x, rim_bc, pad_x, pad_bc,
    got_f, got_r, back_f, back_r, decay_f, decay_r, sin, rin, all_ref, ldx, stepx, within, grad0,
    gated_ref, act, scores, shared, grad_b, grad_c, heads, const, gbc, other,
    main, extra, sums, more, slots, got,
    send, recv, back_send, back_recv, decay_send, decay_recv, go_send, go_recv,
    g_send, g_recv, w_send, w_recv, bc_send, bc_recv, rim_send, rim_recv,
):
    me = lax.axis_index("ctx")
    core = lax.axis_index("tp")
    line, spot = me // LINE, lax.rem(me, LINE)
    lines = count // LINE
    half = count // 2
    length = x_ref.shape[0]
    state = bcraw_ref.shape[1] // 2
    tiles = f_ref.shape[0]
    pieces = tiles * ROW_TILES
    quarter = lax.rem(line, 4)
    barrier = pltpu.get_barrier_semaphore()

    def greet(k, carry):
        peer = lax.rem(me + k, count)
        for d in range(2):

            @pl.when(jnp.logical_or(k > 0, core != d))
            def _():
                pl.semaphore_signal(
                    barrier, inc=1, device_id={"ctx": peer, "tp": d}, device_id_type=MESH
                )

        return carry

    lax.fori_loop(0, count, greet, 0)

    def copy(src, dst, peer, here, there):
        return pltpu.make_async_remote_copy(
            src_ref=src, dst_ref=dst, send_sem=here, recv_sem=there,
            device_id={"ctx": peer}, device_id_type=MESH,
        )

    def across(src, dst, chip, d, here, there):
        return pltpu.make_async_remote_copy(
            src_ref=src, dst_ref=dst, send_sem=here, recv_sem=there,
            device_id={"ctx": chip, "tp": d}, device_id_type=MESH,
        )

    sets = (
        (0, f_ref, decay_f, sin, got_f, back_f, False),
        (1, r_ref, decay_r, rin, got_r, back_r, True),
    )

    def give(which, tile):
        _, src, decay, dst, arrived, back, reverse = sets[which]
        for j in range(ROW_TILES):
            row = lax.rem(me + j, ROW_TILES)
            owner = owner_of(tile, row, which)

            @pl.when(owner != me)
            def _():
                copy(
                    src.at[tile, row], arrived.at[me], owner, send.at[which], recv.at[which]
                ).start()
                copy(
                    decay_ref.at[tile], decay.at[me], owner,
                    decay_send.at[which], decay_recv.at[which],
                ).start()

    def scan(which):
        _, src, decay, dst, arrived, back, reverse = sets[which]
        own_tile, own_row, owns = piece_of(me, which)

        @pl.when(owns)
        def _():
            arrived[me] = src[own_tile, own_row]
            decay[me] = decay_ref[own_tile]
            some = arrived.at[pl.ds(0, count - 1)]
            copy(some, some, 0, send.at[which], recv.at[which]).wait_recv()
            some = decay.at[pl.ds(0, count - 1)]
            copy(some, some, 0, decay_send.at[which], decay_recv.at[which]).wait_recv()

            def step(k, value):
                for u in range(4):
                    at = 4 * k + u
                    at = count - 1 - at if reverse else at
                    back[at] = value
                    value = decay[at] * value + arrived[at].astype(jnp.float32)
                return value

            lax.fori_loop(0, count // 4, step, jnp.zeros((ROWS, LANES), jnp.float32))
            dst[own_tile, own_row] = back[me]

            def give_back(k, carry):
                peer = lax.rem(me + k, count)
                copy(
                    back.at[peer], dst.at[own_tile, own_row], peer,
                    back_send.at[which], back_recv.at[which],
                ).start()
                return carry

            lax.fori_loop(1, count, give_back, 0)

    def wait_back(which):
        _, src, decay, dst, arrived, back, reverse = sets[which]
        own_tile, own_row, owns = piece_of(me, which)
        for flag, number in ((owns, pieces - 1), (jnp.logical_not(owns), pieces)):

            @pl.when(flag)
            def _():
                some = back.at[pl.ds(0, number)]
                copy(some, some, 0, send.at[which], back_recv.at[which]).wait_recv()

    def finish_scan(which):
        _, src, decay, dst, arrived, back, reverse = sets[which]
        own_tile, own_row, owns = piece_of(me, which)
        for flag, number in ((owns, pieces - 1), (jnp.logical_not(owns), pieces)):

            @pl.when(flag)
            def _():
                some = arrived.at[pl.ds(0, number)]
                few = decay.at[pl.ds(0, number)]
                copy(some, some, 0, send.at[which], back_recv.at[which]).wait_send()
                copy(few, few, 0, decay_send.at[which], decay_recv.at[which]).wait_send()

        @pl.when(owns)
        def _():
            rest = back.at[pl.ds(0, count - 1)]
            copy(rest, rest, 0, back_send.at[which], back_recv.at[which]).wait_send()

    x_at, y_at = line // SIDE, lax.rem(line, SIDE)
    features = go_ref.shape[1] // 2
    middle = features // 2
    early, late = pl.ds(0, middle), pl.ds(middle, middle)
    start_go = pl.multiple_of(core * features, LANES)
    go_early = pl.ds(start_go, middle)
    go_late = pl.ds(pl.multiple_of(core * features + middle, LANES), middle)
    along_x = [lax.rem(x_at + d, SIDE) * SIDE + y_at for d in range(SIDE)]
    along_y = [x_at * SIDE + lax.rem(y_at + d, SIDE) for d in range(SIDE)]

    def shift_go(src, dst, to, at):
        copy(src, dst, to * LINE + spot, go_send.at[at], go_recv.at[at]).start()

    def first_go():
        all_ref[line] = go_ref[:, pl.ds(start_go, features)]
        for d in range(1, SIDE):
            shift_go(go_ref.at[:, go_early], all_ref.at[line, :, early], along_y[d], 0)
            shift_go(go_ref.at[:, go_late], all_ref.at[line, :, late], along_x[d], 1)

    def second_go():
        some = all_ref.at[pl.ds(0, SIDE - 1), :, early]
        for at in range(2):
            copy(some, some, 0, go_send.at[at], go_recv.at[at]).wait_recv()
        for d in range(1, SIDE):
            for k in range(SIDE):
                held = all_ref.at[along_y[k], :, early]
                shift_go(held, held, along_x[d], 2)
                held = all_ref.at[along_x[k], :, late]
                shift_go(held, held, along_y[d], 3)

    def finish_go():
        some = all_ref.at[pl.ds(0, SIDE - 1), :, early]
        most = all_ref.at[pl.ds(0, SIDE * (SIDE - 1)), :, early]
        for at in range(2):
            copy(some, some, 0, go_send.at[at], go_recv.at[at]).wait_send()
            copy(most, most, 0, go_send.at[2 + at], go_recv.at[2 + at]).wait()

    def tile_of(q):
        return (slice(None), pl.ds(pl.multiple_of(q * LANES, LANES), LANES))

    def dskip_of(q):
        return (slice(KERNEL + 1, KERNEL + 2), pl.ds(pl.multiple_of(q * LANES, LANES), LANES))

    def gated_gradient(q, carry):
        rows = pl.ds(pl.multiple_of(q * LANES, LANES), LANES)
        gg_ref[tile_of(q)] = lax.dot_general(
            go_ref[...], weights_ref[rows, :], (NT, ((), ())), preferred_element_type=jnp.float32
        )
        return carry

    lax.fori_loop(0, tiles, gated_gradient, 0)
    row_at = lax.broadcasted_iota(jnp.int32, (length, length), 0)
    col_at = lax.broadcasted_iota(jnp.int32, (length, length), 1)
    lower = row_at >= col_at
    ldt_ref[...] = jnp.zeros_like(ldt_ref)
    ldt_ref[: dt_ref.shape[0], :] = dt_ref[...]
    shifted = ldt_ref[...].T + chan_ref[7:8, :LANES]
    rate = -jnp.exp(chan_ref[7:8, LANES : 2 * LANES])
    softplus = jnp.maximum(shifted, 0.0) + jnp.log1p(jnp.exp(-jnp.abs(shifted)))
    step_ref[...] = softplus
    ld_ref[...] = dot(jnp.where(lower, 1.0, 0.0), softplus * rate, NN)
    ldt_ref[...] = ld_ref[...].T
    stept_ref[...] = softplus.T

    pl.semaphore_wait(barrier, 2 * count - 1)

    end = pl.ds(length - RIM, RIM)
    rims = (
        lambda: copy(x_ref.at[end, :], rim_x, me + 1, rim_send.at[0], rim_recv.at[0]),
        lambda: copy(bcraw_ref.at[end, :], rim_bc, me + 1, rim_send.at[1], rim_recv.at[1]),
    )

    @pl.when(me < count - 1)
    def _():
        for make in rims:
            make().start()

    first_go()

    @pl.when(me == 0)
    def _():
        rim_x[...] = jnp.zeros_like(rim_x)
        rim_bc[...] = jnp.zeros_like(rim_bc)

    @pl.when(me > 0)
    def _():
        copy(rim_x, rim_x, 0, rim_send.at[0], rim_recv.at[0]).wait_recv()
        copy(rim_bc, rim_bc, 0, rim_send.at[1], rim_recv.at[1]).wait_recv()

    pre_bc = convolve(
        bcraw_ref[...].astype(jnp.float32), rim_bc[...].astype(jnp.float32),
        [chan_ref[6:7, k * 2 * state : (k + 1) * 2 * state] for k in range(KERNEL + 1)], pad_bc,
    )
    prebc_ref[...] = pre_bc
    act[...] = silu(pre_bc)
    b_rows = act.at[:, :state]
    c_rows = act.at[:, state:]
    split = (ROW_TILES, ROWS, LANES)

    def forward(k, carry):
        q = lax.rem(k + me, tiles)
        at = tile_of(q)
        pre = convolve(
            x_ref[at].astype(jnp.float32), rim_x[at].astype(jnp.float32),
            [chan_ref[k : k + 1, at[1]] for k in range(KERNEL + 1)], pad_x,
        )
        prex_ref[at] = pre
        ld = expand(ld_ref[...], q)
        step = expand(step_ref[...], q)
        ldx[at] = ld
        stepx[at] = step
        last = ld[length - 1 :, :]
        f_ref[q] = dot(b_rows[...], jnp.exp(last - ld) * step * silu(pre), TN).reshape(split).astype(f_ref.dtype)
        decay_ref[q] = jnp.exp(last)
        give(0, q)
        return carry

    lax.fori_loop(0, tiles, forward, 0)

    def backward(k, carry):
        q = lax.rem(k + me, tiles)
        at = tile_of(q)
        gy = gg_ref[at] * silu(gate_ref[at].astype(jnp.float32))
        r_ref[q] = dot(c_rows[...], jnp.exp(ldx[at]) * gy, TN).reshape(split)
        give(1, q)
        return carry

    lax.fori_loop(0, tiles, backward, 0)

    lane = lax.broadcasted_iota(jnp.int32, (length, LANES), 1)
    first = lane < HEAD
    scores[...] = dot(c_rows[...], b_rows[...], NT)
    for ref in (shared, grad_b, grad_c, heads, const):
        ref[...] = jnp.zeros_like(ref)

    def inside(q, carry):
        at = tile_of(q)
        x = silu(prex_ref[at])
        gy = gg_ref[at] * silu(gate_ref[at].astype(jnp.float32))
        ld = ldx[at]
        xs = stepx[at] * x
        parts, grads = [], []
        total = shared[...]
        for a in range(2):
            mine = row_at == 2 * q + a
            ldt = jnp.sum(jnp.where(mine, ldt_ref[...], 0.0), axis=0, keepdims=True)
            stept = jnp.sum(jnp.where(mine, stept_ref[...], 0.0), axis=0, keepdims=True)
            spread = ld[:, a * HEAD : a * HEAD + 1] - ldt
            decays = jnp.where(lower, jnp.exp(jnp.where(lower, spread, 0.0)), 0.0)
            mixing = decays * scores[...]
            parts.append(dot(mixing, xs, NN))
            grads.append(dot(mixing, gy, TN))
            own = first if a == 0 else jnp.logical_not(first)
            products = dot(jnp.where(own, gy, 0.0), x, NT)
            total = total + decays * products * stept
        shared[...] = total
        within[at] = jnp.where(first, parts[0], parts[1])
        grad0[at] = jnp.where(first, grads[0], grads[1])
        return carry

    lax.fori_loop(0, tiles, inside, 0)

    def head_sums(value, q):
        left = jnp.sum(jnp.where(first, value, 0.0), axis=1, keepdims=True)
        right = jnp.sum(jnp.where(first, 0.0, value), axis=1, keepdims=True)
        return jnp.where(lane == 2 * q, left, jnp.where(lane == 2 * q + 1, right, 0.0))

    scan(0)
    second_go()
    scan(1)
    wait_back(0)

    def outputs(q, carry):
        at = tile_of(q)
        gate = gate_ref[at].astype(jnp.float32)
        gate_silu = silu(gate)
        gg = gg_ref[at]
        grow = jnp.exp(ldx[at])
        carried = dot(c_rows[...], sin[q].reshape(state, LANES), NN)
        y = within[at] + grow * carried + chan_ref[dskip_of(q)] * silu(prex_ref[at])
        gated_ref[q] = (y * gate_silu).T.astype(gated_ref.dtype)
        gradz_ref[at] = (gg * y * silu_slope(gate)).astype(gradz_ref.dtype)
        heads[3] += head_sums(gg * gate_silu * carried, q)
        return carry

    lax.fori_loop(0, tiles, outputs, 0)

    def placed(store, at):
        return store.at[:, pl.ds(pl.multiple_of(at * length, LANES), length)]

    def give_gated(k, carry):
        to = lax.rem(line + k, lines)
        chip = to * LINE + spot
        for d in range(2):
            away = jnp.logical_or(to != line, core != d)
            for at, tile, store in ((0, to, main), (1, 16 + to // 4, extra)):
                mine = tile_core(tile) == core

                @pl.when(jnp.logical_and(mine, away))
                def _():
                    across(
                        gated_ref.at[tile - 10 * core], placed(store, line), chip, d,
                        g_send.at[2 * at + d], g_recv.at[at],
                    ).start()

                @pl.when(jnp.logical_and(mine, jnp.logical_not(away)))
                def _():
                    placed(store, line)[...] = gated_ref[tile - 10 * core]

        return carry

    lax.fori_loop(0, lines, give_gated, 0)

    units = all_ref.at[:, :, pl.ds(0, LANES)]

    def wait_for(number, options, ref, act_on):
        for n in options:

            @pl.when(number == n)
            def _():
                act_on(ref.at[pl.ds(0, n)])

    one = lambda flag: jnp.where(flag, 1, 0)

    def wait_gated(at):
        tile = line if at == 0 else 16 + line // 4
        number = lines - one(tile_core(tile) == core)
        wait_for(
            number, (lines - 1, lines), units,
            lambda ref: across(ref, ref, 0, 0, g_send.at[0], g_recv.at[at]).wait_recv(),
        )

    wait_gated(0)
    finish_go()

    def product(store, start, width):
        value = lax.dot_general(
            store[...],
            all_ref[:, :, pl.ds(start, width)].reshape(lines * length, width),
            (NN, ((), ())),
            preferred_element_type=jnp.float32,
        )
        return value.T

    main_core = tile_core(line)
    column = line - 10 * main_core
    part = half // 2
    wide_part = part * OWN
    for turn in range(2):
        which = lax.rem(me + turn, 2)
        for j in range(wide_part // LANES):
            start = pl.multiple_of(which * wide_part + j * LANES, LANES)
            sums[j * LANES : (j + 1) * LANES, :] = product(main, start, LANES)
        for i in range(part):
            slots[which * part + i] = sums[i * OWN : (i + 1) * OWN, :].astype(slots.dtype)

        def send_main(k, carry):
            i = which * part + lax.rem(k + me // 2, part)
            to = half * core + i
            away = jnp.logical_or(to != me, main_core != core)

            @pl.when(away)
            def _():
                across(
                    slots.at[i], got.at[column, spot], to, main_core, w_send.at[0], w_recv.at[0]
                ).start()

            @pl.when(jnp.logical_not(away))
            def _():
                got[column, spot] = slots[i]

            return carry

        lax.fori_loop(0, part, send_main, 0)

    wait_gated(1)
    first_tile = (5 * quarter) // 2
    for j in range(3):
        more[j * LANES : (j + 1) * LANES, :] = product(
            extra, pl.multiple_of((first_tile + j) * LANES, LANES), LANES
        )
    kept = more[pl.ds(pl.multiple_of(64 * lax.rem(quarter, 2), 64), 16 * OWN), :]
    for i in range(16):
        slots[half + i] = kept[i * OWN : (i + 1) * OWN, :].astype(slots.dtype)

    extra_column = 6 + line // 4

    def send_extra(k, carry):
        i = lax.rem(k + spot, 16)
        to = half * core + 16 * quarter + i
        away = jnp.logical_or(to != me, core != 1)

        @pl.when(away)
        def _():
            across(
                slots.at[half + i], got.at[extra_column, spot], to, 1, w_send.at[0], w_recv.at[0]
            ).start()

        @pl.when(jnp.logical_not(away))
        def _():
            got[extra_column, spot] = slots[half + i]

        return carry

    lax.fori_loop(0, 16, send_extra, 0)

    wait_back(1)

    def gradients(q, carry):
        at = tile_of(q)
        pre = prex_ref[at]
        x = silu(pre)
        gy = gg_ref[at] * silu(gate_ref[at].astype(jnp.float32))
        ld = ldx[at]
        step = stepx[at]
        weight = jnp.exp(ld[length - 1 :, :] - ld) * step
        s_in = sin[q].reshape(state, LANES)
        r_in = rin[q].reshape(state, LANES)
        carry_b = dot(b_rows[...], r_in, NN)
        inner = grad0[at]
        grad_in = chan_ref[dskip_of(q)] * gy + step * inner + weight * carry_b
        gxc_ref[at] = (grad_in * silu_slope(pre)).astype(gxc_ref.dtype)
        grad_b[...] += dot(weight * x, r_in, NT)
        grad_c[...] += dot(jnp.exp(ld) * gy, s_in, NT)
        heads[0] += head_sums(gy * within[at], q)
        heads[1] += head_sums(x * inner, q)
        heads[2] += head_sums(x * carry_b, q)
        const[...] += head_sums(
            jnp.broadcast_to(jnp.sum(r_in * s_in, axis=0, keepdims=True), x.shape), q
        )
        return carry

    lax.fori_loop(0, tiles, gradients, 0)
    gbc[:, :state] = grad_b[...] + dot(shared[...], c_rows[...], TN)
    gbc[:, state:] = grad_c[...] + dot(shared[...], b_rows[...], NN)
    swap = across(gbc, other, me, 1 - core, bc_send.at[0], bc_recv.at[0])
    swap.start()
    ldh = ld_ref[...]
    steph = step_ref[...]
    lasth = ldh[length - 1 :, :]
    to_endh = jnp.exp(lasth - ldh)
    direct, carry_dot = heads[1], heads[2]
    leaving = to_endh * steph * carry_dot
    grad_log = heads[0] - steph * direct + jnp.exp(ldh) * heads[3] - leaving
    constant = jnp.sum(leaving, axis=0, keepdims=True) + jnp.exp(lasth) * const[0:1, :]
    upper = jnp.where(col_at >= row_at, 1.0, 0.0)
    grad_rate = dot(upper, grad_log, NN) + constant
    gstep_ref[...] = (direct + to_endh * carry_dot + rate * grad_rate) * jax.nn.sigmoid(shifted)
    gstep_ref[...] = gstep_ref[...].T

    at_home = me // half == core
    own_main = one(jnp.logical_and(at_home, main_core == core))
    own_extra = one(
        jnp.logical_and(
            jnp.logical_and(at_home, core == 1), lax.rem(me, half) // 16 == quarter
        )
    )
    total = half + 16
    number = total - own_main - own_extra
    wait_for(
        number, (total - 2, total - 1, total), slots,
        lambda ref: across(ref, ref, 0, 0, w_send.at[0], w_recv.at[0]).wait_recv(),
    )
    for t in range(10):
        value = got[t, 0].astype(jnp.float32)
        for z in range(1, LINE):
            value = value + got[t, z].astype(jnp.float32)
        out_ref[:, t * LANES : (t + 1) * LANES] = value
    swap.wait()
    bc_ref[...] = ((gbc[...] + other[...]) * silu_slope(prebc_ref[...])).astype(bc_ref.dtype)
    wait_for(
        number, (total - 2, total - 1, total), slots,
        lambda ref: across(ref, ref, 0, 0, w_send.at[0], w_recv.at[0]).wait_send(),
    )
    for d in range(2):
        same = jnp.logical_and(main_core == core, core == d)
        wait_for(
            jnp.where(core == 0, 10, 6) - one(same), (5, 6, 9, 10), units,
            lambda ref: across(ref, ref, 0, 0, g_send.at[d], g_recv.at[0]).wait_send(),
        )
        wait_for(
            jnp.where(core == 0, 0, lines - d), (lines - d,), units,
            lambda ref: across(ref, ref, 0, 0, g_send.at[2 + d], g_recv.at[0]).wait_send(),
        )
    finish_scan(0)
    finish_scan(1)

    @pl.when(me < count - 1)
    def _():
        for make in rims:
            make().wait_send()


def finish_kernel(out, bc, gradz, gxc, gstep, out_to, bc_to, gradz_to, gxc_to, gstep_to):
    for source, target in ((out, out_to), (bc, bc_to), (gradz, gradz_to), (gxc, gxc_to)):
        target[...] = source[...]
    gstep_to[...] = gstep[: gstep_to.shape[0], :]


def finish(values, heads):
    vmem = pl.BlockSpec(memory_space=pltpu.VMEM)
    shapes = [jax.ShapeDtypeStruct(v.shape, v.dtype) for v in values[:-1]]
    shapes.append(jax.ShapeDtypeStruct((heads, values[-1].shape[1]), values[-1].dtype))
    return pl.pallas_call(
        finish_kernel, out_shape=shapes, in_specs=[vmem] * 5, out_specs=[vmem] * 5, name="finish"
    )(*values)


def main_part(x_raw, bc_raw, gate, dt, chan, w, go, count):
    length, channels = x_raw.shape
    states = bc_raw.shape[1]
    state = states // 2
    tiles = channels // LANES
    lines = count // LINE
    half = count // 2
    f32, bf16 = jnp.float32, jnp.bfloat16
    vmem = pl.BlockSpec(memory_space=pltpu.VMEM)
    dma = pltpu.SemaphoreType.DMA
    wide = pltpu.VMEM((length, channels), f32)
    square = pltpu.VMEM((length, LANES), f32)
    piece = pltpu.VMEM((tiles, ROW_TILES, ROWS, LANES), f32)
    return pl.pallas_call(
        functools.partial(main_kernel, count),
        out_shape=[
            jax.ShapeDtypeStruct((OWN, channels), f32),
            jax.ShapeDtypeStruct((length, 2 * state), bf16),
            jax.ShapeDtypeStruct((length, channels), bf16),
            jax.ShapeDtypeStruct((length, channels), bf16),
            jax.ShapeDtypeStruct((length, LANES), f32),
        ],
        in_specs=[vmem] * 7,
        out_specs=[vmem] * 5,
        scratch_shapes=[
            pltpu.VMEM((tiles, ROW_TILES, ROWS, LANES), bf16), piece,
            pltpu.VMEM((tiles, 1, LANES), f32), wide, wide,
            pltpu.VMEM((length, states), f32), square, square, square, square,
            pltpu.VMEM((RIM, channels), bf16), pltpu.VMEM((RIM, states), bf16),
            pltpu.VMEM((length + RIM, LANES), f32), pltpu.VMEM((length + RIM, states), f32),
        ]
        + [pltpu.VMEM((count, ROWS, LANES), bf16)]
        + [pltpu.VMEM((count, ROWS, LANES), f32)] * 3
        + [pltpu.VMEM((count, 1, LANES), f32)] * 2
        + [piece] * 2
        + [pltpu.VMEM((lines, length, go.shape[1] // 2), go.dtype)]
        + [wide] * 4
        + [
            pltpu.VMEM((tiles, LANES, length), bf16),
            pltpu.VMEM((length, 2 * state), f32),
            square, square, square, square,
            pltpu.VMEM((4, length, LANES), f32),
            square,
            pltpu.VMEM((length, 2 * state), f32),
            pltpu.VMEM((length, 2 * state), f32),
            pltpu.VMEM((LANES, lines * length), bf16),
            pltpu.VMEM((LANES, lines * length), bf16),
            pltpu.VMEM((half // 2 * OWN, LANES), f32),
            pltpu.VMEM((3 * LANES, LANES), f32),
            pltpu.VMEM((half + 16, OWN, LANES), bf16),
            pltpu.VMEM((10, LINE, OWN, LANES), bf16),
        ]
        + [dma((2,))] * 6
        + [dma((4,))] * 3
        + [dma((2,))]
        + [dma((1,))] * 4
        + [dma((2,))] * 2,
        compiler_params=pltpu.CompilerParams(collective_id=0, has_side_effects=True),
        name="main",
    )(x_raw, bc_raw, gate, dt, chan, w, go)


def per_device(
    x_raw, bc_raw, gate_branch, dt_raw, conv_x, conv_x_bias, conv_bc, conv_bc_bias, dt_bias, a_log,
    d_skip, out_weight, grad_out,
):
    length, heads = dt_raw.shape
    channels = x_raw.shape[1]
    gap = jnp.zeros((LANES - heads,), jnp.float32)
    row = jnp.concatenate(
        [
            conv_x_bias, jnp.repeat(d_skip, HEAD), conv_bc.reshape(-1), conv_bc_bias,
            dt_bias, gap, a_log, gap, jnp.zeros((channels - 2 * LANES,), jnp.float32),
        ]
    )
    chan = jnp.concatenate([conv_x, row.reshape(4, channels)])
    values = main_part(
        x_raw, bc_raw, gate_branch, dt_raw.T, chan, out_weight, grad_out, lax.axis_size("ctx")
    )
    weight_grad, grad_bc_conv, grad_z, gxc, grad_dt_raw = finish(values, heads)
    return (gxc, grad_bc_conv, grad_z, grad_dt_raw.T, weight_grad)


def solution(mesh):
    placed = (
        P("ctx", "tp"), P("ctx", None), P("ctx", "tp"), P("ctx", "tp"), P(None, "tp"), P("tp"),
        P(), P(), P("tp"), P("tp"), P("tp"), P("tp", None), P("ctx", None),
    )
    return jax.shard_map(
        per_device,
        mesh=mesh,
        in_specs=placed,
        out_specs=(P("ctx", "tp"), P("ctx", None), P("ctx", "tp"), P("ctx", "tp"), P("ctx", "tp")),
        check_vma=False,
    )
```
